32 devices in a mesh: groups: 2 (over y), ctx: 16 (over z, x, core).
Axes of the slice: x: 2, y: 2, z: 4, core: 2. Of those that a mesh axis runs over, the one named last changes fastest.
Arguments:
- queries: bfloat16 [12288, 1024], P(('groups', 'ctx')), parts along dimension 0, may hold values from -14 to 14
- inputs: bfloat16 [12288, 1024], P(('groups', 'ctx')), parts along dimension 0, may hold values from -6 to 6
- w_kv: bfloat16 [1024, 2048], replicated, may hold values from -1 to 1
- rand_blocks: int32 [192, 3], P('groups'), parts along dimension 0, may hold values from 1 to 94, as said below
- w_cross: bfloat16 [1024, 2048], replicated, may hold values from -1 to 1
- vocab_table: bfloat16 [6144, 1024], P('ctx'), may hold values from -14 to 14
- summary_ids: int32 [512], P('groups'), parts along dimension 0, may hold values from 0 to 6143
Outputs:
- attended: bfloat16 [12288, 1024], P(('groups', 'ctx')), parts along dimension 0
- summary: bfloat16 [512, 1024], P(('groups', 'ctx')), parts along dimension 0
The draws below stay inside these ranges and needn't reach their ends.
There are 2 independent parts, one for each index of `groups`. The reference program is written for one: setup_inputs(seed, part) draws one part's arguments, and reference() takes and returns one part's arrays. A program takes and returns all parts, laid end to end along the dimension named above; an argument that names none is the same for every part. Nothing has to cross between parts.
Inputs may be any that keep to these rules, and one draw needn't show every extreme that they name: `rand_blocks`: take each run of 6 query blocks that starts at a multiple of 6: its 18 random blocks never lie in its own run (they may lie in any other run, and may repeat a block of the window), the 3 blocks of one query block lie in different runs, at most 2 of them lie in any one other run and some run holds exactly 2 of them. No random block is block 0 or block 95.
All inputs are finite; a program needn't handle non-finite values.
Results may differ from the reference program's by a relative error of at most 0.0075.
Values may be sent and summed in bfloat16 or wider, within the bound.
A program may use at most 192 MiB of HBM per device.

```python
import math
import jax
import jax.numpy as jnp
import numpy as np
from jax import lax

D = 1024
HEADS = 16
HEAD = 64
BLOCK = 64
RAND = 3
BLK_DEV = 6
SUM = 256
NBLOCKS = 96
SEQ = 6144
VOCAB = 6144
N_CTX = 16


def draw_queries(key, part):
    sub_key = jax.random.fold_in(key, 11)
    base_rows = jnp.clip(jax.random.normal(sub_key, (SEQ, D), jnp.float32), -6.0, 6.0)
    return base_rows.astype(jnp.bfloat16)


def draw_inputs(key, part):
    sub_key = jax.random.fold_in(key, 12)
    base_rows = jnp.clip(jax.random.normal(sub_key, (SEQ, D), jnp.float32), -6.0, 6.0)
    return base_rows.astype(jnp.bfloat16)


def projection_pair(key):
    noise = jax.random.normal(jax.random.fold_in(key, 1), (D, 2 * D), jnp.float32) * D ** (-0.5)
    matrix = noise
    return jnp.clip(matrix, -1.0, 1.0).astype(jnp.bfloat16)


def draw_w_kv(key, part):
    return projection_pair(jax.random.fold_in(key, 21))


def draw_w_cross(key, part):
    return projection_pair(jax.random.fold_in(key, 22))


def draw_vocab_table(key, part):
    sub_key = jax.random.fold_in(key, 31)
    base_rows = jnp.clip(jax.random.normal(sub_key, (VOCAB, D), jnp.float32), -6.0, 6.0)
    return base_rows.astype(jnp.bfloat16)


def draw_rand_blocks(key, part):
    request_count = RAND * BLK_DEV
    spare = N_CTX - 1
    reach = min(request_count, spare)

    def one_device(device_key, device_index):
        rest = jax.random.permutation(jax.random.fold_in(device_key, 1), spare - 1).astype(jnp.int32)
        forced = jax.random.randint(jax.random.fold_in(device_key, 3), (), 0, reach, dtype=jnp.int32)
        places = jnp.arange(spare, dtype=jnp.int32)
        shifted = rest[jnp.clip(places - 1, 0, spare - 2)]
        unshifted = rest[jnp.clip(places, 0, spare - 2)]
        order = jnp.where(places < forced, unshifted, jnp.where(places == forced, spare - 1, shifted)).astype(jnp.int32)
        slots = jnp.arange(request_count, dtype=jnp.int32) % spare
        owners = (device_index + 1 + order[slots]) % N_CTX
        lowest = jnp.where(owners == 0, 1, 0).astype(jnp.int32)
        highest = jnp.where(owners == N_CTX - 1, BLK_DEV - 1, BLK_DEV).astype(jnp.int32)
        within = jax.random.randint(jax.random.fold_in(device_key, 2), (request_count,), lowest, highest, dtype=jnp.int32)
        return (owners * BLK_DEV + within).reshape(BLK_DEV, RAND)
    device_keys = jax.random.split(jax.random.fold_in(key, 41), N_CTX)
    table = jax.vmap(one_device)(device_keys, jnp.arange(N_CTX, dtype=jnp.int32))
    return table.reshape(NBLOCKS, RAND).astype(jnp.int32)


def plant(values, key, least, high):
    place = [jax.random.randint(jax.random.fold_in(key, axis), (), 0, length) for axis, length in enumerate(values.shape)]
    longest = values.shape.index(max(values.shape))
    next_to = place[:longest] + [(place[longest] + 1) % values.shape[longest]] + place[longest + 1:]
    return values.at[tuple(place)].set(least).at[tuple(next_to)].set(high)


def rank_bounds(count, lean):
    weights = [(1 << 20) // math.isqrt(standing ** lean) + 1 for standing in range(1, count + 1)]
    spread = 1 + sum(weights) // (1 << 30)
    return np.cumsum(np.array([max(1, weight // spread) for weight in weights]))


def ranked(key, extent, number_of, lean):
    listing = rank_bounds(number_of, lean)
    ticket = jax.random.randint(jax.random.fold_in(key, 1), extent, 0, int(listing[number_of - 1]))
    standing = jnp.searchsorted(jnp.asarray(listing, jnp.int32), ticket, side="right")
    return jax.random.permutation(jax.random.fold_in(key, 2), number_of)[standing].astype(jnp.int32)


def setup_inputs(seed: int = 0, part: int = 0) -> dict:
    keys = jax.random.split(jax.random.key(seed), 8)
    part_keys = jax.random.split(jax.random.fold_in(keys[7], part), 8)
    queries = draw_queries(jax.random.fold_in(jax.random.fold_in(keys[7], part), 71), part)
    inputs = draw_inputs(jax.random.fold_in(jax.random.fold_in(keys[7], part), 71), part)
    w_kv = draw_w_kv(jax.random.fold_in(keys[7], 71), part)
    rand_blocks = draw_rand_blocks(jax.random.fold_in(jax.random.fold_in(keys[7], part), 71), part)
    w_cross = draw_w_cross(jax.random.fold_in(keys[7], 71), part)
    vocab_table = draw_vocab_table(jax.random.fold_in(keys[7], 71), part)
    summary_ids = plant(ranked(part_keys[6], (SUM,), VOCAB, 2), jax.random.fold_in(part_keys[6], 3), 0, VOCAB - 1).astype(jnp.int32)
    return {"queries": queries, "inputs": inputs, "w_kv": w_kv, "rand_blocks": rand_blocks, "w_cross": w_cross, "vocab_table": vocab_table, "summary_ids": summary_ids}


MASKED_SCORE = -1e30


def split_heads(block_rows):
    return block_rows.astype(jnp.float32).reshape(block_rows.shape[0], HEADS, HEAD)


def window_rows(query_rows, key_rows, value_rows, valid):
    scores = jnp.einsum("qhe,khe->hqk", split_heads(query_rows), split_heads(key_rows)) * (HEAD ** -0.5)
    scores = jnp.where(valid[None, None, :], scores, MASKED_SCORE)
    scores = scores - jnp.max(scores, axis=2, keepdims=True)
    weights = jnp.exp(scores)
    weights = (weights / jnp.sum(weights, axis=2, keepdims=True)).astype(jnp.bfloat16)
    result = jnp.einsum("hqk,khe->qhe", weights.astype(jnp.float32), split_heads(value_rows))
    return result.reshape(query_rows.shape[0], HEADS * HEAD)


def full_rows(query_rows, key_heads, value_heads):
    scores = jnp.einsum("qhe,khe->hqk", split_heads(query_rows), key_heads) * (HEAD ** -0.5)
    weights = jnp.exp(scores - jnp.max(scores, axis=2, keepdims=True))
    totals = jnp.sum(weights, axis=2)
    result = jnp.einsum("hqk,khe->qhe", weights, value_heads, precision=lax.Precision.HIGHEST)
    return (result / jnp.transpose(totals)[:, :, None]).reshape(query_rows.shape[0], HEADS * HEAD)


def reference(queries, inputs, w_kv, rand_blocks, w_cross, vocab_table, summary_ids):
    seq_rows, feature_count = inputs.shape
    block_total = seq_rows // BLOCK
    pick_count = rand_blocks.shape[1]
    key_value = jnp.dot(inputs, w_kv, preferred_element_type=jnp.float32).astype(jnp.bfloat16)
    key_blocks = key_value[:, :feature_count].reshape(block_total, BLOCK, feature_count)
    value_blocks = key_value[:, feature_count:].reshape(block_total, BLOCK, feature_count)
    query_blocks = queries.reshape(block_total, BLOCK, feature_count)
    always = jnp.ones((), dtype=bool)

    def one_block(block_index):
        near = jnp.stack([block_index - 1, block_index, block_index + 1, 0 * block_index, 0 * block_index + block_total - 1])
        chosen = jnp.concatenate([near.astype(jnp.int32), rand_blocks[block_index].astype(jnp.int32)])
        chosen = jnp.clip(chosen, 0, block_total - 1).astype(jnp.int32)
        flags = jnp.concatenate([jnp.stack([block_index >= 2, always, block_index <= block_total - 3, always, always]), jnp.ones((pick_count,), dtype=bool)])
        valid = jnp.repeat(flags, BLOCK)
        key_rows = key_blocks[chosen].reshape(-1, feature_count)
        value_rows = value_blocks[chosen].reshape(-1, feature_count)
        return window_rows(query_blocks[block_index], key_rows, value_rows, valid)

    def one_group(group_index):
        return jax.vmap(one_block)(group_index * BLK_DEV + jnp.arange(BLK_DEV, dtype=jnp.int32))

    group_count = block_total // BLK_DEV
    sparse_out = lax.map(one_group, jnp.arange(group_count, dtype=jnp.int32)).reshape(block_total, BLOCK, feature_count)
    key_heads = split_heads(key_value[:, :feature_count])
    value_heads = split_heads(key_value[:, feature_count:])
    first_rows = full_rows(query_blocks[0], key_heads, value_heads)
    last_rows = full_rows(query_blocks[block_total - 1], key_heads, value_heads)
    sparse_out = sparse_out.at[0].set(first_rows).at[block_total - 1].set(last_rows)
    attended = sparse_out.reshape(seq_rows, feature_count).astype(jnp.bfloat16)
    encoded = (inputs.astype(jnp.float32) + attended.astype(jnp.float32)).astype(jnp.bfloat16)
    cross = jnp.dot(encoded, w_cross, preferred_element_type=jnp.float32).astype(jnp.bfloat16)
    cross_keys = split_heads(cross[:, :feature_count])
    cross_values = split_heads(cross[:, feature_count:])
    summary_queries = vocab_table[summary_ids]
    summary_count = summary_queries.shape[0]

    def summary_block(query_rows):
        return full_rows(query_rows, cross_keys, cross_values)

    summary = lax.map(summary_block, summary_queries.reshape(summary_count // 16, 16, feature_count))
    summary = summary.reshape(summary_count, feature_count).astype(jnp.bfloat16)
    return (attended, summary)
```

```python
import functools

import jax
import jax.numpy as jnp
from jax import lax
from jax.experimental import pallas as pl
from jax.experimental.pallas import tpu as pltpu
from jax.sharding import PartitionSpec as P

HEADS = 16
HEAD = 64
BLOCK = 64
LANES = 128
PAIRS = HEADS // 2
MASKED_SCORE = -1e30
MESH = pl.DeviceIdType.MESH
VMEM = pl.BlockSpec(memory_space=pltpu.VMEM)
ANY = pl.BlockSpec(memory_space=pl.ANY)
SMEM = pl.BlockSpec(memory_space=pltpu.SMEM)
VMEM_LIMIT = 48 * 1024 * 1024
FUSED_LIMIT = 60 * 1024 * 1024
HELD_LIMIT = 40 * 1024 * 1024


def greet_all(me, n):
    barrier = pltpu.get_barrier_semaphore()

    def greet(k, carry):
        peer = lax.rem(me + k, n)
        pl.semaphore_signal(barrier, inc=1, device_id={"ctx": peer}, device_id_type=MESH)
        return carry

    lax.fori_loop(1, n, greet, 0)
    pl.semaphore_wait(barrier, n - 1)


def push(source, target, send_sem, recv_sem, peer):
    return pltpu.make_async_remote_copy(
        source, target, send_sem, recv_sem, device_id={"ctx": peer}, device_id_type=MESH
    )


def each_peer(me, n, body):
    def step(k, carry):
        body(lax.rem(me + k, n))
        return carry

    lax.fori_loop(1, n, step, 0)


def gather_kernel(
    n,
    x_ref,
    q_ref,
    looked_ref,
    all_ref,
    ends_ref,
    got_ref,
    ring_send,
    ring_recv,
    side_send,
    side_recv,
    got_send,
    got_recv,
    ends_send,
    ends_recv,
    own_sem,
):
    me = lax.axis_index("ctx")
    chips = n // 2
    half = chips // 2
    core = me % 2
    chip = me // 2
    odd = chip % 2
    place = (1 - odd) * (chip // 2) + odd * (chips - 1 - chip // 2)
    sibling = me + 1 - 2 * core
    row_count = q_ref.shape[0]

    def device(at, on_core):
        at = (at + chips) % chips
        back = at // half
        return 2 * ((1 - back) * 2 * at + back * (2 * (chips - 1 - at) + 1)) + on_core

    streams = [(d, h) for h in range(2) for d in range(2)]

    def hops(d, h):
        return half if d == h else half - 1

    def ring(d, h, s):
        sign = 1 - 2 * d
        owner = device(place - sign * s, core)
        source = x_ref.at[h] if s == 0 else all_ref.at[owner, h]
        return push(
            source,
            all_ref.at[owner, h],
            ring_send.at[d, h, s],
            ring_recv.at[d, h, s],
            device(place + sign, core),
        )

    def arrival(d, h, s):
        owner = device(place - (1 - 2 * d) * (s + 1), core)
        landed = all_ref.at[owner, h]
        return push(landed, landed, ring_send.at[d, h, s], ring_recv.at[d, h, s], sibling)

    def side(d, h, s, on_core):
        owner = device(place - (1 - 2 * d) * s, on_core)
        source = all_ref.at[owner, h]
        if s == 0:
            source = x_ref.at[h]
        return push(
            source, all_ref.at[owner, h], side_send.at[d, h, s], side_recv.at[d, h, s], sibling
        )

    own = [pltpu.make_async_copy(x_ref.at[h], all_ref.at[me, h], own_sem.at[h]) for h in range(2)]
    own.append(pltpu.make_async_copy(looked_ref.at[me], got_ref.at[me], own_sem.at[2]))
    greet_all(me, n)
    for d, h in streams:
        ring(d, h, 0).start()

    def send_looked(peer):
        push(
            looked_ref.at[peer], got_ref.at[me], got_send.at[peer], got_recv.at[me], peer
        ).start()

    each_peer(me, n, send_looked)
    ends = [q_ref.at[pl.ds(0, BLOCK)], q_ref.at[pl.ds(row_count - BLOCK, BLOCK)]]
    holders = [0, n - 1]

    steps = [(place - at + chips) % chips for at in (0, half)]
    right, left = device(place + 1, core), device(place - 1, core)

    def send_end(e, k, source):
        peer = (right, left, sibling)[k]
        return push(source, ends_ref.at[e], ends_send.at[e, k], ends_recv.at[e], peer)

    def routes(e):
        away = steps[e]
        return [
            (0, away < half),
            (1, jnp.logical_or(away == 0, away > chips - half + 1)),
            (2, me == holders[e]),
        ]

    def start_routes(e, source):
        for k, goes in routes(e)[:2]:

            @pl.when(goes)
            def _():
                send_end(e, k, source).start()

    def pass_end(e):
        send_end(e, 0, ends_ref.at[e]).wait_recv()
        start_routes(e, ends_ref.at[e])

    for e in range(2):

        @pl.when(me == holders[e])
        def _():
            send_end(e, 2, ends[e]).start()
            start_routes(e, ends[e])
            copy = pltpu.make_async_copy(ends[e], ends_ref.at[e], own_sem.at[3])
            copy.start()
            copy.wait()

        @pl.when(jnp.logical_and(steps[e] == 0, me != holders[e]))
        def _():
            pass_end(e)

    for copy in own:
        copy.start()
    for h in range(2):
        side(0, h, 0, core).start()
    for s in range(half):
        for d, h in streams:
            if s < hops(d, h):
                arrival(d, h, s).wait_recv()
                if s + 1 < hops(d, h):
                    ring(d, h, s + 1).start()
                side(d, h, s + 1, core).start()
        for e in range(2):
            near = steps[e] == s + 1
            if s + 1 < half:
                near = jnp.logical_or(near, steps[e] == chips - s - 1)

            @pl.when(near)
            def _():
                pass_end(e)

    for h in range(2):
        side(0, h, 0, core).wait_send()
        side(0, h, 0, 1 - core).wait_recv()
    for s in range(half):
        for d, h in streams:
            if s < hops(d, h):
                ring(d, h, s).wait_send()
                side(d, h, s + 1, core).wait_send()
                side(d, h, s + 1, 1 - core).wait_recv()

    def end_looked(peer):
        copy = push(
            looked_ref.at[peer], got_ref.at[peer], got_send.at[peer], got_recv.at[peer], peer
        )
        copy.wait_recv()
        copy.wait_send()

    each_peer(me, n, end_looked)
    for e in range(2):
        for k, goes in routes(e):

            @pl.when(goes)
            def _():
                send_end(e, k, ends[e]).wait_send()

    for copy in own:
        copy.wait()


def gather_inputs(x, q, looked):
    n = lax.axis_size("ctx")
    rows, features = x.shape
    half = n // 4
    dma = pltpu.SemaphoreType.DMA
    gathered, ends, got = pl.pallas_call(
        functools.partial(gather_kernel, n),
        out_shape=[
            jax.ShapeDtypeStruct((n, 2, rows // 2, features), x.dtype),
            jax.ShapeDtypeStruct((2, BLOCK, features), q.dtype),
            jax.ShapeDtypeStruct(looked.shape, looked.dtype),
        ],
        in_specs=[ANY] * 3,
        out_specs=[ANY] * 3,
        scratch_shapes=[
            dma((2, 2, half)),
            dma((2, 2, half)),
            dma((2, 2, half + 1)),
            dma((2, 2, half + 1)),
            dma((n,)),
            dma((n,)),
            dma((2, 3)),
            dma((2,)),
            dma((4,)),
        ],
        compiler_params=pltpu.CompilerParams(collective_id=1, has_side_effects=True),
        name="gather_inputs",
    )(x.reshape(2, rows // 2, features), q, looked)
    return gathered.reshape(n * rows // BLOCK, BLOCK, features), ends, got


def ends_kernel(
    n,
    mine_ref,
    out_ref,
    log_ref,
    rows_ref,
    outs_ref,
    logs_ref,
    rows_send,
    rows_recv,
    ends_send,
    ends_recv,
    own_sem,
):
    me = lax.axis_index("ctx")
    holders = [0, n - 1]
    pairs = [(out_ref, outs_ref), (log_ref, logs_ref)]

    def end(e, i, slot):
        source, target = pairs[i]
        return push(
            source.at[e], target.at[slot], ends_send.at[e, i], ends_recv.at[i, slot], holders[e]
        )

    own = pltpu.make_async_copy(mine_ref, rows_ref.at[me], own_sem.at[2])
    own.start()
    greet_all(me, n)
    for e in range(2):

        @pl.when(me != holders[e])
        def _():
            for i in range(2):
                end(e, i, me).start()

        @pl.when(me == holders[e])
        def _():
            for i in range(2):
                source, target = pairs[i]
                copy = pltpu.make_async_copy(source.at[e], target.at[me], own_sem.at[i])
                copy.start()
                copy.wait()

    def send_rows(peer):
        push(mine_ref, rows_ref.at[me], rows_send.at[peer], rows_recv.at[me], peer).start()

    each_peer(me, n, send_rows)

    def end_rows(peer):
        copy = push(mine_ref, rows_ref.at[peer], rows_send.at[peer], rows_recv.at[peer], peer)
        copy.wait_recv()
        copy.wait_send()

    each_peer(me, n, end_rows)
    for e in range(2):

        @pl.when(me != holders[e])
        def _():
            for i in range(2):
                end(e, i, me).wait_send()

        @pl.when(me == holders[e])
        def _():
            def arrived(peer):
                for i in range(2):
                    source, target = pairs[i]
                    push(
                        source.at[e],
                        target.at[peer],
                        ends_send.at[e, i],
                        ends_recv.at[i, peer],
                        peer,
                    ).wait_recv()

            each_peer(me, n, arrived)

    own.wait()


def send_ends(mine, out, log):
    n = lax.axis_size("ctx")
    dma = pltpu.SemaphoreType.DMA
    out = out.reshape(2, BLOCK, out.shape[1])
    log = log.reshape(2, BLOCK, LANES)
    return pl.pallas_call(
        functools.partial(ends_kernel, n),
        out_shape=[
            jax.ShapeDtypeStruct((n,) + mine.shape, mine.dtype),
            jax.ShapeDtypeStruct((n,) + out.shape[1:], out.dtype),
            jax.ShapeDtypeStruct((n,) + log.shape[1:], log.dtype),
        ],
        in_specs=[ANY] * 3,
        out_specs=[ANY] * 3,
        scratch_shapes=[dma((n,)), dma((n,)), dma((2, 2)), dma((2, n)), dma((3,))],
        compiler_params=pltpu.CompilerParams(collective_id=2, has_side_effects=True),
        name="send_ends",
    )(mine, out, log)


def combine(outs_ref, logs_ref, total_ref):
    n, rows, features = outs_ref.shape
    peak = lax.fori_loop(
        1, n, lambda i, peak: jnp.maximum(peak, logs_ref[i]), logs_ref[0]
    )
    left = lax.broadcasted_iota(jnp.int32, (rows, LANES), 1) < HEAD
    total_ref[...] = jnp.zeros_like(total_ref)

    def spread(x, p):
        return jnp.where(left, x[:, 2 * p : 2 * p + 1], x[:, 2 * p + 1 : 2 * p + 2])

    def add(i, total):
        weights = jnp.exp(logs_ref[i] - peak)
        for p in range(PAIRS):
            lanes = slice(p * LANES, (p + 1) * LANES)
            total_ref[:, lanes] += outs_ref[i, :, lanes].astype(jnp.float32) * spread(weights, p)
        return total + weights

    scale = 1.0 / lax.fori_loop(0, n, add, jnp.zeros((rows, LANES), jnp.float32))
    for p in range(PAIRS):
        lanes = slice(p * LANES, (p + 1) * LANES)
        total_ref[:, lanes] = total_ref[:, lanes] * spread(scale, p)


def summary_kernel(
    n,
    part_ref,
    log_ref,
    out_ref,
    outs_ref,
    logs_ref,
    total_ref,
    send_sem,
    recv_sem,
    own_sem,
):
    me = lax.axis_index("ctx")
    pairs = [(part_ref, outs_ref), (log_ref, logs_ref)]
    own = [
        pltpu.make_async_copy(source.at[me], target.at[me], own_sem.at[i])
        for i, (source, target) in enumerate(pairs)
    ]
    for copy in own:
        copy.start()
    greet_all(me, n)

    def copies(peer, slot):
        return [
            push(
                source.at[peer], target.at[slot], send_sem.at[i, peer], recv_sem.at[i, slot], peer
            )
            for i, (source, target) in enumerate(pairs)
        ]

    def send(peer):
        for copy in copies(peer, me):
            copy.start()

    each_peer(me, n, send)

    def finish(peer):
        for copy in copies(peer, peer):
            copy.wait_recv()
            copy.wait_send()

    each_peer(me, n, finish)
    for copy in own:
        copy.wait()
    combine(outs_ref, logs_ref, total_ref)
    out_ref[...] = total_ref[...].astype(out_ref.dtype)


def combined_summary(part, logs):
    n, share, features = part.shape
    dma = pltpu.SemaphoreType.DMA
    return pl.pallas_call(
        functools.partial(summary_kernel, n),
        out_shape=jax.ShapeDtypeStruct((share, features), jnp.bfloat16),
        in_specs=[ANY] * 2,
        out_specs=VMEM,
        scratch_shapes=[
            pltpu.VMEM(part.shape, part.dtype),
            pltpu.VMEM(logs.shape, logs.dtype),
            pltpu.VMEM((share, features), jnp.float32),
            dma((2, n)),
            dma((2, n)),
            dma((2,)),
        ],
        compiler_params=pltpu.CompilerParams(collective_id=3, has_side_effects=True),
        name="combined_summary",
    )(part, logs)


def dot_t(a, b):
    return lax.dot_general(a, b, (((1,), (1,)), ((), ())), preferred_element_type=jnp.float32)


def stacked_pair(q):
    q = q * jnp.asarray(HEAD**-0.5, q.dtype)
    left = lax.broadcasted_iota(jnp.int32, q.shape, 1) < HEAD
    zero = jnp.zeros_like(q)
    return jnp.concatenate([jnp.where(left, q, zero), jnp.where(left, zero, q)], axis=0)


def unstacked_pair(o):
    rows = o.shape[0] // 2
    left = lax.broadcasted_iota(jnp.int32, (rows, LANES), 1) < HEAD
    return jnp.where(left, o[:rows], o[rows:])


def project(x_ref, w_ref, out_ref, tile):
    rows, cols = out_ref.shape
    width = 512

    def step(t, carry):
        at = pl.ds(pl.multiple_of(t * tile, tile), tile)
        x = x_ref[at, :]
        for c in range(cols // width):
            y = jnp.dot(
                x, w_ref[:, c * width : (c + 1) * width], preferred_element_type=jnp.float32
            )
            out_ref[at, c * width : (c + 1) * width] = y.astype(out_ref.dtype)
        return carry

    lax.fori_loop(0, rows // tile, step, 0)


def partial_attention(q_ref, kv_ref, out_ref, log_ref):
    rows, features = q_ref.shape
    place = lax.broadcasted_iota(jnp.int32, (rows, LANES), 1)
    logs = jnp.zeros((rows, LANES), jnp.float32)
    for p in range(PAIRS):
        lanes = slice(p * LANES, (p + 1) * LANES)
        values = slice(features + p * LANES, features + (p + 1) * LANES)
        scores = dot_t(stacked_pair(q_ref[:, lanes]), kv_ref[:, lanes])
        peak = jnp.max(scores, axis=1, keepdims=True)
        weights = jnp.exp(scores - peak)
        totals = jnp.sum(weights, axis=1, keepdims=True)
        sums = jnp.dot(
            weights.astype(jnp.bfloat16), kv_ref[:, values], preferred_element_type=jnp.float32
        )
        out_ref[:, lanes] = unstacked_pair(sums / totals).astype(out_ref.dtype)
        log = peak + jnp.log(totals)
        logs = jnp.where(place == 2 * p, log[:rows], logs)
        logs = jnp.where(place == 2 * p + 1, log[rows:], logs)
    log_ref[...] = logs


def global_kernel(q_ref, x_ref, w_ref, out_ref, log_ref, kv_ref):
    project(x_ref, w_ref, kv_ref, 128)
    partial_attention(q_ref, kv_ref, out_ref, log_ref)


def global_partial(q, x, w):
    return pl.pallas_call(
        global_kernel,
        out_shape=[
            jax.ShapeDtypeStruct(q.shape, jnp.bfloat16),
            jax.ShapeDtypeStruct((q.shape[0], LANES), jnp.float32),
        ],
        in_specs=[VMEM] * 3,
        out_specs=[VMEM] * 2,
        scratch_shapes=[pltpu.VMEM((x.shape[0], w.shape[1]), jnp.bfloat16)],
        compiler_params=pltpu.CompilerParams(vmem_limit_bytes=VMEM_LIMIT),
        cost_estimate=pl.CostEstimate(
            flops=2 * x.size * w.shape[1], bytes_accessed=6 << 20, transcendentals=1 << 20
        ),
        name="global_partial",
    )(q, x, w)


def block_kernel(
    pick_count,
    ids_ref,
    edge_ref,
    all_ref,
    q_ref,
    x_ref,
    w_kv_ref,
    w_cross_ref,
    outs_ref,
    logs_ref,
    sq_ref,
    attended_ref,
    out_ref,
    log_ref,
    rows_ref,
    kv_ref,
    total_ref,
    sem,
):
    row_count, features = x_ref.shape
    block_count = row_count // BLOCK
    slots = rows_ref.shape[0] // BLOCK
    far_start = (block_count + 4) * BLOCK
    span = (5 + pick_count) * BLOCK

    def fetch(i):
        return pltpu.make_async_copy(
            all_ref.at[ids_ref[i]],
            rows_ref.at[pl.ds(pl.multiple_of(i * BLOCK, BLOCK), BLOCK)],
            sem.at[i],
        )

    for i in range(slots):
        fetch(i).start()
    for i in range(slots):
        fetch(i).wait()
    project(rows_ref, w_kv_ref, kv_ref, 2 * BLOCK)

    column = lax.broadcasted_iota(jnp.int32, (2 * BLOCK, span), 1)

    def one_block(b, carry):
        first = edge_ref[0] + b
        hidden = jnp.logical_or(
            jnp.logical_and(column < BLOCK, first < 2),
            jnp.logical_and(
                jnp.logical_and(column >= 2 * BLOCK, column < 3 * BLOCK), first > edge_ref[1] - 3
            ),
        )
        near = pl.ds(pl.multiple_of(b * BLOCK, BLOCK), 3 * BLOCK)
        ends = pl.ds((block_count + 2) * BLOCK, 2 * BLOCK)
        far = pl.ds(
            pl.multiple_of(far_start + b * pick_count * BLOCK, BLOCK), pick_count * BLOCK
        )
        here = pl.ds(pl.multiple_of(b * BLOCK, BLOCK), BLOCK)
        for p in range(PAIRS):
            lanes = slice(p * LANES, (p + 1) * LANES)
            values = slice(features + p * LANES, features + (p + 1) * LANES)
            k = jnp.concatenate(
                [kv_ref[near, lanes], kv_ref[ends, lanes], kv_ref[far, lanes]], axis=0
            )
            v = jnp.concatenate(
                [kv_ref[near, values], kv_ref[ends, values], kv_ref[far, values]], axis=0
            )
            scores = dot_t(stacked_pair(q_ref[here, lanes]), k)
            scores = jnp.where(hidden, MASKED_SCORE, scores)
            weights = jnp.exp(scores - jnp.max(scores, axis=1, keepdims=True))
            totals = jnp.sum(weights, axis=1, keepdims=True)
            probs = (weights * (1.0 / totals)).astype(jnp.bfloat16)
            o = jnp.dot(probs, v, preferred_element_type=jnp.float32)
            attended_ref[here, lanes] = unstacked_pair(o).astype(jnp.bfloat16)
        return carry

    lax.fori_loop(0, block_count, one_block, 0)

    def place(rows):
        combine(outs_ref, logs_ref, total_ref)
        attended_ref[rows] = total_ref[...].astype(jnp.bfloat16)

    @pl.when(edge_ref[0] == 0)
    def _():
        place(slice(0, BLOCK))

    @pl.when(edge_ref[0] + block_count == edge_ref[1])
    def _():
        place(slice(row_count - BLOCK, row_count))

    encoded = x_ref[...].astype(jnp.float32) + attended_ref[...].astype(jnp.float32)
    rows_ref[:row_count] = encoded.astype(jnp.bfloat16)
    project(rows_ref.at[:row_count], w_cross_ref, kv_ref.at[:row_count], 2 * BLOCK)
    partial_attention(sq_ref, kv_ref.at[:row_count], out_ref, log_ref)


def block_attention(ids, edge, everything, q, x, w_kv, w_cross, outs, end_logs, sq, pick_count):
    slots = ids.shape[0]
    features = x.shape[1]
    return pl.pallas_call(
        functools.partial(block_kernel, pick_count),
        out_shape=[
            jax.ShapeDtypeStruct(q.shape, jnp.bfloat16),
            jax.ShapeDtypeStruct(sq.shape, jnp.bfloat16),
            jax.ShapeDtypeStruct((sq.shape[0], LANES), jnp.float32),
        ],
        in_specs=[SMEM, SMEM, ANY] + [VMEM] * 7,
        out_specs=[VMEM] * 3,
        scratch_shapes=[
            pltpu.VMEM((slots * BLOCK, features), jnp.bfloat16),
            pltpu.VMEM((slots * BLOCK, 2 * features), jnp.bfloat16),
            pltpu.VMEM((BLOCK, features), jnp.float32),
            pltpu.SemaphoreType.DMA((slots,)),
        ],
        compiler_params=pltpu.CompilerParams(vmem_limit_bytes=VMEM_LIMIT),
        cost_estimate=pl.CostEstimate(
            flops=20 << 30, bytes_accessed=16 << 20, transcendentals=5 << 20
        ),
        name="block_attention",
    )(ids, edge, everything, q, x, w_kv, w_cross, outs, end_logs, sq)


def staged(queries, inputs, w_kv, rand_blocks, w_cross, vocab_table, summary_ids):
    n = lax.axis_size("ctx")
    position = lax.axis_index("ctx")
    row_count, features = inputs.shape
    block_count = row_count // BLOCK
    pick_count = rand_blocks.shape[1]
    total_blocks = block_count * n
    shard_rows = vocab_table.shape[0]
    summary_count = summary_ids.shape[0]
    share = summary_count // n
    offsets = summary_ids - position * shard_rows
    inside = jnp.logical_and(offsets >= 0, offsets < shard_rows)
    looked = vocab_table[jnp.clip(offsets, 0, shard_rows - 1)]
    looked = jnp.where(inside[:, None], looked, jnp.zeros((), looked.dtype))
    everything, end_queries, got = gather_inputs(
        inputs, queries, looked.reshape(n, share, features)
    )
    mine = jnp.sum(got.astype(jnp.float32), axis=0).astype(jnp.bfloat16)
    end_out, end_log = global_partial(end_queries.reshape(2 * BLOCK, features), inputs, w_kv)
    rows, outs, end_logs = send_ends(mine, end_out, end_log)
    summary_queries = rows.reshape(summary_count, features)

    start = position * block_count
    near = jnp.clip(start - 1 + jnp.arange(block_count + 2, dtype=jnp.int32), 0, total_blocks - 1)
    fixed = jnp.array([0, total_blocks - 1], jnp.int32)
    picks = lax.dynamic_slice_in_dim(rand_blocks, start, block_count, 0).reshape(-1)
    ids = jnp.concatenate([near, fixed, picks.astype(jnp.int32)])
    edge = jnp.stack([start, jnp.full_like(start, total_blocks)]).astype(jnp.int32)
    attended, part, logs = block_attention(
        ids,
        edge,
        everything,
        queries,
        inputs,
        w_kv,
        w_cross,
        outs,
        end_logs,
        summary_queries,
        pick_count,
    )
    summary = combined_summary(
        part.reshape(n, share, features), logs.reshape(n, share, LANES)
    )
    return attended, summary


def dots(x, w_ref, store):
    width = 512
    for c in range(w_ref.shape[1] // width):
        cols = slice(c * width, (c + 1) * width)
        y = jnp.dot(x, w_ref[:, cols], preferred_element_type=jnp.float32)
        store(cols, y.astype(jnp.bfloat16))


def with_log(log, rows):
    place = lax.broadcasted_iota(jnp.int32, (rows, LANES), 1)
    high = log.astype(jnp.bfloat16)
    rest = log - high.astype(jnp.float32)
    middle = rest.astype(jnp.bfloat16)
    low = (rest - middle.astype(jnp.float32)).astype(jnp.bfloat16)
    low, middle = low.astype(jnp.float32), middle.astype(jnp.float32)
    packed = jnp.where(place < HEADS, high.astype(jnp.float32), 0.0)
    packed = jnp.where(place // HEADS == 1, pltpu.roll(middle, HEADS, 1), packed)
    packed = jnp.where(place // HEADS == 2, pltpu.roll(low, 2 * HEADS, 1), packed)
    return packed.astype(jnp.bfloat16)


def without_log(packed):
    packed = packed.astype(jnp.float32)
    middle = pltpu.roll(packed, LANES - HEADS, 1)
    low = pltpu.roll(packed, LANES - 2 * HEADS, 1)
    return packed + (middle + low)


def fused_kernel(
    n,
    picks_ref,
    sids_ref,
    x_ref,
    q_hbm,
    w_kv_hbm,
    w_cross_hbm,
    vocab_hbm,
    attended_ref,
    summary_ref,
    x_all,
    kv_all,
    w_kv_ref,
    w_cross_ref,
    q_ref,
    vocab_ref,
    looked_ref,
    sibq_ref,
    chipq_ref,
    partq_ref,
    mine_ref,
    sumq_ref,
    acc_ref,
    peak_ref,
    sum_ref,
    encoded_ref,
    cross_ref,
    part_ref,
    sibp_ref,
    chipp_ref,
    got_ref,
    total_ref,
    ring_send,
    ring_recv,
    side_send,
    side_recv,
    own_send,
    own_recv,
    pair_send,
    pair_recv,
    across_send,
    across_recv,
    local_sem,
):
    me = lax.axis_index("ctx")
    chips = n // 2
    half = chips // 2
    core = me % 2
    chip = me // 2
    odd = chip % 2
    place = (1 - odd) * (chip // 2) + odd * (chips - 1 - chip // 2)
    sibling = me + 1 - 2 * core
    blocks = x_ref.shape[0]
    features = x_ref.shape[2]
    rows = blocks * BLOCK
    share = summary_ref.shape[0]
    steps = (half - 1) * blocks + blocks // 2
    total_blocks = n * blocks
    holder = jnp.logical_or(me == 0, me == n - 1)

    def device(at, on_core):
        at = (at + chips) % chips
        back = at // half
        return 2 * ((1 - back) * 2 * at + back * (2 * (chips - 1 - at) + 1)) + on_core

    def block_of(d, t):
        j = t % blocks
        return j if d == 0 else blocks - 1 - j

    def ring(d, t):
        owner = device(place - (1 - 2 * d) * (t // blocks), core)
        return push(
            x_all.at[owner, block_of(d, t)],
            x_all.at[owner, block_of(d, t)],
            ring_send.at[d, t],
            ring_recv.at[d, t],
            device(place + 1 - 2 * d, core),
        )

    def ring_own(d, t):
        return push(
            x_ref.at[block_of(d, t)],
            x_all.at[me, block_of(d, t)],
            ring_send.at[d, t],
            ring_recv.at[d, t],
            device(place + 1 - 2 * d, core),
        )

    def owner_of(d, t, on_core):
        return device(place - (1 - 2 * d) * (t // blocks + 1), on_core)

    def arrival(d, t):
        landed = x_all.at[owner_of(d, t, core), block_of(d, t)]
        return push(landed, landed, ring_send.at[d, t], ring_recv.at[d, t], sibling)

    def side(d, t, on_core):
        landed = x_all.at[owner_of(d, t, on_core), block_of(d, t)]
        return push(landed, landed, side_send.at[d, t], side_recv.at[d, t], sibling)

    def side_own(on):
        return push(x_ref, x_all.at[on], own_send, own_recv, sibling)

    def peer_of(k):
        other = lax.rem(chip + k, chips)
        return other, 2 * other + core

    loads = [
        pltpu.make_async_copy(source, target, local_sem.at[i])
        for i, (source, target) in enumerate(
            [
                (vocab_hbm, vocab_ref),
                (w_kv_hbm, w_kv_ref),
                (x_ref, x_all.at[me]),
                (q_hbm, q_ref),
                (w_cross_hbm, w_cross_ref),
            ]
        )
    ]
    for load in loads:
        load.start()

    barrier = pltpu.get_barrier_semaphore()
    pl.semaphore_signal(barrier, inc=1, device_id={"ctx": sibling}, device_id_type=MESH)
    for k in range(1, chips):
        pl.semaphore_signal(
            barrier, inc=1, device_id={"ctx": peer_of(k)[1]}, device_id_type=MESH
        )
    pl.semaphore_wait(barrier, chips)

    for t in range(blocks):
        for d in range(2):
            ring_own(d, t).start()
    side_own(me).start()

    loads[0].wait()
    shard_rows = vocab_ref.shape[0]
    summary_count = sids_ref.shape[1]
    offsets = sids_ref[...] - me * shard_rows
    hot = lax.broadcasted_iota(jnp.int32, (shard_rows, summary_count), 0) == offsets
    hot = jnp.where(hot, 1.0, 0.0).astype(jnp.bfloat16)
    looked = lax.dot_general(
        hot, vocab_ref[...], (((0,), (0,)), ((), ())), preferred_element_type=jnp.float32
    ).astype(jnp.bfloat16)
    for k in range(chips):
        for c in range(2):
            at = (2 * k + c) * share
            looked_ref[c, k] = looked[at : at + share]

    def pair_q():
        return push(
            looked_ref.at[1 - core], sibq_ref, pair_send.at[0], pair_recv.at[0], sibling
        )

    pair_q().start()
    loads[1].wait()
    loads[2].wait()

    def project_owner(owner):
        def step(t, carry):
            x = x_all[owner, pl.ds(2 * t, 2)].reshape(2 * BLOCK, features)

            def store(cols, y):
                kv_all[pl.ds(owner * blocks + 2 * t, 2), :, cols] = y.reshape(2, BLOCK, -1)

            dots(x, w_kv_ref, store)
            return carry

        lax.fori_loop(0, blocks // 2, step, 0)

    project_owner(me)
    pair_q().wait_recv()
    chipq_ref[...] = looked_ref[core] + sibq_ref[...]

    def across_q(k, slot):
        other, peer = peer_of(k)
        return push(
            chipq_ref.at[other],
            partq_ref.at[slot],
            across_send.at[0, k],
            across_recv.at[0, slot],
            peer,
        )

    for k in range(1, chips):
        across_q(k, chip).start()
    partq_ref[chip] = chipq_ref[chip]
    side_own(sibling).wait_recv()
    project_owner(sibling)

    loads[3].wait()
    end_row = pl.multiple_of(jnp.where(me == 0, 0, rows - BLOCK), BLOCK)

    def take_keys(parts):
        for p in range(PAIRS):
            lanes = slice(p * LANES, (p + 1) * LANES)
            values = slice(features + p * LANES, features + (p + 1) * LANES)
            q = stacked_pair(q_ref[pl.ds(end_row, BLOCK), lanes])
            k = jnp.concatenate([kv_all[at, :, lanes] for at in parts], axis=0)
            v = jnp.concatenate([kv_all[at, :, values] for at in parts], axis=0)
            k, v = k.reshape(-1, LANES), v.reshape(-1, LANES)
            scores = dot_t(q, k)
            before = peak_ref[p]
            peak = jnp.maximum(before, jnp.max(scores, axis=1, keepdims=True))
            weights = jnp.exp(scores - peak[:, :1])
            fade = jnp.exp(before - peak)
            peak_ref[p] = peak
            sum_ref[p] = sum_ref[p] * fade + jnp.sum(weights, axis=1, keepdims=True)
            acc_ref[p] = acc_ref[p] * fade + jnp.dot(
                weights.astype(jnp.bfloat16), v, preferred_element_type=jnp.float32
            )

    @pl.when(holder)
    def _():
        peak_ref[...] = jnp.full_like(peak_ref, MASKED_SCORE)
        sum_ref[...] = jnp.zeros_like(sum_ref)
        acc_ref[...] = jnp.zeros_like(acc_ref)
        for i in range(2):
            take_keys([pl.ds((2 * chip + i) * blocks, blocks)])

    def process(found):
        x = jnp.concatenate([x_all[owner, block] for owner, block in found], axis=0)
        parts = [owner * blocks + block for owner, block in found]

        def store(cols, y):
            for i, at in enumerate(parts):
                kv_all[at, :, cols] = y[i * BLOCK : (i + 1) * BLOCK]

        dots(x, w_kv_ref, store)

        @pl.when(holder)
        def _():
            take_keys(parts)

    def own_blocks(t):
        return [(owner_of(d, t, core), block_of(d, t)) for d in range(2)]

    def side_blocks(t):
        return [(owner_of(d, t, 1 - core), block_of(d, t)) for d in range(2)]

    def pass_on(t):
        for d in range(2):
            arrival(d, t).wait_recv()

            @pl.when(t + blocks < steps)
            def _():
                ring(d, t + blocks).start()

            side(d, t, core).start()

    def first(t):
        pass_on(t)
        process(own_blocks(t))

    def one_step(t, carry):
        pass_on(t)
        for d in range(2):
            side(d, t - 1, 1 - core).wait_recv()
        process(own_blocks(t) + side_blocks(t - 1))
        return carry

    first(0)
    lax.fori_loop(1, steps, one_step, 0)

    for k in range(1, chips):
        other, _ = peer_of(k)
        across_q(k, other).wait_recv()
    mine = partq_ref[0].astype(jnp.float32)
    for k in range(1, chips):
        mine = mine + partq_ref[k].astype(jnp.float32)
    mine_ref[...] = mine.astype(jnp.bfloat16)

    def spread_q(k, slot):
        _, peer = peer_of(k)
        return push(
            mine_ref, sumq_ref.at[core, slot], across_send.at[1, k], across_recv.at[1, slot], peer
        )

    for k in range(1, chips):
        spread_q(k, chip).start()
    sumq_ref[core, chip] = mine_ref[...]

    for d in range(2):
        side(d, steps - 1, 1 - core).wait_recv()
    process(side_blocks(steps - 1))

    start = me * blocks
    span = (5 + picks_ref.shape[0]) * BLOCK
    column = lax.broadcasted_iota(jnp.int32, (2 * BLOCK, span), 1)

    def one_block(b, carry):
        here = start + b
        hidden = jnp.logical_or(
            jnp.logical_and(column < BLOCK, here < 2),
            jnp.logical_and(column // BLOCK == 2, here > total_blocks - 3),
        )
        chosen = [
            jnp.maximum(here - 1, 0),
            here,
            jnp.minimum(here + 1, total_blocks - 1),
            0,
            total_blocks - 1,
        ] + [picks_ref[i, here] for i in range(picks_ref.shape[0])]
        out = pl.ds(pl.multiple_of(b * BLOCK, BLOCK), BLOCK)
        for p in range(PAIRS):
            lanes = slice(p * LANES, (p + 1) * LANES)
            values = slice(features + p * LANES, features + (p + 1) * LANES)
            k = jnp.concatenate([kv_all[at, :, lanes] for at in chosen], axis=0)
            v = jnp.concatenate([kv_all[at, :, values] for at in chosen], axis=0)
            scores = dot_t(stacked_pair(q_ref[out, lanes]), k)
            scores = jnp.where(hidden, MASKED_SCORE, scores)
            weights = jnp.exp(scores - jnp.max(scores, axis=1, keepdims=True))
            totals = jnp.sum(weights, axis=1, keepdims=True)
            o = jnp.dot(weights.astype(jnp.bfloat16), v, preferred_element_type=jnp.float32)
            attended_ref[out, lanes] = unstacked_pair(o * (1.0 / totals)).astype(jnp.bfloat16)
        return carry

    lax.fori_loop(0, blocks, one_block, 0)

    @pl.when(holder)
    def _():
        for p in range(PAIRS):
            lanes = slice(p * LANES, (p + 1) * LANES)
            attended_ref[pl.ds(end_row, BLOCK), lanes] = unstacked_pair(
                acc_ref[p] * (1.0 / sum_ref[p])
            ).astype(jnp.bfloat16)

    encoded = x_all[me].reshape(rows, features).astype(jnp.float32)
    encoded = encoded + attended_ref[...].astype(jnp.float32)
    encoded_ref[...] = encoded.astype(jnp.bfloat16)
    loads[4].wait()
    project(encoded_ref, w_cross_ref, cross_ref, 2 * BLOCK)

    for k in range(1, chips):
        other, _ = peer_of(k)
        spread_q(k, other).wait_recv()

    def pair_all(c):
        return push(sumq_ref.at[c], sumq_ref.at[c], pair_send.at[1], pair_recv.at[1], sibling)

    pair_all(core).start()

    group = chips * share
    width = features + LANES

    def summary_half(c):
        place_ = lax.broadcasted_iota(jnp.int32, (group, LANES), 1)
        logs = jnp.zeros((group, LANES), jnp.float32)
        for p in range(PAIRS):
            lanes = slice(p * LANES, (p + 1) * LANES)
            values = slice(features + p * LANES, features + (p + 1) * LANES)
            q = stacked_pair(sumq_ref[c, :, :, lanes].reshape(group, LANES))
            scores = dot_t(q, cross_ref[:, lanes])
            peak = jnp.max(scores, axis=1, keepdims=True)
            weights = jnp.exp(scores - peak)
            totals = jnp.sum(weights, axis=1, keepdims=True)
            sums = jnp.dot(
                weights.astype(jnp.bfloat16),
                cross_ref[:, values],
                preferred_element_type=jnp.float32,
            )
            part = unstacked_pair(sums * (1.0 / totals)).astype(jnp.bfloat16)
            part_ref[c, :, :, lanes] = part.reshape(chips, share, LANES)
            log = peak + jnp.log(totals)
            logs = jnp.where(place_ == 2 * p, log[:group], logs)
            logs = jnp.where(place_ == 2 * p + 1, log[group:], logs)
        part_ref[c, :, :, features:width] = with_log(logs, group).reshape(chips, share, LANES)

    pair_all(1 - core).wait_recv()
    summary_half(1 - core)

    def pair_part():
        return push(part_ref.at[1 - core], sibp_ref, pair_send.at[2], pair_recv.at[2], sibling)

    pair_part().start()
    summary_half(core)
    pair_part().wait_recv()

    left = lax.broadcasted_iota(jnp.int32, (group, LANES), 1) < HEAD

    def spread(x, p, left):
        return jnp.where(left, x[:, 2 * p : 2 * p + 1], x[:, 2 * p + 1 : 2 * p + 2])

    a = part_ref.at[core]
    log_a = without_log(a[:, :, features:width].reshape(group, LANES))
    log_b = without_log(sibp_ref[:, :, features:width].reshape(group, LANES))
    peak = jnp.maximum(log_a, log_b)
    weight_a = jnp.exp(log_a - peak)
    weight_b = jnp.exp(log_b - peak)
    total = weight_a + weight_b
    weight_a, weight_b = weight_a / total, weight_b / total
    for p in range(PAIRS):
        lanes = slice(p * LANES, (p + 1) * LANES)
        mixed = a[:, :, lanes].reshape(group, LANES).astype(jnp.float32) * spread(
            weight_a, p, left
        ) + sibp_ref[:, :, lanes].reshape(group, LANES).astype(jnp.float32) * spread(
            weight_b, p, left
        )
        chipp_ref[:, :, lanes] = mixed.astype(jnp.bfloat16).reshape(chips, share, LANES)
    chipp_ref[:, :, features:width] = with_log(peak + jnp.log(total), group).reshape(
        chips, share, LANES
    )

    def across_p(k, slot):
        other, peer = peer_of(k)
        return push(
            chipp_ref.at[other], got_ref.at[slot], across_send.at[2, k], across_recv.at[2, slot], peer
        )

    for k in range(1, chips):
        across_p(k, chip).start()
    got_ref[chip] = chipp_ref[chip]
    for k in range(1, chips):
        other, _ = peer_of(k)
        across_p(k, other).wait_recv()
    left = lax.broadcasted_iota(jnp.int32, (share, LANES), 1) < HEAD
    logs = [without_log(got_ref[k, :, features:width]) for k in range(chips)]
    peak = functools.reduce(jnp.maximum, logs)
    weights = [jnp.exp(log - peak) for log in logs]
    scale = 1.0 / functools.reduce(jnp.add, weights)
    weights = [w * scale for w in weights]
    for p in range(PAIRS):
        lanes = slice(p * LANES, (p + 1) * LANES)
        total = jnp.zeros((share, LANES), jnp.float32)
        for k in range(chips):
            total = total + got_ref[k, :, lanes].astype(jnp.float32) * spread(weights[k], p, left)
        summary_ref[:, lanes] = total.astype(jnp.bfloat16)

    def sent(t, carry):
        for d in range(2):
            ring(d, t).wait_send()
            side(d, t, core).wait_send()
        return carry

    lax.fori_loop(0, steps, sent, 0)
    side_own(me).wait_send()
    pair_q().wait_send()
    pair_all(core).wait_send()
    pair_part().wait_send()
    for k in range(1, chips):
        across_q(k, chip).wait_send()
        spread_q(k, chip).wait_send()
        across_p(k, chip).wait_send()


def fused(queries, inputs, w_kv, rand_blocks, w_cross, vocab_table, summary_ids):
    n = lax.axis_size("ctx")
    rows, features = inputs.shape
    blocks = rows // BLOCK
    chips = n // 2
    half = chips // 2
    steps = (half - 1) * blocks + blocks // 2
    share = summary_ids.shape[0] // n
    group = chips * share
    wide = features + LANES
    bf16, f32 = jnp.bfloat16, jnp.float32
    dma = pltpu.SemaphoreType.DMA
    return pl.pallas_call(
        functools.partial(fused_kernel, n),
        out_shape=[
            jax.ShapeDtypeStruct(queries.shape, bf16),
            jax.ShapeDtypeStruct((share, features), bf16),
        ],
        in_specs=[SMEM, VMEM] + [ANY] * 5,
        out_specs=[VMEM] * 2,
        scratch_shapes=[
            pltpu.VMEM((n, blocks, BLOCK, features), bf16),
            pltpu.VMEM((n * blocks, BLOCK, 2 * features), bf16),
            pltpu.VMEM(w_kv.shape, bf16),
            pltpu.VMEM(w_cross.shape, bf16),
            pltpu.VMEM(queries.shape, bf16),
            pltpu.VMEM(vocab_table.shape, bf16),
            pltpu.VMEM((2, chips, share, features), bf16),
            pltpu.VMEM((chips, share, features), bf16),
            pltpu.VMEM((chips, share, features), bf16),
            pltpu.VMEM((chips, share, features), bf16),
            pltpu.VMEM((share, features), bf16),
            pltpu.VMEM((2, chips, share, features), bf16),
            pltpu.VMEM((PAIRS, 2 * BLOCK, LANES), f32),
            pltpu.VMEM((PAIRS, 2 * BLOCK, LANES), f32),
            pltpu.VMEM((PAIRS, 2 * BLOCK, LANES), f32),
            pltpu.VMEM((rows, features), bf16),
            pltpu.VMEM((rows, 2 * features), bf16),
            pltpu.VMEM((2, chips, share, wide), bf16),
            pltpu.VMEM((chips, share, wide), bf16),
            pltpu.VMEM((chips, share, wide), bf16),
            pltpu.VMEM((chips, share, wide), bf16),
            pltpu.VMEM((share, features), f32),
            dma((2, steps)),
            dma((2, steps)),
            dma((2, steps)),
            dma((2, steps)),
            dma,
            dma,
            dma((3,)),
            dma((3,)),
            dma((3, chips)),
            dma((3, chips)),
            dma((5,)),
        ],
        compiler_params=pltpu.CompilerParams(
            collective_id=4, has_side_effects=True, vmem_limit_bytes=FUSED_LIMIT
        ),
        name="fused",
    )(
        rand_blocks.T,
        summary_ids.reshape(1, -1),
        inputs.reshape(blocks, BLOCK, features),
        queries,
        w_kv,
        w_cross,
        vocab_table,
    )


def local(queries, inputs, w_kv, rand_blocks, w_cross, vocab_table, summary_ids):
    n = lax.axis_size("ctx")
    held = 3 * n * inputs.size * 2
    path = fused if held <= HELD_LIMIT else staged
    return path(queries, inputs, w_kv, rand_blocks, w_cross, vocab_table, summary_ids)


def solution(mesh):
    return jax.shard_map(
        local,
        mesh=mesh,
        in_specs=(
            P(("groups", "ctx"), None),
            P(("groups", "ctx"), None),
            P(),
            P("groups", None),
            P(),
            P("ctx", None),
            P("groups"),
        ),
        out_specs=(P(("groups", "ctx"), None), P(("groups", "ctx"), None)),
        check_vma=False,
    )
```

```python
import functools

import jax
import jax.numpy as jnp
from jax import lax
from jax.experimental import pallas as pl
from jax.experimental.pallas import tpu as pltpu
from jax.sharding import PartitionSpec as P

HEADS = 16
HEAD = 64
BLOCK = 64
LANES = 128
PAIRS = HEADS // 2
MASKED_SCORE = -1e30
MESH = pl.DeviceIdType.MESH
VMEM = pl.BlockSpec(memory_space=pltpu.VMEM)
ANY = pl.BlockSpec(memory_space=pl.ANY)
SMEM = pl.BlockSpec(memory_space=pltpu.SMEM)
VMEM_LIMIT = 48 * 1024 * 1024
FUSED_LIMIT = 60 * 1024 * 1024
HELD_LIMIT = 40 * 1024 * 1024


def greet_all(me, n):
    barrier = pltpu.get_barrier_semaphore()

    def greet(k, carry):
        peer = lax.rem(me + k, n)
        pl.semaphore_signal(barrier, inc=1, device_id={"ctx": peer}, device_id_type=MESH)
        return carry

    lax.fori_loop(1, n, greet, 0)
    pl.semaphore_wait(barrier, n - 1)


def push(source, target, send_sem, recv_sem, peer):
    return pltpu.make_async_remote_copy(
        source, target, send_sem, recv_sem, device_id={"ctx": peer}, device_id_type=MESH
    )


def each_peer(me, n, body):
    def step(k, carry):
        body(lax.rem(me + k, n))
        return carry

    lax.fori_loop(1, n, step, 0)


def gather_kernel(
    n,
    x_ref,
    q_ref,
    looked_ref,
    all_ref,
    ends_ref,
    got_ref,
    ring_send,
    ring_recv,
    side_send,
    side_recv,
    got_send,
    got_recv,
    ends_send,
    ends_recv,
    own_sem,
):
    me = lax.axis_index("ctx")
    chips = n // 2
    half = chips // 2
    core = me % 2
    chip = me // 2
    odd = chip % 2
    place = (1 - odd) * (chip // 2) + odd * (chips - 1 - chip // 2)
    sibling = me + 1 - 2 * core
    row_count = q_ref.shape[0]

    def device(at, on_core):
        at = (at + chips) % chips
        back = at // half
        return 2 * ((1 - back) * 2 * at + back * (2 * (chips - 1 - at) + 1)) + on_core

    streams = [(d, h) for h in range(2) for d in range(2)]

    def hops(d, h):
        return half if d == h else half - 1

    def ring(d, h, s):
        sign = 1 - 2 * d
        owner = device(place - sign * s, core)
        source = x_ref.at[h] if s == 0 else all_ref.at[owner, h]
        return push(
            source,
            all_ref.at[owner, h],
            ring_send.at[d, h, s],
            ring_recv.at[d, h, s],
            device(place + sign, core),
        )

    def arrival(d, h, s):
        owner = device(place - (1 - 2 * d) * (s + 1), core)
        landed = all_ref.at[owner, h]
        return push(landed, landed, ring_send.at[d, h, s], ring_recv.at[d, h, s], sibling)

    def side(d, h, s, on_core):
        owner = device(place - (1 - 2 * d) * s, on_core)
        source = all_ref.at[owner, h]
        if s == 0:
            source = x_ref.at[h]
        return push(
            source, all_ref.at[owner, h], side_send.at[d, h, s], side_recv.at[d, h, s], sibling
        )

    own = [pltpu.make_async_copy(x_ref.at[h], all_ref.at[me, h], own_sem.at[h]) for h in range(2)]
    own.append(pltpu.make_async_copy(looked_ref.at[me], got_ref.at[me], own_sem.at[2]))
    greet_all(me, n)
    for d, h in streams:
        ring(d, h, 0).start()

    def send_looked(peer):
        push(
            looked_ref.at[peer], got_ref.at[me], got_send.at[peer], got_recv.at[me], peer
        ).start()

    each_peer(me, n, send_looked)
    ends = [q_ref.at[pl.ds(0, BLOCK)], q_ref.at[pl.ds(row_count - BLOCK, BLOCK)]]
    holders = [0, n - 1]

    steps = [(place - at + chips) % chips for at in (0, half)]
    right, left = device(place + 1, core), device(place - 1, core)

    def send_end(e, k, source):
        peer = (right, left, sibling)[k]
        return push(source, ends_ref.at[e], ends_send.at[e, k], ends_recv.at[e], peer)

    def routes(e):
        away = steps[e]
        return [
            (0, away < half),
            (1, jnp.logical_or(away == 0, away > chips - half + 1)),
            (2, me == holders[e]),
        ]

    def start_routes(e, source):
        for k, goes in routes(e)[:2]:

            @pl.when(goes)
            def _():
                send_end(e, k, source).start()

    def pass_end(e):
        send_end(e, 0, ends_ref.at[e]).wait_recv()
        start_routes(e, ends_ref.at[e])

    for e in range(2):

        @pl.when(me == holders[e])
        def _():
            send_end(e, 2, ends[e]).start()
            start_routes(e, ends[e])
            copy = pltpu.make_async_copy(ends[e], ends_ref.at[e], own_sem.at[3])
            copy.start()
            copy.wait()

        @pl.when(jnp.logical_and(steps[e] == 0, me != holders[e]))
        def _():
            pass_end(e)

    for copy in own:
        copy.start()
    for h in range(2):
        side(0, h, 0, core).start()
    for s in range(half):
        for d, h in streams:
            if s < hops(d, h):
                arrival(d, h, s).wait_recv()
                if s + 1 < hops(d, h):
                    ring(d, h, s + 1).start()
                side(d, h, s + 1, core).start()
        for e in range(2):
            near = steps[e] == s + 1
            if s + 1 < half:
                near = jnp.logical_or(near, steps[e] == chips - s - 1)

            @pl.when(near)
            def _():
                pass_end(e)

    for h in range(2):
        side(0, h, 0, core).wait_send()
        side(0, h, 0, 1 - core).wait_recv()
    for s in range(half):
        for d, h in streams:
            if s < hops(d, h):
                ring(d, h, s).wait_send()
                side(d, h, s + 1, core).wait_send()
                side(d, h, s + 1, 1 - core).wait_recv()

    def end_looked(peer):
        copy = push(
            looked_ref.at[peer], got_ref.at[peer], got_send.at[peer], got_recv.at[peer], peer
        )
        copy.wait_recv()
        copy.wait_send()

    each_peer(me, n, end_looked)
    for e in range(2):
        for k, goes in routes(e):

            @pl.when(goes)
            def _():
                send_end(e, k, ends[e]).wait_send()

    for copy in own:
        copy.wait()


def gather_inputs(x, q, looked):
    n = lax.axis_size("ctx")
    rows, features = x.shape
    half = n // 4
    dma = pltpu.SemaphoreType.DMA
    gathered, ends, got = pl.pallas_call(
        functools.partial(gather_kernel, n),
        out_shape=[
            jax.ShapeDtypeStruct((n, 2, rows // 2, features), x.dtype),
            jax.ShapeDtypeStruct((2, BLOCK, features), q.dtype),
            jax.ShapeDtypeStruct(looked.shape, looked.dtype),
        ],
        in_specs=[ANY] * 3,
        out_specs=[ANY] * 3,
        scratch_shapes=[
            dma((2, 2, half)),
            dma((2, 2, half)),
            dma((2, 2, half + 1)),
            dma((2, 2, half + 1)),
            dma((n,)),
            dma((n,)),
            dma((2, 3)),
            dma((2,)),
            dma((4,)),
        ],
        compiler_params=pltpu.CompilerParams(collective_id=1, has_side_effects=True),
        name="gather_inputs",
    )(x.reshape(2, rows // 2, features), q, looked)
    return gathered.reshape(n * rows // BLOCK, BLOCK, features), ends, got


def ends_kernel(
    n,
    mine_ref,
    out_ref,
    log_ref,
    rows_ref,
    outs_ref,
    logs_ref,
    rows_send,
    rows_recv,
    ends_send,
    ends_recv,
    own_sem,
):
    me = lax.axis_index("ctx")
    holders = [0, n - 1]
    pairs = [(out_ref, outs_ref), (log_ref, logs_ref)]

    def end(e, i, slot):
        source, target = pairs[i]
        return push(
            source.at[e], target.at[slot], ends_send.at[e, i], ends_recv.at[i, slot], holders[e]
        )

    own = pltpu.make_async_copy(mine_ref, rows_ref.at[me], own_sem.at[2])
    own.start()
    greet_all(me, n)
    for e in range(2):

        @pl.when(me != holders[e])
        def _():
            for i in range(2):
                end(e, i, me).start()

        @pl.when(me == holders[e])
        def _():
            for i in range(2):
                source, target = pairs[i]
                copy = pltpu.make_async_copy(source.at[e], target.at[me], own_sem.at[i])
                copy.start()
                copy.wait()

    def send_rows(peer):
        push(mine_ref, rows_ref.at[me], rows_send.at[peer], rows_recv.at[me], peer).start()

    each_peer(me, n, send_rows)

    def end_rows(peer):
        copy = push(mine_ref, rows_ref.at[peer], rows_send.at[peer], rows_recv.at[peer], peer)
        copy.wait_recv()
        copy.wait_send()

    each_peer(me, n, end_rows)
    for e in range(2):

        @pl.when(me != holders[e])
        def _():
            for i in range(2):
                end(e, i, me).wait_send()

        @pl.when(me == holders[e])
        def _():
            def arrived(peer):
                for i in range(2):
                    source, target = pairs[i]
                    push(
                        source.at[e],
                        target.at[peer],
                        ends_send.at[e, i],
                        ends_recv.at[i, peer],
                        peer,
                    ).wait_recv()

            each_peer(me, n, arrived)

    own.wait()


def send_ends(mine, out, log):
    n = lax.axis_size("ctx")
    dma = pltpu.SemaphoreType.DMA
    out = out.reshape(2, BLOCK, out.shape[1])
    log = log.reshape(2, BLOCK, LANES)
    return pl.pallas_call(
        functools.partial(ends_kernel, n),
        out_shape=[
            jax.ShapeDtypeStruct((n,) + mine.shape, mine.dtype),
            jax.ShapeDtypeStruct((n,) + out.shape[1:], out.dtype),
            jax.ShapeDtypeStruct((n,) + log.shape[1:], log.dtype),
        ],
        in_specs=[ANY] * 3,
        out_specs=[ANY] * 3,
        scratch_shapes=[dma((n,)), dma((n,)), dma((2, 2)), dma((2, n)), dma((3,))],
        compiler_params=pltpu.CompilerParams(collective_id=2, has_side_effects=True),
        name="send_ends",
    )(mine, out, log)


def combine(outs_ref, logs_ref, total_ref):
    n, rows, features = outs_ref.shape
    peak = lax.fori_loop(
        1, n, lambda i, peak: jnp.maximum(peak, logs_ref[i]), logs_ref[0]
    )
    left = lax.broadcasted_iota(jnp.int32, (rows, LANES), 1) < HEAD
    total_ref[...] = jnp.zeros_like(total_ref)

    def spread(x, p):
        return jnp.where(left, x[:, 2 * p : 2 * p + 1], x[:, 2 * p + 1 : 2 * p + 2])

    def add(i, total):
        weights = jnp.exp(logs_ref[i] - peak)
        for p in range(PAIRS):
            lanes = slice(p * LANES, (p + 1) * LANES)
            total_ref[:, lanes] += outs_ref[i, :, lanes].astype(jnp.float32) * spread(weights, p)
        return total + weights

    scale = 1.0 / lax.fori_loop(0, n, add, jnp.zeros((rows, LANES), jnp.float32))
    for p in range(PAIRS):
        lanes = slice(p * LANES, (p + 1) * LANES)
        total_ref[:, lanes] = total_ref[:, lanes] * spread(scale, p)


def summary_kernel(
    n,
    part_ref,
    log_ref,
    out_ref,
    outs_ref,
    logs_ref,
    total_ref,
    send_sem,
    recv_sem,
    own_sem,
):
    me = lax.axis_index("ctx")
    pairs = [(part_ref, outs_ref), (log_ref, logs_ref)]
    own = [
        pltpu.make_async_copy(source.at[me], target.at[me], own_sem.at[i])
        for i, (source, target) in enumerate(pairs)
    ]
    for copy in own:
        copy.start()
    greet_all(me, n)

    def copies(peer, slot):
        return [
            push(
                source.at[peer], target.at[slot], send_sem.at[i, peer], recv_sem.at[i, slot], peer
            )
            for i, (source, target) in enumerate(pairs)
        ]

    def send(peer):
        for copy in copies(peer, me):
            copy.start()

    each_peer(me, n, send)

    def finish(peer):
        for copy in copies(peer, peer):
            copy.wait_recv()
            copy.wait_send()

    each_peer(me, n, finish)
    for copy in own:
        copy.wait()
    combine(outs_ref, logs_ref, total_ref)
    out_ref[...] = total_ref[...].astype(out_ref.dtype)


def combined_summary(part, logs):
    n, share, features = part.shape
    dma = pltpu.SemaphoreType.DMA
    return pl.pallas_call(
        functools.partial(summary_kernel, n),
        out_shape=jax.ShapeDtypeStruct((share, features), jnp.bfloat16),
        in_specs=[ANY] * 2,
        out_specs=VMEM,
        scratch_shapes=[
            pltpu.VMEM(part.shape, part.dtype),
            pltpu.VMEM(logs.shape, logs.dtype),
            pltpu.VMEM((share, features), jnp.float32),
            dma((2, n)),
            dma((2, n)),
            dma((2,)),
        ],
        compiler_params=pltpu.CompilerParams(collective_id=3, has_side_effects=True),
        name="combined_summary",
    )(part, logs)


def dot_t(a, b):
    return lax.dot_general(a, b, (((1,), (1,)), ((), ())), preferred_element_type=jnp.float32)


def stacked_pair(q):
    q = q * jnp.asarray(HEAD**-0.5, q.dtype)
    left = lax.broadcasted_iota(jnp.int32, q.shape, 1) < HEAD
    zero = jnp.zeros_like(q)
    return jnp.concatenate([jnp.where(left, q, zero), jnp.where(left, zero, q)], axis=0)


def unstacked_pair(o):
    rows = o.shape[0] // 2
    left = lax.broadcasted_iota(jnp.int32, (rows, LANES), 1) < HEAD
    return jnp.where(left, o[:rows], o[rows:])


def project(x_ref, w_ref, out_ref, tile):
    rows, cols = out_ref.shape
    width = 512

    def step(t, carry):
        at = pl.ds(pl.multiple_of(t * tile, tile), tile)
        x = x_ref[at, :]
        for c in range(cols // width):
            y = jnp.dot(
                x, w_ref[:, c * width : (c + 1) * width], preferred_element_type=jnp.float32
            )
            out_ref[at, c * width : (c + 1) * width] = y.astype(out_ref.dtype)
        return carry

    lax.fori_loop(0, rows // tile, step, 0)


def partial_attention(q_ref, kv_ref, out_ref, log_ref):
    rows, features = q_ref.shape
    place = lax.broadcasted_iota(jnp.int32, (rows, LANES), 1)
    logs = jnp.zeros((rows, LANES), jnp.float32)
    for p in range(PAIRS):
        lanes = slice(p * LANES, (p + 1) * LANES)
        values = slice(features + p * LANES, features + (p + 1) * LANES)
        scores = dot_t(stacked_pair(q_ref[:, lanes]), kv_ref[:, lanes])
        peak = jnp.max(scores, axis=1, keepdims=True)
        weights = jnp.exp(scores - peak)
        totals = jnp.sum(weights, axis=1, keepdims=True)
        sums = jnp.dot(
            weights.astype(jnp.bfloat16), kv_ref[:, values], preferred_element_type=jnp.float32
        )
        out_ref[:, lanes] = unstacked_pair(sums / totals).astype(out_ref.dtype)
        log = peak + jnp.log(totals)
        logs = jnp.where(place == 2 * p, log[:rows], logs)
        logs = jnp.where(place == 2 * p + 1, log[rows:], logs)
    log_ref[...] = logs


def global_kernel(q_ref, x_ref, w_ref, out_ref, log_ref, kv_ref):
    project(x_ref, w_ref, kv_ref, 128)
    partial_attention(q_ref, kv_ref, out_ref, log_ref)


def global_partial(q, x, w):
    return pl.pallas_call(
        global_kernel,
        out_shape=[
            jax.ShapeDtypeStruct(q.shape, jnp.bfloat16),
            jax.ShapeDtypeStruct((q.shape[0], LANES), jnp.float32),
        ],
        in_specs=[VMEM] * 3,
        out_specs=[VMEM] * 2,
        scratch_shapes=[pltpu.VMEM((x.shape[0], w.shape[1]), jnp.bfloat16)],
        compiler_params=pltpu.CompilerParams(vmem_limit_bytes=VMEM_LIMIT),
        cost_estimate=pl.CostEstimate(
            flops=2 * x.size * w.shape[1], bytes_accessed=6 << 20, transcendentals=1 << 20
        ),
        name="global_partial",
    )(q, x, w)


def block_kernel(
    pick_count,
    ids_ref,
    edge_ref,
    all_ref,
    q_ref,
    x_ref,
    w_kv_ref,
    w_cross_ref,
    outs_ref,
    logs_ref,
    sq_ref,
    attended_ref,
    out_ref,
    log_ref,
    rows_ref,
    kv_ref,
    total_ref,
    sem,
):
    row_count, features = x_ref.shape
    block_count = row_count // BLOCK
    slots = rows_ref.shape[0] // BLOCK
    far_start = (block_count + 4) * BLOCK
    span = (5 + pick_count) * BLOCK

    def fetch(i):
        return pltpu.make_async_copy(
            all_ref.at[ids_ref[i]],
            rows_ref.at[pl.ds(pl.multiple_of(i * BLOCK, BLOCK), BLOCK)],
            sem.at[i],
        )

    for i in range(slots):
        fetch(i).start()
    for i in range(slots):
        fetch(i).wait()
    project(rows_ref, w_kv_ref, kv_ref, 2 * BLOCK)

    column = lax.broadcasted_iota(jnp.int32, (2 * BLOCK, span), 1)

    def one_block(b, carry):
        first = edge_ref[0] + b
        hidden = jnp.logical_or(
            jnp.logical_and(column < BLOCK, first < 2),
            jnp.logical_and(
                jnp.logical_and(column >= 2 * BLOCK, column < 3 * BLOCK), first > edge_ref[1] - 3
            ),
        )
        near = pl.ds(pl.multiple_of(b * BLOCK, BLOCK), 3 * BLOCK)
        ends = pl.ds((block_count + 2) * BLOCK, 2 * BLOCK)
        far = pl.ds(
            pl.multiple_of(far_start + b * pick_count * BLOCK, BLOCK), pick_count * BLOCK
        )
        here = pl.ds(pl.multiple_of(b * BLOCK, BLOCK), BLOCK)
        for p in range(PAIRS):
            lanes = slice(p * LANES, (p + 1) * LANES)
            values = slice(features + p * LANES, features + (p + 1) * LANES)
            k = jnp.concatenate(
                [kv_ref[near, lanes], kv_ref[ends, lanes], kv_ref[far, lanes]], axis=0
            )
            v = jnp.concatenate(
                [kv_ref[near, values], kv_ref[ends, values], kv_ref[far, values]], axis=0
            )
            scores = dot_t(stacked_pair(q_ref[here, lanes]), k)
            scores = jnp.where(hidden, MASKED_SCORE, scores)
            weights = jnp.exp(scores - jnp.max(scores, axis=1, keepdims=True))
            totals = jnp.sum(weights, axis=1, keepdims=True)
            probs = (weights * (1.0 / totals)).astype(jnp.bfloat16)
            o = jnp.dot(probs, v, preferred_element_type=jnp.float32)
            attended_ref[here, lanes] = unstacked_pair(o).astype(jnp.bfloat16)
        return carry

    lax.fori_loop(0, block_count, one_block, 0)

    def place(rows):
        combine(outs_ref, logs_ref, total_ref)
        attended_ref[rows] = total_ref[...].astype(jnp.bfloat16)

    @pl.when(edge_ref[0] == 0)
    def _():
        place(slice(0, BLOCK))

    @pl.when(edge_ref[0] + block_count == edge_ref[1])
    def _():
        place(slice(row_count - BLOCK, row_count))

    encoded = x_ref[...].astype(jnp.float32) + attended_ref[...].astype(jnp.float32)
    rows_ref[:row_count] = encoded.astype(jnp.bfloat16)
    project(rows_ref.at[:row_count], w_cross_ref, kv_ref.at[:row_count], 2 * BLOCK)
    partial_attention(sq_ref, kv_ref.at[:row_count], out_ref, log_ref)


def block_attention(ids, edge, everything, q, x, w_kv, w_cross, outs, end_logs, sq, pick_count):
    slots = ids.shape[0]
    features = x.shape[1]
    return pl.pallas_call(
        functools.partial(block_kernel, pick_count),
        out_shape=[
            jax.ShapeDtypeStruct(q.shape, jnp.bfloat16),
            jax.ShapeDtypeStruct(sq.shape, jnp.bfloat16),
            jax.ShapeDtypeStruct((sq.shape[0], LANES), jnp.float32),
        ],
        in_specs=[SMEM, SMEM, ANY] + [VMEM] * 7,
        out_specs=[VMEM] * 3,
        scratch_shapes=[
            pltpu.VMEM((slots * BLOCK, features), jnp.bfloat16),
            pltpu.VMEM((slots * BLOCK, 2 * features), jnp.bfloat16),
            pltpu.VMEM((BLOCK, features), jnp.float32),
            pltpu.SemaphoreType.DMA((slots,)),
        ],
        compiler_params=pltpu.CompilerParams(vmem_limit_bytes=VMEM_LIMIT),
        cost_estimate=pl.CostEstimate(
            flops=20 << 30, bytes_accessed=16 << 20, transcendentals=5 << 20
        ),
        name="block_attention",
    )(ids, edge, everything, q, x, w_kv, w_cross, outs, end_logs, sq)


def staged(queries, inputs, w_kv, rand_blocks, w_cross, vocab_table, summary_ids):
    n = lax.axis_size("ctx")
    position = lax.axis_index("ctx")
    row_count, features = inputs.shape
    block_count = row_count // BLOCK
    pick_count = rand_blocks.shape[1]
    total_blocks = block_count * n
    shard_rows = vocab_table.shape[0]
    summary_count = summary_ids.shape[0]
    share = summary_count // n
    offsets = summary_ids - position * shard_rows
    inside = jnp.logical_and(offsets >= 0, offsets < shard_rows)
    looked = vocab_table[jnp.clip(offsets, 0, shard_rows - 1)]
    looked = jnp.where(inside[:, None], looked, jnp.zeros((), looked.dtype))
    everything, end_queries, got = gather_inputs(
        inputs, queries, looked.reshape(n, share, features)
    )
    mine = jnp.sum(got.astype(jnp.float32), axis=0).astype(jnp.bfloat16)
    end_out, end_log = global_partial(end_queries.reshape(2 * BLOCK, features), inputs, w_kv)
    rows, outs, end_logs = send_ends(mine, end_out, end_log)
    summary_queries = rows.reshape(summary_count, features)

    start = position * block_count
    near = jnp.clip(start - 1 + jnp.arange(block_count + 2, dtype=jnp.int32), 0, total_blocks - 1)
    fixed = jnp.array([0, total_blocks - 1], jnp.int32)
    picks = lax.dynamic_slice_in_dim(rand_blocks, start, block_count, 0).reshape(-1)
    ids = jnp.concatenate([near, fixed, picks.astype(jnp.int32)])
    edge = jnp.stack([start, jnp.full_like(start, total_blocks)]).astype(jnp.int32)
    attended, part, logs = block_attention(
        ids,
        edge,
        everything,
        queries,
        inputs,
        w_kv,
        w_cross,
        outs,
        end_logs,
        summary_queries,
        pick_count,
    )
    summary = combined_summary(
        part.reshape(n, share, features), logs.reshape(n, share, LANES)
    )
    return attended, summary


def ring_order(half, blocks, d):
    ends_first = [j // 2 if j % 2 == 0 else blocks - 1 - j // 2 for j in range(blocks)]
    group = blocks // 2
    order = []
    for g in range(2):
        members = range(g * group, (g + 1) * group)
        last = [i for i in members if i % 2 == d]
        rest = [i for i in members if i % 2 != d]
        for hop in range(half):
            order += [(hop, ends_first[i]) for i in (last if hop == half - 1 else last + rest)]
    return order


def look_up(values, t):
    found = values[0]
    for j in range(1, len(values)):
        if values[j] != values[j - 1]:
            found = jnp.where(t >= j, values[j], found)
    return found


def dots(x, w_ref, store):
    width = 512
    for c in range(w_ref.shape[1] // width):
        cols = slice(c * width, (c + 1) * width)
        y = jnp.dot(x, w_ref[:, cols], preferred_element_type=jnp.float32)
        store(cols, y.astype(jnp.bfloat16))


def lanes_of(p):
    return slice(p * LANES, (p + 1) * LANES)


def row_max(x):
    return jnp.max(x, axis=1, keepdims=True)


def row_sum(x):
    return jnp.sum(x, axis=1, keepdims=True)


def weighted(weights, v):
    return jnp.dot(weights.astype(jnp.bfloat16), v, preferred_element_type=jnp.float32)


def with_log(log, rows):
    place = lax.broadcasted_iota(jnp.int32, (rows, LANES), 1)
    high = log.astype(jnp.bfloat16)
    rest = log - high.astype(jnp.float32)
    middle = rest.astype(jnp.bfloat16)
    low = (rest - middle.astype(jnp.float32)).astype(jnp.bfloat16)
    low, middle = low.astype(jnp.float32), middle.astype(jnp.float32)
    packed = jnp.where(place < HEADS, high.astype(jnp.float32), 0.0)
    packed = jnp.where(place // HEADS == 1, pltpu.roll(middle, HEADS, 1), packed)
    packed = jnp.where(place // HEADS == 2, pltpu.roll(low, 2 * HEADS, 1), packed)
    return packed.astype(jnp.bfloat16)


def without_log(packed):
    packed = packed.astype(jnp.float32)
    middle = pltpu.roll(packed, LANES - HEADS, 1)
    low = pltpu.roll(packed, LANES - 2 * HEADS, 1)
    return packed + (middle + low)


def fused_kernel(
    n,
    picks_ref,
    sids_ref,
    x_ref,
    q_hbm,
    w_kv_hbm,
    w_cross_hbm,
    vocab_hbm,
    attended_ref,
    summary_ref,
    x_all,
    kv_all,
    w_kv_ref,
    q_ref,
    shared_ref,
    looked_ref,
    sibq_ref,
    chipq_ref,
    partq_ref,
    mine_ref,
    sumq_ref,
    acc_ref,
    peak_ref,
    sum_ref,
    end_q_ref,
    end_out_ref,
    end_half_ref,
    near_ref,
    near_log_ref,
    part_ref,
    sibp_ref,
    chipp_ref,
    got_ref,
    ring_send,
    ring_recv,
    side_send,
    side_recv,
    own_send,
    own_recv,
    pair_send,
    pair_recv,
    across_send,
    across_recv,
    local_sem,
):
    me = lax.axis_index("ctx")
    chips = n // 2
    half = chips // 2
    core = me % 2
    chip = me // 2
    odd = chip % 2
    place = (1 - odd) * (chip // 2) + odd * (chips - 1 - chip // 2)
    sibling = me + 1 - 2 * core
    blocks = x_ref.shape[0]
    features = x_ref.shape[2]
    rows = blocks * BLOCK
    share = summary_ref.shape[0]
    steps = (half - 1) * blocks + blocks // 2
    total_blocks = n * blocks
    holder = jnp.logical_or(me == 0, me == n - 1)
    at_end = jnp.logical_or(chip == 0, chip == chips - 1)
    orders = [ring_order(half, blocks, d) for d in range(2)]
    ahead = blocks // 2

    def device(at, on_core):
        at = (at + chips) % chips
        back = at // half
        return 2 * ((1 - back) * 2 * at + back * (2 * (chips - 1 - at) + 1)) + on_core

    def block_of(d, t):
        if isinstance(t, int):
            return orders[d][t][1]
        return look_up([block for _, block in orders[d]], t)

    def hop_of(d, t):
        if isinstance(t, int):
            return orders[d][t][0]
        return look_up([hop for hop, _ in orders[d]], t)

    def ring(d, t):
        held = x_all.at[device(place - (1 - 2 * d) * hop_of(d, t), core), block_of(d, t)]
        return push(
            held, held, ring_send.at[d, t], ring_recv.at[d, t], device(place + 1 - 2 * d, core)
        )

    def ring_own(d, t):
        return push(
            x_ref.at[block_of(d, t)],
            x_all.at[me, block_of(d, t)],
            ring_send.at[d, t],
            ring_recv.at[d, t],
            device(place + 1 - 2 * d, core),
        )

    def owner_of(d, t, on_core):
        return device(place - (1 - 2 * d) * (hop_of(d, t) + 1), on_core)

    def arrival(d, t):
        landed = x_all.at[owner_of(d, t, core), block_of(d, t)]
        return push(landed, landed, ring_send.at[d, t], ring_recv.at[d, t], sibling)

    def side(d, t, on_core):
        landed = x_all.at[owner_of(d, t, on_core), block_of(d, t)]
        return push(landed, landed, side_send.at[d, t], side_recv.at[d, t], sibling)

    def side_own(on):
        return push(x_ref, x_all.at[on], own_send, own_recv, sibling)

    def peer_of(k):
        other = lax.rem(chip + k, chips)
        return other, 2 * other + core

    shard_rows = vocab_hbm.shape[0]
    vocab_ref = shared_ref.at[:shard_rows]
    encoded_ref = shared_ref.at[:rows]
    cross_ref = kv_all.at[:blocks]
    loads = [
        pltpu.make_async_copy(source, target, local_sem.at[i])
        for i, (source, target) in enumerate(
            [
                (vocab_hbm, vocab_ref),
                (w_kv_hbm, w_kv_ref),
                (x_ref, x_all.at[me]),
                (q_hbm, q_ref),
            ]
        )
    ]
    for load in loads:
        load.start()

    barrier = pltpu.get_barrier_semaphore()
    pl.semaphore_signal(barrier, inc=1, device_id={"ctx": sibling}, device_id_type=MESH)
    for k in range(1, chips):
        pl.semaphore_signal(
            barrier, inc=1, device_id={"ctx": peer_of(k)[1]}, device_id_type=MESH
        )
    pl.semaphore_wait(barrier, chips)

    for t in range(ahead):
        for d in range(2):
            ring_own(d, t).start()
    end_row = pl.multiple_of(jnp.where(chip == 0, 0, rows - BLOCK), BLOCK)

    def end_q():
        return push(
            q_hbm.at[pl.ds(end_row, BLOCK)], end_q_ref, pair_send.at[3], pair_recv.at[3], sibling
        )

    def end_out():
        return push(end_out_ref, end_half_ref, pair_send.at[4], pair_recv.at[4], sibling)

    @pl.when(holder)
    def _():
        end_q().start()
        copy = pltpu.make_async_copy(
            q_hbm.at[pl.ds(end_row, BLOCK)], end_q_ref, local_sem.at[5]
        )
        copy.start()
        copy.wait()

    side_own(me).start()

    loads[0].wait()
    summary_count = sids_ref.shape[1]
    offsets = sids_ref[...] - me * shard_rows
    hot = lax.broadcasted_iota(jnp.int32, (shard_rows, summary_count), 0) == offsets
    hot = jnp.where(hot, 1.0, 0.0).astype(jnp.bfloat16)
    looked = lax.dot_general(
        hot, vocab_ref[...], (((0,), (0,)), ((), ())), preferred_element_type=jnp.float32
    ).astype(jnp.bfloat16)
    for k in range(chips):
        for c in range(2):
            at = (2 * k + c) * share
            looked_ref[c, k] = looked[at : at + share]

    def pair_q():
        return push(
            looked_ref.at[1 - core], sibq_ref, pair_send.at[0], pair_recv.at[0], sibling
        )

    pair_q().start()
    loads[1].wait()
    loads[2].wait()

    def project_owner(owner):
        def step(t, carry):
            x = x_all[owner, pl.ds(2 * t, 2)].reshape(2 * BLOCK, features)

            def store(cols, y):
                kv_all[pl.ds(owner * blocks + 2 * t, 2), :, cols] = y.reshape(2, BLOCK, -1)

            dots(x, w_kv_ref, store)
            return carry

        lax.fori_loop(0, blocks // 2, step, 0)

    project_owner(me)
    pair_q().wait_recv()
    chipq_ref[...] = looked_ref[core] + sibq_ref[...]

    def across_q(k, slot):
        other, peer = peer_of(k)
        return push(
            chipq_ref.at[other],
            partq_ref.at[slot],
            across_send.at[0, k],
            across_recv.at[0, slot],
            peer,
        )

    for k in range(1, chips):
        across_q(k, chip).start()
    partq_ref[chip] = chipq_ref[chip]
    side_own(sibling).wait_recv()
    project_owner(sibling)

    loads[3].wait()
    half_pairs = PAIRS // 2

    def half_lanes(p):
        return pl.multiple_of((core * half_pairs + p) * LANES, LANES)

    def take_keys(parts):
        every = range(half_pairs)
        scores = []
        for p in every:
            lanes = pl.ds(half_lanes(p), LANES)
            k = jnp.concatenate([kv_all[at, :, lanes] for at in parts], axis=0)
            scores.append(dot_t(stacked_pair(end_q_ref[:, lanes]), k.reshape(-1, LANES)))
        before = [peak_ref[p] for p in every]
        peaks = [jnp.maximum(before[p], row_max(scores[p])) for p in every]
        weights = [jnp.exp(scores[p] - peaks[p][:, :1]) for p in every]
        fades = [jnp.exp(before[p] - peaks[p]) for p in every]
        totals = [row_sum(weights[p]) for p in every]
        sums = []
        for p in every:
            values = pl.ds(features + half_lanes(p), LANES)
            v = jnp.concatenate([kv_all[at, :, values] for at in parts], axis=0)
            sums.append(weighted(weights[p], v.reshape(-1, LANES)))
        for p in every:
            peak_ref[p] = peaks[p]
            sum_ref[p] = sum_ref[p] * fades[p] + totals[p]
            acc_ref[p] = acc_ref[p] * fades[p] + sums[p]

    @pl.when(jnp.logical_and(at_end, jnp.logical_not(holder)))
    def _():
        end_q().wait_recv()

    @pl.when(at_end)
    def _():
        peak_ref[...] = jnp.full_like(peak_ref, MASKED_SCORE)
        sum_ref[...] = jnp.zeros_like(sum_ref)
        acc_ref[...] = jnp.zeros_like(acc_ref)
        for i in range(2):
            take_keys([pl.ds((2 * chip + i) * blocks, blocks)])

    def process(found):
        x = jnp.concatenate([x_all[owner, block] for owner, block in found], axis=0)
        parts = [owner * blocks + block for owner, block in found]

        def store(cols, y):
            for i, at in enumerate(parts):
                kv_all[at, :, cols] = y[i * BLOCK : (i + 1) * BLOCK]

        dots(x, w_kv_ref, store)

        @pl.when(at_end)
        def _():
            take_keys(parts)

    def own_blocks(t):
        return [(owner_of(d, t, core), block_of(d, t)) for d in range(2)]

    def side_blocks(t):
        return [(owner_of(d, t, 1 - core), block_of(d, t)) for d in range(2)]

    def pass_on(t):
        for d in range(2):
            arrival(d, t).wait_recv()

            @pl.when(t + ahead < steps)
            def _():
                ring(d, t + ahead).start()

            side(d, t, core).start()

    def first(t):
        pass_on(t)
        process(own_blocks(t))

    def one_step(t, carry):
        pass_on(t)
        for d in range(2):
            side(d, t - 1, 1 - core).wait_recv()
        process(own_blocks(t) + side_blocks(t - 1))

        @pl.when(jnp.logical_and(t >= near_from, t < near_from + blocks))
        def _():
            near_keys(t - near_from)

        return carry

    start = me * blocks
    near_from = 2 + max(
        t for d in range(2) for t, (_, b) in enumerate(orders[d]) if b in (0, blocks - 1)
    )
    column = lax.broadcasted_iota(jnp.int32, (2 * BLOCK, 5 * BLOCK), 1)

    def near_keys(b):
        here = start + b
        hidden = jnp.logical_or(
            jnp.logical_and(column < BLOCK, here < 2),
            jnp.logical_and(column // BLOCK == 2, here > total_blocks - 3),
        )
        chosen = [
            jnp.maximum(here - 1, 0),
            here,
            jnp.minimum(here + 1, total_blocks - 1),
            0,
            total_blocks - 1,
        ]
        out = pl.ds(pl.multiple_of(b * BLOCK, BLOCK), BLOCK)
        scores = []
        for p in range(PAIRS):
            k = jnp.concatenate([kv_all[at, :, lanes_of(p)] for at in chosen], axis=0)
            scores.append(dot_t(stacked_pair(q_ref[out, lanes_of(p)]), k))
        scores = [jnp.where(hidden, MASKED_SCORE, x) for x in scores]
        peaks = [row_max(x) for x in scores]
        weights = [jnp.exp(x - peak) for x, peak in zip(scores, peaks)]
        totals = [row_sum(x) for x in weights]
        sums = []
        for p in range(PAIRS):
            v = jnp.concatenate([kv_all[at, :, lanes_of(PAIRS + p)] for at in chosen], axis=0)
            sums.append(weighted(weights[p], v))
        for p in range(PAIRS):
            near_ref[out, lanes_of(p)] = unstacked_pair(sums[p] * (1.0 / totals[p]))
            near_log_ref[b, p] = jnp.broadcast_to(
                peaks[p] + jnp.log(totals[p]), (2 * BLOCK, LANES)
            )

    first(0)
    lax.fori_loop(1, steps, one_step, 0)

    for k in range(1, chips):
        other, _ = peer_of(k)
        across_q(k, other).wait_recv()
    mine = partq_ref[0].astype(jnp.float32)
    for k in range(1, chips):
        mine = mine + partq_ref[k].astype(jnp.float32)
    mine_ref[...] = mine.astype(jnp.bfloat16)

    def spread_q(k, slot):
        _, peer = peer_of(k)
        return push(
            mine_ref, sumq_ref.at[core, slot], across_send.at[1, k], across_recv.at[1, slot], peer
        )

    for k in range(1, chips):
        spread_q(k, chip).start()
    sumq_ref[core, chip] = mine_ref[...]

    for d in range(2):
        side(d, steps - 1, 1 - core).wait_recv()
    process(side_blocks(steps - 1))
    load_cross = pltpu.make_async_copy(w_cross_hbm, w_kv_ref, local_sem.at[4])
    load_cross.start()

    @pl.when(jnp.logical_and(at_end, jnp.logical_not(holder)))
    def _():
        for p in range(half_pairs):
            lanes = slice(p * LANES, (p + 1) * LANES)
            end_out_ref[:, lanes] = unstacked_pair(acc_ref[p] * (1.0 / sum_ref[p])).astype(
                jnp.bfloat16
            )
        end_out().start()

    together = 2

    def random_keys(t, carry):
        work = [(together * t + i, p) for i in range(together) for p in range(PAIRS)]
        chosen = [[picks_ref[i, start + b] for i in range(picks_ref.shape[0])] for b, _ in work]
        outs = [pl.ds(pl.multiple_of(b * BLOCK, BLOCK), BLOCK) for b, _ in work]
        scores = []
        for (_, p), out, found in zip(work, outs, chosen):
            k = jnp.concatenate([kv_all[at, :, lanes_of(p)] for at in found], axis=0)
            scores.append(dot_t(stacked_pair(q_ref[out, lanes_of(p)]), k))
        logs = [near_log_ref[b, p] for b, p in work]
        peaks = [jnp.maximum(log, row_max(x)) for log, x in zip(logs, scores)]
        weights = [jnp.exp(x - peak[:, :1]) for x, peak in zip(scores, peaks)]
        fades = [jnp.exp(log - peak) for log, peak in zip(logs, peaks)]
        scales = [1.0 / (fade + row_sum(x)) for fade, x in zip(fades, weights)]
        sums = []
        for (_, p), x, found in zip(work, weights, chosen):
            v = jnp.concatenate([kv_all[at, :, lanes_of(PAIRS + p)] for at in found], axis=0)
            sums.append(weighted(x, v))
        for i, (b, p) in enumerate(work):
            o = unstacked_pair(sums[i] * scales[i])
            o = o + near_ref[outs[i], lanes_of(p)] * unstacked_pair(fades[i] * scales[i])
            attended_ref[outs[i], lanes_of(p)] = o.astype(jnp.bfloat16)
        return carry

    lax.fori_loop(0, blocks // together, random_keys, 0)

    @pl.when(holder)
    def _():
        for p in range(half_pairs):
            attended_ref[pl.ds(end_row, BLOCK), pl.ds(half_lanes(p), LANES)] = unstacked_pair(
                acc_ref[p] * (1.0 / sum_ref[p])
            ).astype(jnp.bfloat16)
        end_out().wait_recv()
        there = pl.multiple_of((1 - core) * half_pairs * LANES, LANES)
        attended_ref[pl.ds(end_row, BLOCK), pl.ds(there, half_pairs * LANES)] = end_half_ref[...]

    for k in range(1, chips):
        other, _ = peer_of(k)
        spread_q(k, other).wait_recv()

    def pair_all(c):
        return push(sumq_ref.at[c], sumq_ref.at[c], pair_send.at[1], pair_recv.at[1], sibling)

    pair_all(core).start()
    encoded = x_all[me].reshape(rows, features).astype(jnp.float32)
    encoded = encoded + attended_ref[...].astype(jnp.float32)
    encoded_ref[...] = encoded.astype(jnp.bfloat16)
    load_cross.wait()

    def project_cross(t, carry):
        x = encoded_ref[pl.ds(pl.multiple_of(t * 2 * BLOCK, 2 * BLOCK), 2 * BLOCK)]

        def store(cols, y):
            cross_ref[pl.ds(2 * t, 2), :, cols] = y.reshape(2, BLOCK, -1)

        dots(x, w_kv_ref, store)
        return carry

    lax.fori_loop(0, blocks // 2, project_cross, 0)

    def cross_of(p):
        return cross_ref[:, :, lanes_of(p)].reshape(rows, LANES)

    group = chips * share
    width = features + LANES

    def summary_half(c):
        place_ = lax.broadcasted_iota(jnp.int32, (group, LANES), 1)
        logs = jnp.zeros((group, LANES), jnp.float32)
        scores = []
        for p in range(PAIRS):
            q = sumq_ref[c, :, :, lanes_of(p)].reshape(group, LANES)
            scores.append(dot_t(stacked_pair(q), cross_of(p)))
        peaks = [row_max(x) for x in scores]
        weights = [jnp.exp(x - peak) for x, peak in zip(scores, peaks)]
        totals = [row_sum(x) for x in weights]
        sums = [weighted(weights[p], cross_of(PAIRS + p)) for p in range(PAIRS)]
        for p in range(PAIRS):
            part = unstacked_pair(sums[p] * (1.0 / totals[p])).astype(jnp.bfloat16)
            part_ref[c, :, :, lanes_of(p)] = part.reshape(chips, share, LANES)
            log = peaks[p] + jnp.log(totals[p])
            logs = jnp.where(place_ == 2 * p, log[:group], logs)
            logs = jnp.where(place_ == 2 * p + 1, log[group:], logs)
        part_ref[c, :, :, features:width] = with_log(logs, group).reshape(chips, share, LANES)

    pair_all(1 - core).wait_recv()
    summary_half(1 - core)

    def pair_part():
        return push(part_ref.at[1 - core], sibp_ref, pair_send.at[2], pair_recv.at[2], sibling)

    pair_part().start()
    summary_half(core)
    pair_part().wait_recv()

    left = lax.broadcasted_iota(jnp.int32, (group, LANES), 1) < HEAD

    def spread(x, p, left):
        return jnp.where(left, x[:, 2 * p : 2 * p + 1], x[:, 2 * p + 1 : 2 * p + 2])

    a = part_ref.at[core]
    log_a = without_log(a[:, :, features:width].reshape(group, LANES))
    log_b = without_log(sibp_ref[:, :, features:width].reshape(group, LANES))
    peak = jnp.maximum(log_a, log_b)
    weight_a = jnp.exp(log_a - peak)
    weight_b = jnp.exp(log_b - peak)
    total = weight_a + weight_b
    weight_a, weight_b = weight_a / total, weight_b / total
    for p in range(PAIRS):
        lanes = slice(p * LANES, (p + 1) * LANES)
        mixed = a[:, :, lanes].reshape(group, LANES).astype(jnp.float32) * spread(
            weight_a, p, left
        ) + sibp_ref[:, :, lanes].reshape(group, LANES).astype(jnp.float32) * spread(
            weight_b, p, left
        )
        chipp_ref[:, :, lanes] = mixed.astype(jnp.bfloat16).reshape(chips, share, LANES)
    chipp_ref[:, :, features:width] = with_log(peak + jnp.log(total), group).reshape(
        chips, share, LANES
    )

    def across_p(k, slot):
        other, peer = peer_of(k)
        return push(
            chipp_ref.at[other], got_ref.at[slot], across_send.at[2, k], across_recv.at[2, slot], peer
        )

    for k in range(1, chips):
        across_p(k, chip).start()
    got_ref[chip] = chipp_ref[chip]
    def sent(t, carry):
        for d in range(2):
            ring(d, t).wait_send()
            side(d, t, core).wait_send()
        return carry

    lax.fori_loop(0, steps, sent, 0)
    side_own(me).wait_send()
    pair_q().wait_send()
    pair_all(core).wait_send()
    pair_part().wait_send()

    @pl.when(holder)
    def _():
        end_q().wait_send()

    @pl.when(jnp.logical_and(at_end, jnp.logical_not(holder)))
    def _():
        end_out().wait_send()

    for k in range(1, chips):
        across_q(k, chip).wait_send()
        spread_q(k, chip).wait_send()

    for k in range(1, chips):
        other, _ = peer_of(k)
        across_p(k, other).wait_recv()
    left = lax.broadcasted_iota(jnp.int32, (share, LANES), 1) < HEAD
    logs = [without_log(got_ref[k, :, features:width]) for k in range(chips)]
    peak = functools.reduce(jnp.maximum, logs)
    weights = [jnp.exp(log - peak) for log in logs]
    scale = 1.0 / functools.reduce(jnp.add, weights)
    weights = [w * scale for w in weights]
    for p in range(PAIRS):
        lanes = slice(p * LANES, (p + 1) * LANES)
        total = jnp.zeros((share, LANES), jnp.float32)
        for k in range(chips):
            total = total + got_ref[k, :, lanes].astype(jnp.float32) * spread(weights[k], p, left)
        summary_ref[:, lanes] = total.astype(jnp.bfloat16)
    for k in range(1, chips):
        across_p(k, chip).wait_send()


def fused(queries, inputs, w_kv, rand_blocks, w_cross, vocab_table, summary_ids):
    n = lax.axis_size("ctx")
    rows, features = inputs.shape
    blocks = rows // BLOCK
    chips = n // 2
    half = chips // 2
    steps = (half - 1) * blocks + blocks // 2
    share = summary_ids.shape[0] // n
    group = chips * share
    wide = features + LANES
    bf16, f32 = jnp.bfloat16, jnp.float32
    dma = pltpu.SemaphoreType.DMA
    return pl.pallas_call(
        functools.partial(fused_kernel, n),
        out_shape=[
            jax.ShapeDtypeStruct(queries.shape, bf16),
            jax.ShapeDtypeStruct((share, features), bf16),
        ],
        in_specs=[SMEM, VMEM] + [ANY] * 5,
        out_specs=[VMEM] * 2,
        scratch_shapes=[
            pltpu.VMEM((n, blocks, BLOCK, features), bf16),
            pltpu.VMEM((n * blocks, BLOCK, 2 * features), bf16),
            pltpu.VMEM(w_kv.shape, bf16),
            pltpu.VMEM(queries.shape, bf16),
            pltpu.VMEM((max(rows, vocab_table.shape[0]), features), bf16),
            pltpu.VMEM((2, chips, share, features), bf16),
            pltpu.VMEM((chips, share, features), bf16),
            pltpu.VMEM((chips, share, features), bf16),
            pltpu.VMEM((chips, share, features), bf16),
            pltpu.VMEM((share, features), bf16),
            pltpu.VMEM((2, chips, share, features), bf16),
            pltpu.VMEM((PAIRS // 2, 2 * BLOCK, LANES), f32),
            pltpu.VMEM((PAIRS // 2, 2 * BLOCK, LANES), f32),
            pltpu.VMEM((PAIRS // 2, 2 * BLOCK, LANES), f32),
            pltpu.VMEM((BLOCK, features), bf16),
            pltpu.VMEM((BLOCK, features // 2), bf16),
            pltpu.VMEM((BLOCK, features // 2), bf16),
            pltpu.VMEM((rows, features), f32),
            pltpu.VMEM((blocks, PAIRS, 2 * BLOCK, LANES), f32),
            pltpu.VMEM((2, chips, share, wide), bf16),
            pltpu.VMEM((chips, share, wide), bf16),
            pltpu.VMEM((chips, share, wide), bf16),
            pltpu.VMEM((chips, share, wide), bf16),
            dma((2, steps)),
            dma((2, steps)),
            dma((2, steps)),
            dma((2, steps)),
            dma,
            dma,
            dma((5,)),
            dma((5,)),
            dma((3, chips)),
            dma((3, chips)),
            dma((6,)),
        ],
        compiler_params=pltpu.CompilerParams(
            collective_id=4, has_side_effects=True, vmem_limit_bytes=FUSED_LIMIT
        ),
        name="fused",
    )(
        rand_blocks.T,
        summary_ids.reshape(1, -1),
        inputs.reshape(blocks, BLOCK, features),
        queries,
        w_kv,
        w_cross,
        vocab_table,
    )


def local(queries, inputs, w_kv, rand_blocks, w_cross, vocab_table, summary_ids):
    n = lax.axis_size("ctx")
    held = 3 * n * inputs.size * 2
    path = fused if held <= HELD_LIMIT else staged
    return path(queries, inputs, w_kv, rand_blocks, w_cross, vocab_table, summary_ids)


def solution(mesh):
    return jax.shard_map(
        local,
        mesh=mesh,
        in_specs=(
            P(("groups", "ctx"), None),
            P(("groups", "ctx"), None),
            P(),
            P("groups", None),
            P(),
            P("ctx", None),
            P("groups"),
        ),
        out_specs=(P(("groups", "ctx"), None), P(("groups", "ctx"), None)),
        check_vma=False,
    )
```

```python
import functools

import jax
import jax.numpy as jnp
from jax import lax
from jax.experimental import pallas as pl
from jax.experimental.pallas import tpu as pltpu
from jax.sharding import PartitionSpec as P

HEADS = 16
HEAD = 64
BLOCK = 64
LANES = 128
PAIRS = HEADS // 2
MASKED_SCORE = -1e30
MESH = pl.DeviceIdType.MESH
VMEM = pl.BlockSpec(memory_space=pltpu.VMEM)
ANY = pl.BlockSpec(memory_space=pl.ANY)
SMEM = pl.BlockSpec(memory_space=pltpu.SMEM)
VMEM_LIMIT = 48 * 1024 * 1024
FUSED_LIMIT = 60 * 1024 * 1024
HELD_LIMIT = 40 * 1024 * 1024


def greet_all(me, n):
    barrier = pltpu.get_barrier_semaphore()

    def greet(k, carry):
        peer = lax.rem(me + k, n)
        pl.semaphore_signal(barrier, inc=1, device_id={"ctx": peer}, device_id_type=MESH)
        return carry

    lax.fori_loop(1, n, greet, 0)
    pl.semaphore_wait(barrier, n - 1)


def push(source, target, send_sem, recv_sem, peer):
    return pltpu.make_async_remote_copy(
        source, target, send_sem, recv_sem, device_id={"ctx": peer}, device_id_type=MESH
    )


def each_peer(me, n, body):
    def step(k, carry):
        body(lax.rem(me + k, n))
        return carry

    lax.fori_loop(1, n, step, 0)


def gather_kernel(
    n,
    x_ref,
    q_ref,
    looked_ref,
    all_ref,
    ends_ref,
    got_ref,
    ring_send,
    ring_recv,
    side_send,
    side_recv,
    got_send,
    got_recv,
    ends_send,
    ends_recv,
    own_sem,
):
    me = lax.axis_index("ctx")
    chips = n // 2
    half = chips // 2
    core = me % 2
    chip = me // 2
    odd = chip % 2
    place = (1 - odd) * (chip // 2) + odd * (chips - 1 - chip // 2)
    sibling = me + 1 - 2 * core
    row_count = q_ref.shape[0]

    def device(at, on_core):
        at = (at + chips) % chips
        back = at // half
        return 2 * ((1 - back) * 2 * at + back * (2 * (chips - 1 - at) + 1)) + on_core

    streams = [(d, h) for h in range(2) for d in range(2)]

    def hops(d, h):
        return half if d == h else half - 1

    def ring(d, h, s):
        sign = 1 - 2 * d
        owner = device(place - sign * s, core)
        source = x_ref.at[h] if s == 0 else all_ref.at[owner, h]
        return push(
            source,
            all_ref.at[owner, h],
            ring_send.at[d, h, s],
            ring_recv.at[d, h, s],
            device(place + sign, core),
        )

    def arrival(d, h, s):
        owner = device(place - (1 - 2 * d) * (s + 1), core)
        landed = all_ref.at[owner, h]
        return push(landed, landed, ring_send.at[d, h, s], ring_recv.at[d, h, s], sibling)

    def side(d, h, s, on_core):
        owner = device(place - (1 - 2 * d) * s, on_core)
        source = all_ref.at[owner, h]
        if s == 0:
            source = x_ref.at[h]
        return push(
            source, all_ref.at[owner, h], side_send.at[d, h, s], side_recv.at[d, h, s], sibling
        )

    own = [pltpu.make_async_copy(x_ref.at[h], all_ref.at[me, h], own_sem.at[h]) for h in range(2)]
    own.append(pltpu.make_async_copy(looked_ref.at[me], got_ref.at[me], own_sem.at[2]))
    greet_all(me, n)
    for d, h in streams:
        ring(d, h, 0).start()

    def send_looked(peer):
        push(
            looked_ref.at[peer], got_ref.at[me], got_send.at[peer], got_recv.at[me], peer
        ).start()

    each_peer(me, n, send_looked)
    ends = [q_ref.at[pl.ds(0, BLOCK)], q_ref.at[pl.ds(row_count - BLOCK, BLOCK)]]
    holders = [0, n - 1]

    steps = [(place - at + chips) % chips for at in (0, half)]
    right, left = device(place + 1, core), device(place - 1, core)

    def send_end(e, k, source):
        peer = (right, left, sibling)[k]
        return push(source, ends_ref.at[e], ends_send.at[e, k], ends_recv.at[e], peer)

    def routes(e):
        away = steps[e]
        return [
            (0, away < half),
            (1, jnp.logical_or(away == 0, away > chips - half + 1)),
            (2, me == holders[e]),
        ]

    def start_routes(e, source):
        for k, goes in routes(e)[:2]:

            @pl.when(goes)
            def _():
                send_end(e, k, source).start()

    def pass_end(e):
        send_end(e, 0, ends_ref.at[e]).wait_recv()
        start_routes(e, ends_ref.at[e])

    for e in range(2):

        @pl.when(me == holders[e])
        def _():
            send_end(e, 2, ends[e]).start()
            start_routes(e, ends[e])
            copy = pltpu.make_async_copy(ends[e], ends_ref.at[e], own_sem.at[3])
            copy.start()
            copy.wait()

        @pl.when(jnp.logical_and(steps[e] == 0, me != holders[e]))
        def _():
            pass_end(e)

    for copy in own:
        copy.start()
    for h in range(2):
        side(0, h, 0, core).start()
    for s in range(half):
        for d, h in streams:
            if s < hops(d, h):
                arrival(d, h, s).wait_recv()
                if s + 1 < hops(d, h):
                    ring(d, h, s + 1).start()
                side(d, h, s + 1, core).start()
        for e in range(2):
            near = steps[e] == s + 1
            if s + 1 < half:
                near = jnp.logical_or(near, steps[e] == chips - s - 1)

            @pl.when(near)
            def _():
                pass_end(e)

    for h in range(2):
        side(0, h, 0, core).wait_send()
        side(0, h, 0, 1 - core).wait_recv()
    for s in range(half):
        for d, h in streams:
            if s < hops(d, h):
                ring(d, h, s).wait_send()
                side(d, h, s + 1, core).wait_send()
                side(d, h, s + 1, 1 - core).wait_recv()

    def end_looked(peer):
        copy = push(
            looked_ref.at[peer], got_ref.at[peer], got_send.at[peer], got_recv.at[peer], peer
        )
        copy.wait_recv()
        copy.wait_send()

    each_peer(me, n, end_looked)
    for e in range(2):
        for k, goes in routes(e):

            @pl.when(goes)
            def _():
                send_end(e, k, ends[e]).wait_send()

    for copy in own:
        copy.wait()


def gather_inputs(x, q, looked):
    n = lax.axis_size("ctx")
    rows, features = x.shape
    half = n // 4
    dma = pltpu.SemaphoreType.DMA
    gathered, ends, got = pl.pallas_call(
        functools.partial(gather_kernel, n),
        out_shape=[
            jax.ShapeDtypeStruct((n, 2, rows // 2, features), x.dtype),
            jax.ShapeDtypeStruct((2, BLOCK, features), q.dtype),
            jax.ShapeDtypeStruct(looked.shape, looked.dtype),
        ],
        in_specs=[ANY] * 3,
        out_specs=[ANY] * 3,
        scratch_shapes=[
            dma((2, 2, half)),
            dma((2, 2, half)),
            dma((2, 2, half + 1)),
            dma((2, 2, half + 1)),
            dma((n,)),
            dma((n,)),
            dma((2, 3)),
            dma((2,)),
            dma((4,)),
        ],
        compiler_params=pltpu.CompilerParams(collective_id=1, has_side_effects=True),
        name="gather_inputs",
    )(x.reshape(2, rows // 2, features), q, looked)
    return gathered.reshape(n * rows // BLOCK, BLOCK, features), ends, got


def ends_kernel(
    n,
    mine_ref,
    out_ref,
    log_ref,
    rows_ref,
    outs_ref,
    logs_ref,
    rows_send,
    rows_recv,
    ends_send,
    ends_recv,
    own_sem,
):
    me = lax.axis_index("ctx")
    holders = [0, n - 1]
    pairs = [(out_ref, outs_ref), (log_ref, logs_ref)]

    def end(e, i, slot):
        source, target = pairs[i]
        return push(
            source.at[e], target.at[slot], ends_send.at[e, i], ends_recv.at[i, slot], holders[e]
        )

    own = pltpu.make_async_copy(mine_ref, rows_ref.at[me], own_sem.at[2])
    own.start()
    greet_all(me, n)
    for e in range(2):

        @pl.when(me != holders[e])
        def _():
            for i in range(2):
                end(e, i, me).start()

        @pl.when(me == holders[e])
        def _():
            for i in range(2):
                source, target = pairs[i]
                copy = pltpu.make_async_copy(source.at[e], target.at[me], own_sem.at[i])
                copy.start()
                copy.wait()

    def send_rows(peer):
        push(mine_ref, rows_ref.at[me], rows_send.at[peer], rows_recv.at[me], peer).start()

    each_peer(me, n, send_rows)

    def end_rows(peer):
        copy = push(mine_ref, rows_ref.at[peer], rows_send.at[peer], rows_recv.at[peer], peer)
        copy.wait_recv()
        copy.wait_send()

    each_peer(me, n, end_rows)
    for e in range(2):

        @pl.when(me != holders[e])
        def _():
            for i in range(2):
                end(e, i, me).wait_send()

        @pl.when(me == holders[e])
        def _():
            def arrived(peer):
                for i in range(2):
                    source, target = pairs[i]
                    push(
                        source.at[e],
                        target.at[peer],
                        ends_send.at[e, i],
                        ends_recv.at[i, peer],
                        peer,
                    ).wait_recv()

            each_peer(me, n, arrived)

    own.wait()


def send_ends(mine, out, log):
    n = lax.axis_size("ctx")
    dma = pltpu.SemaphoreType.DMA
    out = out.reshape(2, BLOCK, out.shape[1])
    log = log.reshape(2, BLOCK, LANES)
    return pl.pallas_call(
        functools.partial(ends_kernel, n),
        out_shape=[
            jax.ShapeDtypeStruct((n,) + mine.shape, mine.dtype),
            jax.ShapeDtypeStruct((n,) + out.shape[1:], out.dtype),
            jax.ShapeDtypeStruct((n,) + log.shape[1:], log.dtype),
        ],
        in_specs=[ANY] * 3,
        out_specs=[ANY] * 3,
        scratch_shapes=[dma((n,)), dma((n,)), dma((2, 2)), dma((2, n)), dma((3,))],
        compiler_params=pltpu.CompilerParams(collective_id=2, has_side_effects=True),
        name="send_ends",
    )(mine, out, log)


def combine(outs_ref, logs_ref, total_ref):
    n, rows, features = outs_ref.shape
    peak = lax.fori_loop(
        1, n, lambda i, peak: jnp.maximum(peak, logs_ref[i]), logs_ref[0]
    )
    left = lax.broadcasted_iota(jnp.int32, (rows, LANES), 1) < HEAD
    total_ref[...] = jnp.zeros_like(total_ref)

    def spread(x, p):
        return jnp.where(left, x[:, 2 * p : 2 * p + 1], x[:, 2 * p + 1 : 2 * p + 2])

    def add(i, total):
        weights = jnp.exp(logs_ref[i] - peak)
        for p in range(PAIRS):
            lanes = slice(p * LANES, (p + 1) * LANES)
            total_ref[:, lanes] += outs_ref[i, :, lanes].astype(jnp.float32) * spread(weights, p)
        return total + weights

    scale = 1.0 / lax.fori_loop(0, n, add, jnp.zeros((rows, LANES), jnp.float32))
    for p in range(PAIRS):
        lanes = slice(p * LANES, (p + 1) * LANES)
        total_ref[:, lanes] = total_ref[:, lanes] * spread(scale, p)


def summary_kernel(
    n,
    part_ref,
    log_ref,
    out_ref,
    outs_ref,
    logs_ref,
    total_ref,
    send_sem,
    recv_sem,
    own_sem,
):
    me = lax.axis_index("ctx")
    pairs = [(part_ref, outs_ref), (log_ref, logs_ref)]
    own = [
        pltpu.make_async_copy(source.at[me], target.at[me], own_sem.at[i])
        for i, (source, target) in enumerate(pairs)
    ]
    for copy in own:
        copy.start()
    greet_all(me, n)

    def copies(peer, slot):
        return [
            push(
                source.at[peer], target.at[slot], send_sem.at[i, peer], recv_sem.at[i, slot], peer
            )
            for i, (source, target) in enumerate(pairs)
        ]

    def send(peer):
        for copy in copies(peer, me):
            copy.start()

    each_peer(me, n, send)

    def finish(peer):
        for copy in copies(peer, peer):
            copy.wait_recv()
            copy.wait_send()

    each_peer(me, n, finish)
    for copy in own:
        copy.wait()
    combine(outs_ref, logs_ref, total_ref)
    out_ref[...] = total_ref[...].astype(out_ref.dtype)


def combined_summary(part, logs):
    n, share, features = part.shape
    dma = pltpu.SemaphoreType.DMA
    return pl.pallas_call(
        functools.partial(summary_kernel, n),
        out_shape=jax.ShapeDtypeStruct((share, features), jnp.bfloat16),
        in_specs=[ANY] * 2,
        out_specs=VMEM,
        scratch_shapes=[
            pltpu.VMEM(part.shape, part.dtype),
            pltpu.VMEM(logs.shape, logs.dtype),
            pltpu.VMEM((share, features), jnp.float32),
            dma((2, n)),
            dma((2, n)),
            dma((2,)),
        ],
        compiler_params=pltpu.CompilerParams(collective_id=3, has_side_effects=True),
        name="combined_summary",
    )(part, logs)


def dot_t(a, b):
    return lax.dot_general(a, b, (((1,), (1,)), ((), ())), preferred_element_type=jnp.float32)


def stacked_pair(q):
    q = q * jnp.asarray(HEAD**-0.5, q.dtype)
    left = lax.broadcasted_iota(jnp.int32, q.shape, 1) < HEAD
    zero = jnp.zeros_like(q)
    return jnp.concatenate([jnp.where(left, q, zero), jnp.where(left, zero, q)], axis=0)


def unstacked_pair(o):
    rows = o.shape[0] // 2
    left = lax.broadcasted_iota(jnp.int32, (rows, LANES), 1) < HEAD
    return jnp.where(left, o[:rows], o[rows:])


def project(x_ref, w_ref, out_ref, tile):
    rows, cols = out_ref.shape
    width = 512

    def step(t, carry):
        at = pl.ds(pl.multiple_of(t * tile, tile), tile)
        x = x_ref[at, :]
        for c in range(cols // width):
            y = jnp.dot(
                x, w_ref[:, c * width : (c + 1) * width], preferred_element_type=jnp.float32
            )
            out_ref[at, c * width : (c + 1) * width] = y.astype(out_ref.dtype)
        return carry

    lax.fori_loop(0, rows // tile, step, 0)


def partial_attention(q_ref, kv_ref, out_ref, log_ref):
    rows, features = q_ref.shape
    place = lax.broadcasted_iota(jnp.int32, (rows, LANES), 1)
    logs = jnp.zeros((rows, LANES), jnp.float32)
    for p in range(PAIRS):
        lanes = slice(p * LANES, (p + 1) * LANES)
        values = slice(features + p * LANES, features + (p + 1) * LANES)
        scores = dot_t(stacked_pair(q_ref[:, lanes]), kv_ref[:, lanes])
        peak = jnp.max(scores, axis=1, keepdims=True)
        weights = jnp.exp(scores - peak)
        totals = jnp.sum(weights, axis=1, keepdims=True)
        sums = jnp.dot(
            weights.astype(jnp.bfloat16), kv_ref[:, values], preferred_element_type=jnp.float32
        )
        out_ref[:, lanes] = unstacked_pair(sums / totals).astype(out_ref.dtype)
        log = peak + jnp.log(totals)
        logs = jnp.where(place == 2 * p, log[:rows], logs)
        logs = jnp.where(place == 2 * p + 1, log[rows:], logs)
    log_ref[...] = logs


def global_kernel(q_ref, x_ref, w_ref, out_ref, log_ref, kv_ref):
    project(x_ref, w_ref, kv_ref, 128)
    partial_attention(q_ref, kv_ref, out_ref, log_ref)


def global_partial(q, x, w):
    return pl.pallas_call(
        global_kernel,
        out_shape=[
            jax.ShapeDtypeStruct(q.shape, jnp.bfloat16),
            jax.ShapeDtypeStruct((q.shape[0], LANES), jnp.float32),
        ],
        in_specs=[VMEM] * 3,
        out_specs=[VMEM] * 2,
        scratch_shapes=[pltpu.VMEM((x.shape[0], w.shape[1]), jnp.bfloat16)],
        compiler_params=pltpu.CompilerParams(vmem_limit_bytes=VMEM_LIMIT),
        cost_estimate=pl.CostEstimate(
            flops=2 * x.size * w.shape[1], bytes_accessed=6 << 20, transcendentals=1 << 20
        ),
        name="global_partial",
    )(q, x, w)


def block_kernel(
    pick_count,
    ids_ref,
    edge_ref,
    all_ref,
    q_ref,
    x_ref,
    w_kv_ref,
    w_cross_ref,
    outs_ref,
    logs_ref,
    sq_ref,
    attended_ref,
    out_ref,
    log_ref,
    rows_ref,
    kv_ref,
    total_ref,
    sem,
):
    row_count, features = x_ref.shape
    block_count = row_count // BLOCK
    slots = rows_ref.shape[0] // BLOCK
    far_start = (block_count + 4) * BLOCK
    span = (5 + pick_count) * BLOCK

    def fetch(i):
        return pltpu.make_async_copy(
            all_ref.at[ids_ref[i]],
            rows_ref.at[pl.ds(pl.multiple_of(i * BLOCK, BLOCK), BLOCK)],
            sem.at[i],
        )

    for i in range(slots):
        fetch(i).start()
    for i in range(slots):
        fetch(i).wait()
    project(rows_ref, w_kv_ref, kv_ref, 2 * BLOCK)

    column = lax.broadcasted_iota(jnp.int32, (2 * BLOCK, span), 1)

    def one_block(b, carry):
        first = edge_ref[0] + b
        hidden = jnp.logical_or(
            jnp.logical_and(column < BLOCK, first < 2),
            jnp.logical_and(
                jnp.logical_and(column >= 2 * BLOCK, column < 3 * BLOCK), first > edge_ref[1] - 3
            ),
        )
        near = pl.ds(pl.multiple_of(b * BLOCK, BLOCK), 3 * BLOCK)
        ends = pl.ds((block_count + 2) * BLOCK, 2 * BLOCK)
        far = pl.ds(
            pl.multiple_of(far_start + b * pick_count * BLOCK, BLOCK), pick_count * BLOCK
        )
        here = pl.ds(pl.multiple_of(b * BLOCK, BLOCK), BLOCK)
        for p in range(PAIRS):
            lanes = slice(p * LANES, (p + 1) * LANES)
            values = slice(features + p * LANES, features + (p + 1) * LANES)
            k = jnp.concatenate(
                [kv_ref[near, lanes], kv_ref[ends, lanes], kv_ref[far, lanes]], axis=0
            )
            v = jnp.concatenate(
                [kv_ref[near, values], kv_ref[ends, values], kv_ref[far, values]], axis=0
            )
            scores = dot_t(stacked_pair(q_ref[here, lanes]), k)
            scores = jnp.where(hidden, MASKED_SCORE, scores)
            weights = jnp.exp(scores - jnp.max(scores, axis=1, keepdims=True))
            totals = jnp.sum(weights, axis=1, keepdims=True)
            probs = (weights * (1.0 / totals)).astype(jnp.bfloat16)
            o = jnp.dot(probs, v, preferred_element_type=jnp.float32)
            attended_ref[here, lanes] = unstacked_pair(o).astype(jnp.bfloat16)
        return carry

    lax.fori_loop(0, block_count, one_block, 0)

    def place(rows):
        combine(outs_ref, logs_ref, total_ref)
        attended_ref[rows] = total_ref[...].astype(jnp.bfloat16)

    @pl.when(edge_ref[0] == 0)
    def _():
        place(slice(0, BLOCK))

    @pl.when(edge_ref[0] + block_count == edge_ref[1])
    def _():
        place(slice(row_count - BLOCK, row_count))

    encoded = x_ref[...].astype(jnp.float32) + attended_ref[...].astype(jnp.float32)
    rows_ref[:row_count] = encoded.astype(jnp.bfloat16)
    project(rows_ref.at[:row_count], w_cross_ref, kv_ref.at[:row_count], 2 * BLOCK)
    partial_attention(sq_ref, kv_ref.at[:row_count], out_ref, log_ref)


def block_attention(ids, edge, everything, q, x, w_kv, w_cross, outs, end_logs, sq, pick_count):
    slots = ids.shape[0]
    features = x.shape[1]
    return pl.pallas_call(
        functools.partial(block_kernel, pick_count),
        out_shape=[
            jax.ShapeDtypeStruct(q.shape, jnp.bfloat16),
            jax.ShapeDtypeStruct(sq.shape, jnp.bfloat16),
            jax.ShapeDtypeStruct((sq.shape[0], LANES), jnp.float32),
        ],
        in_specs=[SMEM, SMEM, ANY] + [VMEM] * 7,
        out_specs=[VMEM] * 3,
        scratch_shapes=[
            pltpu.VMEM((slots * BLOCK, features), jnp.bfloat16),
            pltpu.VMEM((slots * BLOCK, 2 * features), jnp.bfloat16),
            pltpu.VMEM((BLOCK, features), jnp.float32),
            pltpu.SemaphoreType.DMA((slots,)),
        ],
        compiler_params=pltpu.CompilerParams(vmem_limit_bytes=VMEM_LIMIT),
        cost_estimate=pl.CostEstimate(
            flops=20 << 30, bytes_accessed=16 << 20, transcendentals=5 << 20
        ),
        name="block_attention",
    )(ids, edge, everything, q, x, w_kv, w_cross, outs, end_logs, sq)


def staged(queries, inputs, w_kv, rand_blocks, w_cross, vocab_table, summary_ids):
    n = lax.axis_size("ctx")
    position = lax.axis_index("ctx")
    row_count, features = inputs.shape
    block_count = row_count // BLOCK
    pick_count = rand_blocks.shape[1]
    total_blocks = block_count * n
    shard_rows = vocab_table.shape[0]
    summary_count = summary_ids.shape[0]
    share = summary_count // n
    offsets = summary_ids - position * shard_rows
    inside = jnp.logical_and(offsets >= 0, offsets < shard_rows)
    looked = vocab_table[jnp.clip(offsets, 0, shard_rows - 1)]
    looked = jnp.where(inside[:, None], looked, jnp.zeros((), looked.dtype))
    everything, end_queries, got = gather_inputs(
        inputs, queries, looked.reshape(n, share, features)
    )
    mine = jnp.sum(got.astype(jnp.float32), axis=0).astype(jnp.bfloat16)
    end_out, end_log = global_partial(end_queries.reshape(2 * BLOCK, features), inputs, w_kv)
    rows, outs, end_logs = send_ends(mine, end_out, end_log)
    summary_queries = rows.reshape(summary_count, features)

    start = position * block_count
    near = jnp.clip(start - 1 + jnp.arange(block_count + 2, dtype=jnp.int32), 0, total_blocks - 1)
    fixed = jnp.array([0, total_blocks - 1], jnp.int32)
    picks = lax.dynamic_slice_in_dim(rand_blocks, start, block_count, 0).reshape(-1)
    ids = jnp.concatenate([near, fixed, picks.astype(jnp.int32)])
    edge = jnp.stack([start, jnp.full_like(start, total_blocks)]).astype(jnp.int32)
    attended, part, logs = block_attention(
        ids,
        edge,
        everything,
        queries,
        inputs,
        w_kv,
        w_cross,
        outs,
        end_logs,
        summary_queries,
        pick_count,
    )
    summary = combined_summary(
        part.reshape(n, share, features), logs.reshape(n, share, LANES)
    )
    return attended, summary


def ring_order(half, blocks, d):
    ends_first = [j // 2 if j % 2 == 0 else blocks - 1 - j // 2 for j in range(blocks)]
    group = blocks // 2
    order = []
    for g in range(2):
        members = range(g * group, (g + 1) * group)
        last = [i for i in members if i % 2 == d]
        rest = [i for i in members if i % 2 != d]
        for hop in range(half):
            order += [(hop, ends_first[i]) for i in (last if hop == half - 1 else last + rest)]
    return order


def look_up(values, t):
    found = values[0]
    for j in range(1, len(values)):
        if values[j] != values[j - 1]:
            found = jnp.where(t >= j, values[j], found)
    return found


def dots(x, w_ref, store):
    width = 512
    for c in range(w_ref.shape[1] // width):
        cols = slice(c * width, (c + 1) * width)
        y = jnp.dot(x, w_ref[:, cols], preferred_element_type=jnp.float32)
        store(cols, y.astype(jnp.bfloat16))


def lanes_of(p):
    return slice(p * LANES, (p + 1) * LANES)


def row_max(x):
    return jnp.max(x, axis=1, keepdims=True)


def row_sum(x):
    return jnp.sum(x, axis=1, keepdims=True)


def weighted(weights, v):
    return jnp.dot(weights.astype(jnp.bfloat16), v, preferred_element_type=jnp.float32)


def with_log(log, rows):
    place = lax.broadcasted_iota(jnp.int32, (rows, LANES), 1)
    high = log.astype(jnp.bfloat16)
    rest = log - high.astype(jnp.float32)
    middle = rest.astype(jnp.bfloat16)
    low = (rest - middle.astype(jnp.float32)).astype(jnp.bfloat16)
    low, middle = low.astype(jnp.float32), middle.astype(jnp.float32)
    packed = jnp.where(place < HEADS, high.astype(jnp.float32), 0.0)
    packed = jnp.where(place // HEADS == 1, pltpu.roll(middle, HEADS, 1), packed)
    packed = jnp.where(place // HEADS == 2, pltpu.roll(low, 2 * HEADS, 1), packed)
    return packed.astype(jnp.bfloat16)


def without_log(packed):
    packed = packed.astype(jnp.float32)
    middle = pltpu.roll(packed, LANES - HEADS, 1)
    low = pltpu.roll(packed, LANES - 2 * HEADS, 1)
    return packed + (middle + low)


def fused_kernel(
    n,
    picks_ref,
    sids_ref,
    x_ref,
    q_hbm,
    w_kv_hbm,
    w_cross_hbm,
    vocab_hbm,
    attended_hbm,
    summary_ref,
    attended_ref,
    x_all,
    kv_all,
    w_kv_ref,
    q_ref,
    shared_ref,
    looked_ref,
    sibq_ref,
    chipq_ref,
    sideq_ref,
    lineq_ref,
    partq_ref,
    mine_ref,
    sumq_ref,
    acc_ref,
    peak_ref,
    sum_ref,
    end_q_ref,
    end_out_ref,
    end_half_ref,
    near_ref,
    near_log_ref,
    part_ref,
    sibp_ref,
    chipp_ref,
    got_ref,
    ring_send,
    ring_recv,
    side_send,
    side_recv,
    along_send,
    along_recv,
    own_send,
    own_recv,
    pair_send,
    pair_recv,
    across_send,
    across_recv,
    local_sem,
):
    me = lax.axis_index("ctx")
    chips = n // 2
    half = chips // 2
    core = me % 2
    chip = me // 2
    odd = chip % 2
    place = (1 - odd) * (chip // 2) + odd * (chips - 1 - chip // 2)
    sibling = me + 1 - 2 * core
    blocks = x_ref.shape[0]
    features = x_ref.shape[2]
    rows = blocks * BLOCK
    share = summary_ref.shape[0]
    steps = (half - 1) * blocks + blocks // 2
    total_blocks = n * blocks
    holder = jnp.logical_or(me == 0, me == n - 1)
    at_end = jnp.logical_or(chip == 0, chip == chips - 1)
    orders = [ring_order(half, blocks, d) for d in range(2)]
    ahead = blocks // 2

    def device(at, on_core):
        at = (at + chips) % chips
        back = at // half
        return 2 * ((1 - back) * 2 * at + back * (2 * (chips - 1 - at) + 1)) + on_core

    def block_of(d, t):
        if isinstance(t, int):
            return orders[d][t][1]
        return look_up([block for _, block in orders[d]], t)

    def hop_of(d, t):
        if isinstance(t, int):
            return orders[d][t][0]
        return look_up([hop for hop, _ in orders[d]], t)

    def ring(d, t):
        held = x_all.at[device(place - (1 - 2 * d) * hop_of(d, t), core), block_of(d, t)]
        return push(
            held, held, ring_send.at[d, t], ring_recv.at[d, t], device(place + 1 - 2 * d, core)
        )

    def ring_own(d, t):
        return push(
            x_ref.at[block_of(d, t)],
            x_all.at[me, block_of(d, t)],
            ring_send.at[d, t],
            ring_recv.at[d, t],
            device(place + 1 - 2 * d, core),
        )

    def owner_of(d, t, on_core):
        return device(place - (1 - 2 * d) * (hop_of(d, t) + 1), on_core)

    def arrival(d, t):
        landed = x_all.at[owner_of(d, t, core), block_of(d, t)]
        return push(landed, landed, ring_send.at[d, t], ring_recv.at[d, t], sibling)

    def side(d, t, on_core):
        landed = x_all.at[owner_of(d, t, on_core), block_of(d, t)]
        return push(landed, landed, side_send.at[d, t], side_recv.at[d, t], sibling)

    def side_own(on):
        return push(x_ref, x_all.at[on], own_send, own_recv, sibling)

    def peer_of(k):
        other = lax.rem(chip + k, chips)
        return other, 2 * other + core

    shard_rows = vocab_hbm.shape[0]
    vocab_ref = shared_ref.at[:shard_rows]
    encoded_ref = shared_ref.at[:rows]
    cross_ref = kv_all.at[:blocks]
    loads = [
        pltpu.make_async_copy(source, target, local_sem.at[i])
        for i, (source, target) in enumerate(
            [
                (vocab_hbm, vocab_ref),
                (w_kv_hbm, w_kv_ref),
                (x_ref, x_all.at[me]),
                (q_hbm, q_ref),
            ]
        )
    ]
    for load in loads:
        load.start()

    barrier = pltpu.get_barrier_semaphore()
    pl.semaphore_signal(barrier, inc=1, device_id={"ctx": sibling}, device_id_type=MESH)
    for k in range(1, chips):
        pl.semaphore_signal(
            barrier, inc=1, device_id={"ctx": peer_of(k)[1]}, device_id_type=MESH
        )
    pl.semaphore_wait(barrier, chips)

    for t in range(ahead):
        for d in range(2):
            ring_own(d, t).start()
    end_row = pl.multiple_of(jnp.where(chip == 0, 0, rows - BLOCK), BLOCK)

    def end_q():
        return push(
            q_hbm.at[pl.ds(end_row, BLOCK)], end_q_ref, pair_send.at[3], pair_recv.at[3], sibling
        )

    def end_out():
        return push(end_out_ref, end_half_ref, pair_send.at[4], pair_recv.at[4], sibling)

    @pl.when(holder)
    def _():
        end_q().start()
        copy = pltpu.make_async_copy(
            q_hbm.at[pl.ds(end_row, BLOCK)], end_q_ref, local_sem.at[5]
        )
        copy.start()
        copy.wait()

    side_own(me).start()

    loads[0].wait()
    summary_count = sids_ref.shape[1]
    offsets = sids_ref[...] - me * shard_rows
    hot = lax.broadcasted_iota(jnp.int32, (shard_rows, summary_count), 0) == offsets
    hot = jnp.where(hot, 1.0, 0.0).astype(jnp.bfloat16)
    looked = lax.dot_general(
        hot, vocab_ref[...], (((0,), (0,)), ((), ())), preferred_element_type=jnp.float32
    ).astype(jnp.bfloat16)
    for k in range(chips):
        for c in range(2):
            at = (2 * k + c) * share
            looked_ref[c, k % 2, k // 2] = looked[at : at + share]

    def pair_q():
        return push(
            looked_ref.at[1 - core], sibq_ref, pair_send.at[0], pair_recv.at[0], sibling
        )

    pair_q().start()
    loads[1].wait()
    loads[2].wait()

    def project_owner(owner):
        def step(t, carry):
            x = x_all[owner, pl.ds(2 * t, 2)].reshape(2 * BLOCK, features)

            def store(cols, y):
                kv_all[pl.ds(owner * blocks + 2 * t, 2), :, cols] = y.reshape(2, BLOCK, -1)

            dots(x, w_kv_ref, store)
            return carry

        lax.fori_loop(0, blocks // 2, step, 0)

    project_owner(me)
    pair_q().wait_recv()
    chipq_ref[...] = looked_ref[core] + sibq_ref[...]

    column = 2 * (chip + 1 - 2 * odd) + core
    level = chip // 2

    def level_of(k):
        other = lax.rem(level + k, half)
        return other, 2 * (2 * other + odd) + core

    def across_q():
        return push(chipq_ref.at[1 - odd], sideq_ref, pair_send.at[5], pair_recv.at[5], column)

    across_q().start()

    def along_q(k, slot):
        other, peer = level_of(k)
        return push(
            lineq_ref.at[other], partq_ref.at[slot], along_send.at[0, k], along_recv.at[0, slot], peer
        )

    def add_across():
        across_q().wait_recv()
        lineq_ref[...] = chipq_ref[odd] + sideq_ref[...]
        for k in range(1, half):
            along_q(k, level).start()
        partq_ref[level] = lineq_ref[level]

    def spread_along(k, slot):
        _, peer = level_of(k)
        return push(
            mine_ref,
            sumq_ref.at[core, odd, slot],
            along_send.at[1, k],
            along_recv.at[1, slot],
            peer,
        )

    def add_along():
        for k in range(1, half):
            along_q(k, level_of(k)[0]).wait_recv()
        mine = partq_ref[0].astype(jnp.float32)
        for k in range(1, half):
            mine = mine + partq_ref[k].astype(jnp.float32)
        mine_ref[...] = mine.astype(jnp.bfloat16)
        for k in range(1, half):
            spread_along(k, level).start()
        sumq_ref[core, odd, level] = mine_ref[...]

    def spread_across(x):
        held = sumq_ref.at[core, x]
        return push(held, held, pair_send.at[6], pair_recv.at[6], column)

    side_own(sibling).wait_recv()
    project_owner(sibling)

    loads[3].wait()
    half_pairs = PAIRS // 2

    def half_lanes(p):
        return pl.multiple_of((core * half_pairs + p) * LANES, LANES)

    def take_keys(parts):
        every = range(half_pairs)
        scores = []
        for p in every:
            lanes = pl.ds(half_lanes(p), LANES)
            k = jnp.concatenate([kv_all[at, :, lanes] for at in parts], axis=0)
            scores.append(dot_t(stacked_pair(end_q_ref[:, lanes]), k.reshape(-1, LANES)))
        before = [peak_ref[p] for p in every]
        peaks = [jnp.maximum(before[p], row_max(scores[p])) for p in every]
        weights = [jnp.exp(scores[p] - peaks[p][:, :1]) for p in every]
        fades = [jnp.exp(before[p] - peaks[p]) for p in every]
        totals = [row_sum(weights[p]) for p in every]
        sums = []
        for p in every:
            values = pl.ds(features + half_lanes(p), LANES)
            v = jnp.concatenate([kv_all[at, :, values] for at in parts], axis=0)
            sums.append(weighted(weights[p], v.reshape(-1, LANES)))
        for p in every:
            peak_ref[p] = peaks[p]
            sum_ref[p] = sum_ref[p] * fades[p] + totals[p]
            acc_ref[p] = acc_ref[p] * fades[p] + sums[p]

    @pl.when(jnp.logical_and(at_end, jnp.logical_not(holder)))
    def _():
        end_q().wait_recv()

    @pl.when(at_end)
    def _():
        peak_ref[...] = jnp.full_like(peak_ref, MASKED_SCORE)
        sum_ref[...] = jnp.zeros_like(sum_ref)
        acc_ref[...] = jnp.zeros_like(acc_ref)
        for i in range(2):
            take_keys([pl.ds((2 * chip + i) * blocks, blocks)])

    def process(found):
        x = jnp.concatenate([x_all[owner, block] for owner, block in found], axis=0)
        parts = [owner * blocks + block for owner, block in found]

        def store(cols, y):
            for i, at in enumerate(parts):
                kv_all[at, :, cols] = y[i * BLOCK : (i + 1) * BLOCK]

        dots(x, w_kv_ref, store)

        @pl.when(at_end)
        def _():
            take_keys(parts)

    def own_blocks(t):
        return [(owner_of(d, t, core), block_of(d, t)) for d in range(2)]

    def side_blocks(t):
        return [(owner_of(d, t, 1 - core), block_of(d, t)) for d in range(2)]

    def pass_on(t):
        for d in range(2):
            arrival(d, t).wait_recv()

            @pl.when(t + ahead < steps)
            def _():
                ring(d, t + ahead).start()

            side(d, t, core).start()

    def first(t):
        pass_on(t)
        process(own_blocks(t))

    def one_step(t, carry):
        pass_on(t)
        for d in range(2):
            side(d, t - 1, 1 - core).wait_recv()
        process(own_blocks(t) + side_blocks(t - 1))

        @pl.when(jnp.logical_and(t >= near_from, t < near_from + blocks))
        def _():
            near_keys(t - near_from)

        pl.when(t == blocks)(add_across)
        pl.when(t == steps - blocks // 2)(add_along)
        return carry

    start = me * blocks
    near_from = 2 + max(
        t for d in range(2) for t, (_, b) in enumerate(orders[d]) if b in (0, blocks - 1)
    )
    key_at = lax.broadcasted_iota(jnp.int32, (2 * BLOCK, 5 * BLOCK), 1)

    def near_keys(b):
        here = start + b
        hidden = jnp.logical_or(
            jnp.logical_and(key_at < BLOCK, here < 2),
            jnp.logical_and(key_at // BLOCK == 2, here > total_blocks - 3),
        )
        chosen = [
            jnp.maximum(here - 1, 0),
            here,
            jnp.minimum(here + 1, total_blocks - 1),
            0,
            total_blocks - 1,
        ]
        out = pl.ds(pl.multiple_of(b * BLOCK, BLOCK), BLOCK)
        scores = []
        for p in range(PAIRS):
            k = jnp.concatenate([kv_all[at, :, lanes_of(p)] for at in chosen], axis=0)
            scores.append(dot_t(stacked_pair(q_ref[out, lanes_of(p)]), k))
        scores = [jnp.where(hidden, MASKED_SCORE, x) for x in scores]
        peaks = [row_max(x) for x in scores]
        weights = [jnp.exp(x - peak) for x, peak in zip(scores, peaks)]
        totals = [row_sum(x) for x in weights]
        sums = []
        for p in range(PAIRS):
            v = jnp.concatenate([kv_all[at, :, lanes_of(PAIRS + p)] for at in chosen], axis=0)
            sums.append(weighted(weights[p], v))
        for p in range(PAIRS):
            near_ref[out, lanes_of(p)] = unstacked_pair(sums[p] * (1.0 / totals[p]))
            near_log_ref[b, p] = jnp.broadcast_to(
                peaks[p] + jnp.log(totals[p]), (2 * BLOCK, LANES)
            )

    first(0)
    lax.fori_loop(1, steps, one_step, 0)

    for k in range(1, half):
        spread_along(k, level_of(k)[0]).wait_recv()
    spread_across(odd).start()
    for d in range(2):
        side(d, steps - 1, 1 - core).wait_recv()
    process(side_blocks(steps - 1))
    load_cross = pltpu.make_async_copy(w_cross_hbm, w_kv_ref, local_sem.at[4])
    load_cross.start()

    @pl.when(jnp.logical_and(at_end, jnp.logical_not(holder)))
    def _():
        for p in range(half_pairs):
            lanes = slice(p * LANES, (p + 1) * LANES)
            end_out_ref[:, lanes] = unstacked_pair(acc_ref[p] * (1.0 / sum_ref[p])).astype(
                jnp.bfloat16
            )
        end_out().start()

    together = 2

    def random_keys(t, carry):
        work = [(together * t + i, p) for i in range(together) for p in range(PAIRS)]
        chosen = [[picks_ref[i, start + b] for i in range(picks_ref.shape[0])] for b, _ in work]
        outs = [pl.ds(pl.multiple_of(b * BLOCK, BLOCK), BLOCK) for b, _ in work]
        scores = []
        for (_, p), out, found in zip(work, outs, chosen):
            k = jnp.concatenate([kv_all[at, :, lanes_of(p)] for at in found], axis=0)
            scores.append(dot_t(stacked_pair(q_ref[out, lanes_of(p)]), k))
        logs = [near_log_ref[b, p] for b, p in work]
        peaks = [jnp.maximum(log, row_max(x)) for log, x in zip(logs, scores)]
        weights = [jnp.exp(x - peak[:, :1]) for x, peak in zip(scores, peaks)]
        fades = [jnp.exp(log - peak) for log, peak in zip(logs, peaks)]
        scales = [1.0 / (fade + row_sum(x)) for fade, x in zip(fades, weights)]
        sums = []
        for (_, p), x, found in zip(work, weights, chosen):
            v = jnp.concatenate([kv_all[at, :, lanes_of(PAIRS + p)] for at in found], axis=0)
            sums.append(weighted(x, v))
        for i, (b, p) in enumerate(work):
            o = unstacked_pair(sums[i] * scales[i])
            o = o + near_ref[outs[i], lanes_of(p)] * unstacked_pair(fades[i] * scales[i])
            attended_ref[outs[i], lanes_of(p)] = o.astype(jnp.bfloat16)
        return carry

    lax.fori_loop(0, blocks // together, random_keys, 0)

    @pl.when(holder)
    def _():
        for p in range(half_pairs):
            attended_ref[pl.ds(end_row, BLOCK), pl.ds(half_lanes(p), LANES)] = unstacked_pair(
                acc_ref[p] * (1.0 / sum_ref[p])
            ).astype(jnp.bfloat16)
        end_out().wait_recv()
        there = pl.multiple_of((1 - core) * half_pairs * LANES, LANES)
        attended_ref[pl.ds(end_row, BLOCK), pl.ds(there, half_pairs * LANES)] = end_half_ref[...]

    spread_across(1 - odd).wait_recv()

    def pair_all(c):
        return push(sumq_ref.at[c], sumq_ref.at[c], pair_send.at[1], pair_recv.at[1], sibling)

    pair_all(core).start()
    store = pltpu.make_async_copy(attended_ref, attended_hbm, local_sem.at[6])
    store.start()
    encoded = x_all[me].reshape(rows, features).astype(jnp.float32)
    encoded = encoded + attended_ref[...].astype(jnp.float32)
    encoded_ref[...] = encoded.astype(jnp.bfloat16)
    load_cross.wait()

    def project_cross(t, carry):
        x = encoded_ref[pl.ds(pl.multiple_of(t * 2 * BLOCK, 2 * BLOCK), 2 * BLOCK)]

        def store(cols, y):
            cross_ref[pl.ds(2 * t, 2), :, cols] = y.reshape(2, BLOCK, -1)

        dots(x, w_kv_ref, store)
        return carry

    lax.fori_loop(0, blocks // 2, project_cross, 0)

    def cross_of(p):
        return cross_ref[:, :, lanes_of(p)].reshape(rows, LANES)

    group = chips * share
    width = features + LANES

    def summary_half(c):
        place_ = lax.broadcasted_iota(jnp.int32, (group, LANES), 1)
        logs = jnp.zeros((group, LANES), jnp.float32)
        scores = []
        for p in range(PAIRS):
            q = sumq_ref[c, :, :, :, lanes_of(p)].reshape(group, LANES)
            scores.append(dot_t(stacked_pair(q), cross_of(p)))
        peaks = [row_max(x) for x in scores]
        weights = [jnp.exp(x - peak) for x, peak in zip(scores, peaks)]
        totals = [row_sum(x) for x in weights]
        sums = [weighted(weights[p], cross_of(PAIRS + p)) for p in range(PAIRS)]
        for p in range(PAIRS):
            part = unstacked_pair(sums[p] * (1.0 / totals[p])).astype(jnp.bfloat16)
            part_ref[c, :, :, :, lanes_of(p)] = part.reshape(2, half, share, LANES)
            log = peaks[p] + jnp.log(totals[p])
            logs = jnp.where(place_ == 2 * p, log[:group], logs)
            logs = jnp.where(place_ == 2 * p + 1, log[group:], logs)
        part_ref[c, :, :, :, features:width] = with_log(logs, group).reshape(
            2, half, share, LANES
        )

    pair_all(1 - core).wait_recv()
    summary_half(1 - core)

    def pair_part():
        return push(part_ref.at[1 - core], sibp_ref, pair_send.at[2], pair_recv.at[2], sibling)

    pair_part().start()
    summary_half(core)
    pair_part().wait_recv()

    left = lax.broadcasted_iota(jnp.int32, (group, LANES), 1) < HEAD

    def spread(x, p, left):
        return jnp.where(left, x[:, 2 * p : 2 * p + 1], x[:, 2 * p + 1 : 2 * p + 2])

    a = part_ref.at[core]
    log_a = without_log(a[:, :, :, features:width].reshape(group, LANES))
    log_b = without_log(sibp_ref[:, :, :, features:width].reshape(group, LANES))
    peak = jnp.maximum(log_a, log_b)
    weight_a = jnp.exp(log_a - peak)
    weight_b = jnp.exp(log_b - peak)
    total = weight_a + weight_b
    weight_a, weight_b = weight_a / total, weight_b / total
    for p in range(PAIRS):
        lanes = slice(p * LANES, (p + 1) * LANES)
        mixed = a[:, :, :, lanes].reshape(group, LANES).astype(jnp.float32) * spread(
            weight_a, p, left
        ) + sibp_ref[:, :, :, lanes].reshape(group, LANES).astype(jnp.float32) * spread(
            weight_b, p, left
        )
        chipp_ref[:, :, :, lanes] = mixed.astype(jnp.bfloat16).reshape(2, half, share, LANES)
    chipp_ref[:, :, :, features:width] = with_log(peak + jnp.log(total), group).reshape(
        2, half, share, LANES
    )

    def across_p(k, slot):
        other, peer = peer_of(k)
        return push(
            chipp_ref.at[other % 2, other // 2],
            got_ref.at[slot],
            across_send.at[k],
            across_recv.at[slot],
            peer,
        )

    for k in range(1, chips):
        across_p(k, chip).start()
    got_ref[chip] = chipp_ref[odd, level]
    def sent(t, carry):
        for d in range(2):
            ring(d, t).wait_send()
            side(d, t, core).wait_send()
        return carry

    lax.fori_loop(0, steps, sent, 0)
    side_own(me).wait_send()
    pair_q().wait_send()
    pair_all(core).wait_send()
    pair_part().wait_send()

    @pl.when(holder)
    def _():
        end_q().wait_send()

    @pl.when(jnp.logical_and(at_end, jnp.logical_not(holder)))
    def _():
        end_out().wait_send()

    across_q().wait_send()
    spread_across(odd).wait_send()
    for k in range(1, half):
        along_q(k, level).wait_send()
        spread_along(k, level).wait_send()

    for k in range(1, chips):
        other, _ = peer_of(k)
        across_p(k, other).wait_recv()
    left = lax.broadcasted_iota(jnp.int32, (share, LANES), 1) < HEAD
    logs = [without_log(got_ref[k, :, features:width]) for k in range(chips)]
    peak = functools.reduce(jnp.maximum, logs)
    weights = [jnp.exp(log - peak) for log in logs]
    scale = 1.0 / functools.reduce(jnp.add, weights)
    weights = [w * scale for w in weights]
    for p in range(PAIRS):
        lanes = slice(p * LANES, (p + 1) * LANES)
        total = jnp.zeros((share, LANES), jnp.float32)
        for k in range(chips):
            total = total + got_ref[k, :, lanes].astype(jnp.float32) * spread(weights[k], p, left)
        summary_ref[:, lanes] = total.astype(jnp.bfloat16)
    store.wait()
    for k in range(1, chips):
        across_p(k, chip).wait_send()


def finish_kernel(attended_ref, summary_ref, attended_out, summary_out, held, small, sem):
    parts = held.shape[0]
    rows = held.shape[1]

    def moves(i, source, target, through):
        return (
            pltpu.make_async_copy(source, through, sem.at[0, i]),
            pltpu.make_async_copy(through, target, sem.at[1, i]),
        )

    copies = [moves(parts, summary_ref, summary_out, small)] + [
        moves(
            i,
            attended_ref.at[pl.ds(i * rows, rows)],
            attended_out.at[pl.ds(i * rows, rows)],
            held.at[i],
        )
        for i in range(parts)
    ]
    for fetch, _ in copies:
        fetch.start()
    for fetch, store in copies:
        fetch.wait()
        store.start()
    for _, store in copies:
        store.wait()


def fused(queries, inputs, w_kv, rand_blocks, w_cross, vocab_table, summary_ids):
    n = lax.axis_size("ctx")
    rows, features = inputs.shape
    blocks = rows // BLOCK
    chips = n // 2
    half = chips // 2
    steps = (half - 1) * blocks + blocks // 2
    share = summary_ids.shape[0] // n
    group = chips * share
    wide = features + LANES
    bf16, f32 = jnp.bfloat16, jnp.float32
    dma = pltpu.SemaphoreType.DMA
    results = pl.pallas_call(
        functools.partial(fused_kernel, n),
        out_shape=[
            jax.ShapeDtypeStruct(queries.shape, bf16),
            jax.ShapeDtypeStruct((share, features), bf16),
        ],
        in_specs=[SMEM, VMEM] + [ANY] * 5,
        out_specs=[ANY, VMEM],
        scratch_shapes=[
            pltpu.VMEM(queries.shape, bf16),
            pltpu.VMEM((n, blocks, BLOCK, features), bf16),
            pltpu.VMEM((n * blocks, BLOCK, 2 * features), bf16),
            pltpu.VMEM(w_kv.shape, bf16),
            pltpu.VMEM(queries.shape, bf16),
            pltpu.VMEM((max(rows, vocab_table.shape[0]), features), bf16),
            pltpu.VMEM((2, 2, half, share, features), bf16),
            pltpu.VMEM((2, half, share, features), bf16),
            pltpu.VMEM((2, half, share, features), bf16),
            pltpu.VMEM((half, share, features), bf16),
            pltpu.VMEM((half, share, features), bf16),
            pltpu.VMEM((half, share, features), bf16),
            pltpu.VMEM((share, features), bf16),
            pltpu.VMEM((2, 2, half, share, features), bf16),
            pltpu.VMEM((PAIRS // 2, 2 * BLOCK, LANES), f32),
            pltpu.VMEM((PAIRS // 2, 2 * BLOCK, LANES), f32),
            pltpu.VMEM((PAIRS // 2, 2 * BLOCK, LANES), f32),
            pltpu.VMEM((BLOCK, features), bf16),
            pltpu.VMEM((BLOCK, features // 2), bf16),
            pltpu.VMEM((BLOCK, features // 2), bf16),
            pltpu.VMEM((rows, features), f32),
            pltpu.VMEM((blocks, PAIRS, 2 * BLOCK, LANES), f32),
            pltpu.VMEM((2, 2, half, share, wide), bf16),
            pltpu.VMEM((2, half, share, wide), bf16),
            pltpu.VMEM((2, half, share, wide), bf16),
            pltpu.VMEM((chips, share, wide), bf16),
            dma((2, steps)),
            dma((2, steps)),
            dma((2, steps)),
            dma((2, steps)),
            dma((2, half)),
            dma((2, half)),
            dma,
            dma,
            dma((7,)),
            dma((7,)),
            dma((chips,)),
            dma((chips,)),
            dma((7,)),
        ],
        compiler_params=pltpu.CompilerParams(
            collective_id=4, has_side_effects=True, vmem_limit_bytes=FUSED_LIMIT
        ),
        name="fused",
    )(
        rand_blocks.T,
        summary_ids.reshape(1, -1),
        inputs.reshape(blocks, BLOCK, features),
        queries,
        w_kv,
        w_cross,
        vocab_table,
    )
    return pl.pallas_call(
        finish_kernel,
        out_shape=[jax.ShapeDtypeStruct(r.shape, r.dtype) for r in results],
        in_specs=[ANY] * 2,
        out_specs=[ANY] * 2,
        scratch_shapes=[
            pltpu.VMEM((3, rows // 3, features), bf16),
            pltpu.VMEM((share, features), bf16),
            dma((2, 4)),
        ],
        name="finish",
    )(*results)


def local(queries, inputs, w_kv, rand_blocks, w_cross, vocab_table, summary_ids):
    n = lax.axis_size("ctx")
    held = 3 * n * inputs.size * 2
    path = fused if held <= HELD_LIMIT else staged
    return path(queries, inputs, w_kv, rand_blocks, w_cross, vocab_table, summary_ids)


def solution(mesh):
    return jax.shard_map(
        local,
        mesh=mesh,
        in_specs=(
            P(("groups", "ctx"), None),
            P(("groups", "ctx"), None),
            P(),
            P("groups", None),
            P(),
            P("ctx", None),
            P("groups"),
        ),
        out_specs=(P(("groups", "ctx"), None), P(("groups", "ctx"), None)),
        check_vma=False,
    )
```

```python
import functools

import jax
import jax.numpy as jnp
from jax import lax
from jax.experimental import pallas as pl
from jax.experimental.pallas import tpu as pltpu
from jax.sharding import PartitionSpec as P

HEADS = 16
HEAD = 64
BLOCK = 64
LANES = 128
PAIRS = HEADS // 2
MASKED_SCORE = -1e30
MESH = pl.DeviceIdType.MESH
VMEM = pl.BlockSpec(memory_space=pltpu.VMEM)
ANY = pl.BlockSpec(memory_space=pl.ANY)
SMEM = pl.BlockSpec(memory_space=pltpu.SMEM)
VMEM_LIMIT = 48 * 1024 * 1024
FUSED_LIMIT = 60 * 1024 * 1024
HELD_LIMIT = 40 * 1024 * 1024


def greet_all(me, n):
    barrier = pltpu.get_barrier_semaphore()

    def greet(k, carry):
        peer = lax.rem(me + k, n)
        pl.semaphore_signal(barrier, inc=1, device_id={"ctx": peer}, device_id_type=MESH)
        return carry

    lax.fori_loop(1, n, greet, 0)
    pl.semaphore_wait(barrier, n - 1)


def push(source, target, send_sem, recv_sem, peer):
    return pltpu.make_async_remote_copy(
        source, target, send_sem, recv_sem, device_id={"ctx": peer}, device_id_type=MESH
    )


def each_peer(me, n, body):
    def step(k, carry):
        body(lax.rem(me + k, n))
        return carry

    lax.fori_loop(1, n, step, 0)


def gather_kernel(
    n,
    x_ref,
    q_ref,
    looked_ref,
    all_ref,
    ends_ref,
    got_ref,
    ring_send,
    ring_recv,
    side_send,
    side_recv,
    got_send,
    got_recv,
    ends_send,
    ends_recv,
    own_sem,
):
    me = lax.axis_index("ctx")
    chips = n // 2
    half = chips // 2
    core = me % 2
    chip = me // 2
    odd = chip % 2
    place = (1 - odd) * (chip // 2) + odd * (chips - 1 - chip // 2)
    sibling = me + 1 - 2 * core
    row_count = q_ref.shape[0]

    def device(at, on_core):
        at = (at + chips) % chips
        back = at // half
        return 2 * ((1 - back) * 2 * at + back * (2 * (chips - 1 - at) + 1)) + on_core

    streams = [(d, h) for h in range(2) for d in range(2)]

    def hops(d, h):
        return half if d == h else half - 1

    def ring(d, h, s):
        sign = 1 - 2 * d
        owner = device(place - sign * s, core)
        source = x_ref.at[h] if s == 0 else all_ref.at[owner, h]
        return push(
            source,
            all_ref.at[owner, h],
            ring_send.at[d, h, s],
            ring_recv.at[d, h, s],
            device(place + sign, core),
        )

    def arrival(d, h, s):
        owner = device(place - (1 - 2 * d) * (s + 1), core)
        landed = all_ref.at[owner, h]
        return push(landed, landed, ring_send.at[d, h, s], ring_recv.at[d, h, s], sibling)

    def side(d, h, s, on_core):
        owner = device(place - (1 - 2 * d) * s, on_core)
        source = all_ref.at[owner, h]
        if s == 0:
            source = x_ref.at[h]
        return push(
            source, all_ref.at[owner, h], side_send.at[d, h, s], side_recv.at[d, h, s], sibling
        )

    own = [pltpu.make_async_copy(x_ref.at[h], all_ref.at[me, h], own_sem.at[h]) for h in range(2)]
    own.append(pltpu.make_async_copy(looked_ref.at[me], got_ref.at[me], own_sem.at[2]))
    greet_all(me, n)
    for d, h in streams:
        ring(d, h, 0).start()

    def send_looked(peer):
        push(
            looked_ref.at[peer], got_ref.at[me], got_send.at[peer], got_recv.at[me], peer
        ).start()

    each_peer(me, n, send_looked)
    ends = [q_ref.at[pl.ds(0, BLOCK)], q_ref.at[pl.ds(row_count - BLOCK, BLOCK)]]
    holders = [0, n - 1]

    steps = [(place - at + chips) % chips for at in (0, half)]
    right, left = device(place + 1, core), device(place - 1, core)

    def send_end(e, k, source):
        peer = (right, left, sibling)[k]
        return push(source, ends_ref.at[e], ends_send.at[e, k], ends_recv.at[e], peer)

    def routes(e):
        away = steps[e]
        return [
            (0, away < half),
            (1, jnp.logical_or(away == 0, away > chips - half + 1)),
            (2, me == holders[e]),
        ]

    def start_routes(e, source):
        for k, goes in routes(e)[:2]:

            @pl.when(goes)
            def _():
                send_end(e, k, source).start()

    def pass_end(e):
        send_end(e, 0, ends_ref.at[e]).wait_recv()
        start_routes(e, ends_ref.at[e])

    for e in range(2):

        @pl.when(me == holders[e])
        def _():
            send_end(e, 2, ends[e]).start()
            start_routes(e, ends[e])
            copy = pltpu.make_async_copy(ends[e], ends_ref.at[e], own_sem.at[3])
            copy.start()
            copy.wait()

        @pl.when(jnp.logical_and(steps[e] == 0, me != holders[e]))
        def _():
            pass_end(e)

    for copy in own:
        copy.start()
    for h in range(2):
        side(0, h, 0, core).start()
    for s in range(half):
        for d, h in streams:
            if s < hops(d, h):
                arrival(d, h, s).wait_recv()
                if s + 1 < hops(d, h):
                    ring(d, h, s + 1).start()
                side(d, h, s + 1, core).start()
        for e in range(2):
            near = steps[e] == s + 1
            if s + 1 < half:
                near = jnp.logical_or(near, steps[e] == chips - s - 1)

            @pl.when(near)
            def _():
                pass_end(e)

    for h in range(2):
        side(0, h, 0, core).wait_send()
        side(0, h, 0, 1 - core).wait_recv()
    for s in range(half):
        for d, h in streams:
            if s < hops(d, h):
                ring(d, h, s).wait_send()
                side(d, h, s + 1, core).wait_send()
                side(d, h, s + 1, 1 - core).wait_recv()

    def end_looked(peer):
        copy = push(
            looked_ref.at[peer], got_ref.at[peer], got_send.at[peer], got_recv.at[peer], peer
        )
        copy.wait_recv()
        copy.wait_send()

    each_peer(me, n, end_looked)
    for e in range(2):
        for k, goes in routes(e):

            @pl.when(goes)
            def _():
                send_end(e, k, ends[e]).wait_send()

    for copy in own:
        copy.wait()


def gather_inputs(x, q, looked):
    n = lax.axis_size("ctx")
    rows, features = x.shape
    half = n // 4
    dma = pltpu.SemaphoreType.DMA
    gathered, ends, got = pl.pallas_call(
        functools.partial(gather_kernel, n),
        out_shape=[
            jax.ShapeDtypeStruct((n, 2, rows // 2, features), x.dtype),
            jax.ShapeDtypeStruct((2, BLOCK, features), q.dtype),
            jax.ShapeDtypeStruct(looked.shape, looked.dtype),
        ],
        in_specs=[ANY] * 3,
        out_specs=[ANY] * 3,
        scratch_shapes=[
            dma((2, 2, half)),
            dma((2, 2, half)),
            dma((2, 2, half + 1)),
            dma((2, 2, half + 1)),
            dma((n,)),
            dma((n,)),
            dma((2, 3)),
            dma((2,)),
            dma((4,)),
        ],
        compiler_params=pltpu.CompilerParams(collective_id=1, has_side_effects=True),
        name="gather_inputs",
    )(x.reshape(2, rows // 2, features), q, looked)
    return gathered.reshape(n * rows // BLOCK, BLOCK, features), ends, got


def ends_kernel(
    n,
    mine_ref,
    out_ref,
    log_ref,
    rows_ref,
    outs_ref,
    logs_ref,
    rows_send,
    rows_recv,
    ends_send,
    ends_recv,
    own_sem,
):
    me = lax.axis_index("ctx")
    holders = [0, n - 1]
    pairs = [(out_ref, outs_ref), (log_ref, logs_ref)]

    def end(e, i, slot):
        source, target = pairs[i]
        return push(
            source.at[e], target.at[slot], ends_send.at[e, i], ends_recv.at[i, slot], holders[e]
        )

    own = pltpu.make_async_copy(mine_ref, rows_ref.at[me], own_sem.at[2])
    own.start()
    greet_all(me, n)
    for e in range(2):

        @pl.when(me != holders[e])
        def _():
            for i in range(2):
                end(e, i, me).start()

        @pl.when(me == holders[e])
        def _():
            for i in range(2):
                source, target = pairs[i]
                copy = pltpu.make_async_copy(source.at[e], target.at[me], own_sem.at[i])
                copy.start()
                copy.wait()

    def send_rows(peer):
        push(mine_ref, rows_ref.at[me], rows_send.at[peer], rows_recv.at[me], peer).start()

    each_peer(me, n, send_rows)

    def end_rows(peer):
        copy = push(mine_ref, rows_ref.at[peer], rows_send.at[peer], rows_recv.at[peer], peer)
        copy.wait_recv()
        copy.wait_send()

    each_peer(me, n, end_rows)
    for e in range(2):

        @pl.when(me != holders[e])
        def _():
            for i in range(2):
                end(e, i, me).wait_send()

        @pl.when(me == holders[e])
        def _():
            def arrived(peer):
                for i in range(2):
                    source, target = pairs[i]
                    push(
                        source.at[e],
                        target.at[peer],
                        ends_send.at[e, i],
                        ends_recv.at[i, peer],
                        peer,
                    ).wait_recv()

            each_peer(me, n, arrived)

    own.wait()


def send_ends(mine, out, log):
    n = lax.axis_size("ctx")
    dma = pltpu.SemaphoreType.DMA
    out = out.reshape(2, BLOCK, out.shape[1])
    log = log.reshape(2, BLOCK, LANES)
    return pl.pallas_call(
        functools.partial(ends_kernel, n),
        out_shape=[
            jax.ShapeDtypeStruct((n,) + mine.shape, mine.dtype),
            jax.ShapeDtypeStruct((n,) + out.shape[1:], out.dtype),
            jax.ShapeDtypeStruct((n,) + log.shape[1:], log.dtype),
        ],
        in_specs=[ANY] * 3,
        out_specs=[ANY] * 3,
        scratch_shapes=[dma((n,)), dma((n,)), dma((2, 2)), dma((2, n)), dma((3,))],
        compiler_params=pltpu.CompilerParams(collective_id=2, has_side_effects=True),
        name="send_ends",
    )(mine, out, log)


def combine(outs_ref, logs_ref, total_ref):
    n, rows, features = outs_ref.shape
    peak = lax.fori_loop(
        1, n, lambda i, peak: jnp.maximum(peak, logs_ref[i]), logs_ref[0]
    )
    left = lax.broadcasted_iota(jnp.int32, (rows, LANES), 1) < HEAD
    total_ref[...] = jnp.zeros_like(total_ref)

    def spread(x, p):
        return jnp.where(left, x[:, 2 * p : 2 * p + 1], x[:, 2 * p + 1 : 2 * p + 2])

    def add(i, total):
        weights = jnp.exp(logs_ref[i] - peak)
        for p in range(PAIRS):
            lanes = slice(p * LANES, (p + 1) * LANES)
            total_ref[:, lanes] += outs_ref[i, :, lanes].astype(jnp.float32) * spread(weights, p)
        return total + weights

    scale = 1.0 / lax.fori_loop(0, n, add, jnp.zeros((rows, LANES), jnp.float32))
    for p in range(PAIRS):
        lanes = slice(p * LANES, (p + 1) * LANES)
        total_ref[:, lanes] = total_ref[:, lanes] * spread(scale, p)


def summary_kernel(
    n,
    part_ref,
    log_ref,
    out_ref,
    outs_ref,
    logs_ref,
    total_ref,
    send_sem,
    recv_sem,
    own_sem,
):
    me = lax.axis_index("ctx")
    pairs = [(part_ref, outs_ref), (log_ref, logs_ref)]
    own = [
        pltpu.make_async_copy(source.at[me], target.at[me], own_sem.at[i])
        for i, (source, target) in enumerate(pairs)
    ]
    for copy in own:
        copy.start()
    greet_all(me, n)

    def copies(peer, slot):
        return [
            push(
                source.at[peer], target.at[slot], send_sem.at[i, peer], recv_sem.at[i, slot], peer
            )
            for i, (source, target) in enumerate(pairs)
        ]

    def send(peer):
        for copy in copies(peer, me):
            copy.start()

    each_peer(me, n, send)

    def finish(peer):
        for copy in copies(peer, peer):
            copy.wait_recv()
            copy.wait_send()

    each_peer(me, n, finish)
    for copy in own:
        copy.wait()
    combine(outs_ref, logs_ref, total_ref)
    out_ref[...] = total_ref[...].astype(out_ref.dtype)


def combined_summary(part, logs):
    n, share, features = part.shape
    dma = pltpu.SemaphoreType.DMA
    return pl.pallas_call(
        functools.partial(summary_kernel, n),
        out_shape=jax.ShapeDtypeStruct((share, features), jnp.bfloat16),
        in_specs=[ANY] * 2,
        out_specs=VMEM,
        scratch_shapes=[
            pltpu.VMEM(part.shape, part.dtype),
            pltpu.VMEM(logs.shape, logs.dtype),
            pltpu.VMEM((share, features), jnp.float32),
            dma((2, n)),
            dma((2, n)),
            dma((2,)),
        ],
        compiler_params=pltpu.CompilerParams(collective_id=3, has_side_effects=True),
        name="combined_summary",
    )(part, logs)


def dot_t(a, b):
    return lax.dot_general(a, b, (((1,), (1,)), ((), ())), preferred_element_type=jnp.float32)


def stacked_pair(q):
    q = q * jnp.asarray(HEAD**-0.5, q.dtype)
    left = lax.broadcasted_iota(jnp.int32, q.shape, 1) < HEAD
    zero = jnp.zeros_like(q)
    return jnp.concatenate([jnp.where(left, q, zero), jnp.where(left, zero, q)], axis=0)


def unstacked_pair(o):
    rows = o.shape[0] // 2
    left = lax.broadcasted_iota(jnp.int32, (rows, LANES), 1) < HEAD
    return jnp.where(left, o[:rows], o[rows:])


def project(x_ref, w_ref, out_ref, tile):
    rows, cols = out_ref.shape
    width = 512

    def step(t, carry):
        at = pl.ds(pl.multiple_of(t * tile, tile), tile)
        x = x_ref[at, :]
        for c in range(cols // width):
            y = jnp.dot(
                x, w_ref[:, c * width : (c + 1) * width], preferred_element_type=jnp.float32
            )
            out_ref[at, c * width : (c + 1) * width] = y.astype(out_ref.dtype)
        return carry

    lax.fori_loop(0, rows // tile, step, 0)


def partial_attention(q_ref, kv_ref, out_ref, log_ref):
    rows, features = q_ref.shape
    place = lax.broadcasted_iota(jnp.int32, (rows, LANES), 1)
    logs = jnp.zeros((rows, LANES), jnp.float32)
    for p in range(PAIRS):
        lanes = slice(p * LANES, (p + 1) * LANES)
        values = slice(features + p * LANES, features + (p + 1) * LANES)
        scores = dot_t(stacked_pair(q_ref[:, lanes]), kv_ref[:, lanes])
        peak = jnp.max(scores, axis=1, keepdims=True)
        weights = jnp.exp(scores - peak)
        totals = jnp.sum(weights, axis=1, keepdims=True)
        sums = jnp.dot(
            weights.astype(jnp.bfloat16), kv_ref[:, values], preferred_element_type=jnp.float32
        )
        out_ref[:, lanes] = unstacked_pair(sums / totals).astype(out_ref.dtype)
        log = peak + jnp.log(totals)
        logs = jnp.where(place == 2 * p, log[:rows], logs)
        logs = jnp.where(place == 2 * p + 1, log[rows:], logs)
    log_ref[...] = logs


def global_kernel(q_ref, x_ref, w_ref, out_ref, log_ref, kv_ref):
    project(x_ref, w_ref, kv_ref, 128)
    partial_attention(q_ref, kv_ref, out_ref, log_ref)


def global_partial(q, x, w):
    return pl.pallas_call(
        global_kernel,
        out_shape=[
            jax.ShapeDtypeStruct(q.shape, jnp.bfloat16),
            jax.ShapeDtypeStruct((q.shape[0], LANES), jnp.float32),
        ],
        in_specs=[VMEM] * 3,
        out_specs=[VMEM] * 2,
        scratch_shapes=[pltpu.VMEM((x.shape[0], w.shape[1]), jnp.bfloat16)],
        compiler_params=pltpu.CompilerParams(vmem_limit_bytes=VMEM_LIMIT),
        cost_estimate=pl.CostEstimate(
            flops=2 * x.size * w.shape[1], bytes_accessed=6 << 20, transcendentals=1 << 20
        ),
        name="global_partial",
    )(q, x, w)


def block_kernel(
    pick_count,
    ids_ref,
    edge_ref,
    all_ref,
    q_ref,
    x_ref,
    w_kv_ref,
    w_cross_ref,
    outs_ref,
    logs_ref,
    sq_ref,
    attended_ref,
    out_ref,
    log_ref,
    rows_ref,
    kv_ref,
    total_ref,
    sem,
):
    row_count, features = x_ref.shape
    block_count = row_count // BLOCK
    slots = rows_ref.shape[0] // BLOCK
    far_start = (block_count + 4) * BLOCK
    span = (5 + pick_count) * BLOCK

    def fetch(i):
        return pltpu.make_async_copy(
            all_ref.at[ids_ref[i]],
            rows_ref.at[pl.ds(pl.multiple_of(i * BLOCK, BLOCK), BLOCK)],
            sem.at[i],
        )

    for i in range(slots):
        fetch(i).start()
    for i in range(slots):
        fetch(i).wait()
    project(rows_ref, w_kv_ref, kv_ref, 2 * BLOCK)

    column = lax.broadcasted_iota(jnp.int32, (2 * BLOCK, span), 1)

    def one_block(b, carry):
        first = edge_ref[0] + b
        hidden = jnp.logical_or(
            jnp.logical_and(column < BLOCK, first < 2),
            jnp.logical_and(
                jnp.logical_and(column >= 2 * BLOCK, column < 3 * BLOCK), first > edge_ref[1] - 3
            ),
        )
        near = pl.ds(pl.multiple_of(b * BLOCK, BLOCK), 3 * BLOCK)
        ends = pl.ds((block_count + 2) * BLOCK, 2 * BLOCK)
        far = pl.ds(
            pl.multiple_of(far_start + b * pick_count * BLOCK, BLOCK), pick_count * BLOCK
        )
        here = pl.ds(pl.multiple_of(b * BLOCK, BLOCK), BLOCK)
        for p in range(PAIRS):
            lanes = slice(p * LANES, (p + 1) * LANES)
            values = slice(features + p * LANES, features + (p + 1) * LANES)
            k = jnp.concatenate(
                [kv_ref[near, lanes], kv_ref[ends, lanes], kv_ref[far, lanes]], axis=0
            )
            v = jnp.concatenate(
                [kv_ref[near, values], kv_ref[ends, values], kv_ref[far, values]], axis=0
            )
            scores = dot_t(stacked_pair(q_ref[here, lanes]), k)
            scores = jnp.where(hidden, MASKED_SCORE, scores)
            weights = jnp.exp(scores - jnp.max(scores, axis=1, keepdims=True))
            totals = jnp.sum(weights, axis=1, keepdims=True)
            probs = (weights * (1.0 / totals)).astype(jnp.bfloat16)
            o = jnp.dot(probs, v, preferred_element_type=jnp.float32)
            attended_ref[here, lanes] = unstacked_pair(o).astype(jnp.bfloat16)
        return carry

    lax.fori_loop(0, block_count, one_block, 0)

    def place(rows):
        combine(outs_ref, logs_ref, total_ref)
        attended_ref[rows] = total_ref[...].astype(jnp.bfloat16)

    @pl.when(edge_ref[0] == 0)
    def _():
        place(slice(0, BLOCK))

    @pl.when(edge_ref[0] + block_count == edge_ref[1])
    def _():
        place(slice(row_count - BLOCK, row_count))

    encoded = x_ref[...].astype(jnp.float32) + attended_ref[...].astype(jnp.float32)
    rows_ref[:row_count] = encoded.astype(jnp.bfloat16)
    project(rows_ref.at[:row_count], w_cross_ref, kv_ref.at[:row_count], 2 * BLOCK)
    partial_attention(sq_ref, kv_ref.at[:row_count], out_ref, log_ref)


def block_attention(ids, edge, everything, q, x, w_kv, w_cross, outs, end_logs, sq, pick_count):
    slots = ids.shape[0]
    features = x.shape[1]
    return pl.pallas_call(
        functools.partial(block_kernel, pick_count),
        out_shape=[
            jax.ShapeDtypeStruct(q.shape, jnp.bfloat16),
            jax.ShapeDtypeStruct(sq.shape, jnp.bfloat16),
            jax.ShapeDtypeStruct((sq.shape[0], LANES), jnp.float32),
        ],
        in_specs=[SMEM, SMEM, ANY] + [VMEM] * 7,
        out_specs=[VMEM] * 3,
        scratch_shapes=[
            pltpu.VMEM((slots * BLOCK, features), jnp.bfloat16),
            pltpu.VMEM((slots * BLOCK, 2 * features), jnp.bfloat16),
            pltpu.VMEM((BLOCK, features), jnp.float32),
            pltpu.SemaphoreType.DMA((slots,)),
        ],
        compiler_params=pltpu.CompilerParams(vmem_limit_bytes=VMEM_LIMIT),
        cost_estimate=pl.CostEstimate(
            flops=20 << 30, bytes_accessed=16 << 20, transcendentals=5 << 20
        ),
        name="block_attention",
    )(ids, edge, everything, q, x, w_kv, w_cross, outs, end_logs, sq)


def staged(queries, inputs, w_kv, rand_blocks, w_cross, vocab_table, summary_ids):
    n = lax.axis_size("ctx")
    position = lax.axis_index("ctx")
    row_count, features = inputs.shape
    block_count = row_count // BLOCK
    pick_count = rand_blocks.shape[1]
    total_blocks = block_count * n
    shard_rows = vocab_table.shape[0]
    summary_count = summary_ids.shape[0]
    share = summary_count // n
    offsets = summary_ids - position * shard_rows
    inside = jnp.logical_and(offsets >= 0, offsets < shard_rows)
    looked = vocab_table[jnp.clip(offsets, 0, shard_rows - 1)]
    looked = jnp.where(inside[:, None], looked, jnp.zeros((), looked.dtype))
    everything, end_queries, got = gather_inputs(
        inputs, queries, looked.reshape(n, share, features)
    )
    mine = jnp.sum(got.astype(jnp.float32), axis=0).astype(jnp.bfloat16)
    end_out, end_log = global_partial(end_queries.reshape(2 * BLOCK, features), inputs, w_kv)
    rows, outs, end_logs = send_ends(mine, end_out, end_log)
    summary_queries = rows.reshape(summary_count, features)

    start = position * block_count
    near = jnp.clip(start - 1 + jnp.arange(block_count + 2, dtype=jnp.int32), 0, total_blocks - 1)
    fixed = jnp.array([0, total_blocks - 1], jnp.int32)
    picks = lax.dynamic_slice_in_dim(rand_blocks, start, block_count, 0).reshape(-1)
    ids = jnp.concatenate([near, fixed, picks.astype(jnp.int32)])
    edge = jnp.stack([start, jnp.full_like(start, total_blocks)]).astype(jnp.int32)
    attended, part, logs = block_attention(
        ids,
        edge,
        everything,
        queries,
        inputs,
        w_kv,
        w_cross,
        outs,
        end_logs,
        summary_queries,
        pick_count,
    )
    summary = combined_summary(
        part.reshape(n, share, features), logs.reshape(n, share, LANES)
    )
    return attended, summary


def ring_order(half, blocks, d):
    ends_first = [j // 2 if j % 2 == 0 else blocks - 1 - j // 2 for j in range(blocks)]
    group = blocks // 2
    order = []
    for g in range(2):
        members = range(g * group, (g + 1) * group)
        last = [i for i in members if i % 2 == d]
        rest = [i for i in members if i % 2 != d]
        for hop in range(half):
            order += [(hop, ends_first[i]) for i in (last if hop == half - 1 else last + rest)]
    return order


def look_up(values, t):
    found = values[0]
    for j in range(1, len(values)):
        if values[j] != values[j - 1]:
            found = jnp.where(t >= j, values[j], found)
    return found


def dots(x, w_ref, store):
    width = 512
    for c in range(w_ref.shape[1] // width):
        cols = slice(c * width, (c + 1) * width)
        y = jnp.dot(x, w_ref[:, cols], preferred_element_type=jnp.float32)
        store(cols, y.astype(jnp.bfloat16))


def lanes_of(p):
    return slice(p * LANES, (p + 1) * LANES)


def row_max(x):
    return jnp.max(x, axis=1, keepdims=True)


def row_sum(x):
    return jnp.sum(x, axis=1, keepdims=True)


def weighted(weights, v):
    return jnp.dot(weights.astype(jnp.bfloat16), v, preferred_element_type=jnp.float32)


def with_log(log, rows):
    place = lax.broadcasted_iota(jnp.int32, (rows, LANES), 1)
    high = log.astype(jnp.bfloat16)
    rest = log - high.astype(jnp.float32)
    middle = rest.astype(jnp.bfloat16)
    low = (rest - middle.astype(jnp.float32)).astype(jnp.bfloat16)
    low, middle = low.astype(jnp.float32), middle.astype(jnp.float32)
    packed = jnp.where(place < HEADS, high.astype(jnp.float32), 0.0)
    packed = jnp.where(place // HEADS == 1, pltpu.roll(middle, HEADS, 1), packed)
    packed = jnp.where(place // HEADS == 2, pltpu.roll(low, 2 * HEADS, 1), packed)
    return packed.astype(jnp.bfloat16)


def without_log(packed):
    packed = packed.astype(jnp.float32)
    middle = pltpu.roll(packed, LANES - HEADS, 1)
    low = pltpu.roll(packed, LANES - 2 * HEADS, 1)
    return packed + (middle + low)


def fused_kernel(
    n,
    picks_ref,
    sids_ref,
    x_ref,
    q_hbm,
    w_kv_hbm,
    w_cross_hbm,
    vocab_hbm,
    attended_hbm,
    summary_ref,
    attended_ref,
    x_all,
    kv_all,
    w_kv_ref,
    q_ref,
    shared_ref,
    looked_ref,
    sibq_ref,
    chipq_ref,
    sideq_ref,
    lineq_ref,
    partq_ref,
    mine_ref,
    sumq_ref,
    acc_ref,
    peak_ref,
    sum_ref,
    end_q_ref,
    end_out_ref,
    end_half_ref,
    near_ref,
    near_log_ref,
    part_ref,
    sibp_ref,
    chipp_ref,
    got_ref,
    ring_send,
    ring_recv,
    side_send,
    side_recv,
    along_send,
    along_recv,
    own_send,
    own_recv,
    pair_send,
    pair_recv,
    across_send,
    across_recv,
    local_sem,
):
    me = lax.axis_index("ctx")
    chips = n // 2
    half = chips // 2
    core = me % 2
    chip = me // 2
    odd = chip % 2
    place = (1 - odd) * (chip // 2) + odd * (chips - 1 - chip // 2)
    sibling = me + 1 - 2 * core
    blocks = x_ref.shape[0]
    features = x_ref.shape[2]
    rows = blocks * BLOCK
    share = summary_ref.shape[0]
    steps = (half - 1) * blocks + blocks // 2
    total_blocks = n * blocks
    holder = jnp.logical_or(me == 0, me == n - 1)
    at_end = jnp.logical_or(chip == 0, chip == chips - 1)
    orders = [ring_order(half, blocks, d) for d in range(2)]
    ahead = blocks // 2

    def device(at, on_core):
        at = (at + chips) % chips
        back = at // half
        return 2 * ((1 - back) * 2 * at + back * (2 * (chips - 1 - at) + 1)) + on_core

    def block_of(d, t):
        if isinstance(t, int):
            return orders[d][t][1]
        return look_up([block for _, block in orders[d]], t)

    def hop_of(d, t):
        if isinstance(t, int):
            return orders[d][t][0]
        return look_up([hop for hop, _ in orders[d]], t)

    def ring(d, t):
        held = x_all.at[device(place - (1 - 2 * d) * hop_of(d, t), core), block_of(d, t)]
        return push(
            held, held, ring_send.at[d, t], ring_recv.at[d, t], device(place + 1 - 2 * d, core)
        )

    def ring_own(d, t):
        return push(
            x_ref.at[block_of(d, t)],
            x_all.at[me, block_of(d, t)],
            ring_send.at[d, t],
            ring_recv.at[d, t],
            device(place + 1 - 2 * d, core),
        )

    def owner_of(d, t, on_core):
        return device(place - (1 - 2 * d) * (hop_of(d, t) + 1), on_core)

    def arrival(d, t):
        landed = x_all.at[owner_of(d, t, core), block_of(d, t)]
        return push(landed, landed, ring_send.at[d, t], ring_recv.at[d, t], sibling)

    def side(d, t, on_core):
        landed = x_all.at[owner_of(d, t, on_core), block_of(d, t)]
        return push(landed, landed, side_send.at[d, t], side_recv.at[d, t], sibling)

    def side_own(on):
        return push(x_ref, x_all.at[on], own_send, own_recv, sibling)

    def peer_of(k):
        other = lax.rem(chip + k, chips)
        return other, 2 * other + core

    shard_rows = vocab_hbm.shape[0]
    vocab_ref = shared_ref.at[:shard_rows]
    encoded_ref = shared_ref.at[:rows]
    cross_ref = kv_all.at[:blocks]
    loads = [
        pltpu.make_async_copy(source, target, local_sem.at[i])
        for i, (source, target) in enumerate(
            [
                (vocab_hbm, vocab_ref),
                (w_kv_hbm, w_kv_ref),
                (x_ref, x_all.at[me]),
                (q_hbm, q_ref),
            ]
        )
    ]
    for load in loads:
        load.start()

    barrier = pltpu.get_barrier_semaphore()
    pl.semaphore_signal(barrier, inc=1, device_id={"ctx": sibling}, device_id_type=MESH)
    for k in range(1, chips):
        pl.semaphore_signal(
            barrier, inc=1, device_id={"ctx": peer_of(k)[1]}, device_id_type=MESH
        )
    pl.semaphore_wait(barrier, chips)

    for t in range(ahead):
        for d in range(2):
            ring_own(d, t).start()
    end_row = pl.multiple_of(jnp.where(chip == 0, 0, rows - BLOCK), BLOCK)

    def end_q():
        return push(
            q_hbm.at[pl.ds(end_row, BLOCK)], end_q_ref, pair_send.at[3], pair_recv.at[3], sibling
        )

    def end_out():
        return push(end_out_ref, end_half_ref, pair_send.at[4], pair_recv.at[4], sibling)

    @pl.when(holder)
    def _():
        end_q().start()
        copy = pltpu.make_async_copy(
            q_hbm.at[pl.ds(end_row, BLOCK)], end_q_ref, local_sem.at[5]
        )
        copy.start()
        copy.wait()

    side_own(me).start()

    loads[0].wait()
    summary_count = sids_ref.shape[1]
    offsets = sids_ref[...] - me * shard_rows
    hot = lax.broadcasted_iota(jnp.int32, (shard_rows, summary_count), 0) == offsets
    hot = jnp.where(hot, 1.0, 0.0).astype(jnp.bfloat16)
    looked = lax.dot_general(
        hot, vocab_ref[...], (((0,), (0,)), ((), ())), preferred_element_type=jnp.float32
    ).astype(jnp.bfloat16)
    for k in range(chips):
        for c in range(2):
            at = (2 * k + c) * share
            looked_ref[c, k % 2, k // 2] = looked[at : at + share]

    def pair_q():
        return push(
            looked_ref.at[1 - core], sibq_ref, pair_send.at[0], pair_recv.at[0], sibling
        )

    pair_q().start()
    loads[1].wait()
    loads[2].wait()

    def project_owner(owner):
        def step(t, carry):
            x = x_all[owner, pl.ds(2 * t, 2)].reshape(2 * BLOCK, features)

            def store(cols, y):
                kv_all[pl.ds(owner * blocks + 2 * t, 2), :, cols] = y.reshape(2, BLOCK, -1)

            dots(x, w_kv_ref, store)
            return carry

        lax.fori_loop(0, blocks // 2, step, 0)

    project_owner(me)
    pair_q().wait_recv()
    chipq_ref[...] = looked_ref[core] + sibq_ref[...]

    column = 2 * (chip + 1 - 2 * odd) + core
    level = chip // 2

    def level_of(k):
        other = lax.rem(level + k, half)
        return other, 2 * (2 * other + odd) + core

    def across_q():
        return push(chipq_ref.at[1 - odd], sideq_ref, pair_send.at[5], pair_recv.at[5], column)

    across_q().start()

    def along_q(k, slot):
        other, peer = level_of(k)
        return push(
            lineq_ref.at[other], partq_ref.at[slot], along_send.at[0, k], along_recv.at[0, slot], peer
        )

    def add_across():
        across_q().wait_recv()
        lineq_ref[...] = chipq_ref[odd] + sideq_ref[...]
        for k in range(1, half):
            along_q(k, level).start()
        partq_ref[level] = lineq_ref[level]

    def spread_along(k, slot):
        _, peer = level_of(k)
        return push(
            mine_ref,
            sumq_ref.at[core, odd, slot],
            along_send.at[1, k],
            along_recv.at[1, slot],
            peer,
        )

    def add_along():
        for k in range(1, half):
            along_q(k, level_of(k)[0]).wait_recv()
        mine = partq_ref[0].astype(jnp.float32)
        for k in range(1, half):
            mine = mine + partq_ref[k].astype(jnp.float32)
        mine_ref[...] = mine.astype(jnp.bfloat16)
        for k in range(1, half):
            spread_along(k, level).start()
        sumq_ref[core, odd, level] = mine_ref[...]

    def spread_across(x):
        held = sumq_ref.at[core, x]
        return push(held, held, pair_send.at[6], pair_recv.at[6], column)

    side_own(sibling).wait_recv()
    project_owner(sibling)

    loads[3].wait()
    half_pairs = PAIRS // 2

    def half_lanes(p):
        return pl.multiple_of((core * half_pairs + p) * LANES, LANES)

    def take_keys(parts):
        every = range(half_pairs)
        scores = []
        for p in every:
            lanes = pl.ds(half_lanes(p), LANES)
            k = jnp.concatenate([kv_all[at, :, lanes] for at in parts], axis=0)
            scores.append(dot_t(stacked_pair(end_q_ref[:, lanes]), k.reshape(-1, LANES)))
        before = [peak_ref[p] for p in every]
        peaks = [jnp.maximum(before[p], row_max(scores[p])) for p in every]
        weights = [jnp.exp(scores[p] - peaks[p][:, :1]) for p in every]
        fades = [jnp.exp(before[p] - peaks[p]) for p in every]
        totals = [row_sum(weights[p]) for p in every]
        sums = []
        for p in every:
            values = pl.ds(features + half_lanes(p), LANES)
            v = jnp.concatenate([kv_all[at, :, values] for at in parts], axis=0)
            sums.append(weighted(weights[p], v.reshape(-1, LANES)))
        for p in every:
            peak_ref[p] = peaks[p]
            sum_ref[p] = sum_ref[p] * fades[p] + totals[p]
            acc_ref[p] = acc_ref[p] * fades[p] + sums[p]

    @pl.when(jnp.logical_and(at_end, jnp.logical_not(holder)))
    def _():
        end_q().wait_recv()

    @pl.when(at_end)
    def _():
        peak_ref[...] = jnp.full_like(peak_ref, MASKED_SCORE)
        sum_ref[...] = jnp.zeros_like(sum_ref)
        acc_ref[...] = jnp.zeros_like(acc_ref)
        for i in range(2):
            take_keys([pl.ds((2 * chip + i) * blocks, blocks)])

    def process(found):
        x = jnp.concatenate([x_all[owner, block] for owner, block in found], axis=0)
        parts = [owner * blocks + block for owner, block in found]

        def store(cols, y):
            for i, at in enumerate(parts):
                kv_all[at, :, cols] = y[i * BLOCK : (i + 1) * BLOCK]

        dots(x, w_kv_ref, store)

        @pl.when(at_end)
        def _():
            take_keys(parts)

    def own_blocks(t):
        return [(owner_of(d, t, core), block_of(d, t)) for d in range(2)]

    def side_blocks(t):
        return [(owner_of(d, t, 1 - core), block_of(d, t)) for d in range(2)]

    def pass_on(t):
        for d in range(2):
            arrival(d, t).wait_recv()

            @pl.when(t + ahead < steps)
            def _():
                ring(d, t + ahead).start()

            side(d, t, core).start()

    def first(t):
        pass_on(t)
        process(own_blocks(t))

    def one_step(t, carry):
        pass_on(t)
        for d in range(2):
            side(d, t - 1, 1 - core).wait_recv()
        process(own_blocks(t) + side_blocks(t - 1))

        @pl.when(jnp.logical_and(t >= near_from, t < near_from + blocks))
        def _():
            near_keys(t - near_from)

        pl.when(t == blocks)(add_across)
        pl.when(t == steps - blocks // 2)(add_along)
        return carry

    start = me * blocks
    near_from = 2 + max(
        t for d in range(2) for t, (_, b) in enumerate(orders[d]) if b in (0, blocks - 1)
    )
    key_at = lax.broadcasted_iota(jnp.int32, (2 * BLOCK, 5 * BLOCK), 1)

    def near_keys(b):
        here = start + b
        hidden = jnp.logical_or(
            jnp.logical_and(key_at < BLOCK, here < 2),
            jnp.logical_and(key_at // BLOCK == 2, here > total_blocks - 3),
        )
        chosen = [
            jnp.maximum(here - 1, 0),
            here,
            jnp.minimum(here + 1, total_blocks - 1),
            0,
            total_blocks - 1,
        ]
        out = pl.ds(pl.multiple_of(b * BLOCK, BLOCK), BLOCK)
        scores = []
        for p in range(PAIRS):
            k = jnp.concatenate([kv_all[at, :, lanes_of(p)] for at in chosen], axis=0)
            scores.append(dot_t(stacked_pair(q_ref[out, lanes_of(p)]), k))
        scores = [jnp.where(hidden, MASKED_SCORE, x) for x in scores]
        peaks = [row_max(x) for x in scores]
        weights = [jnp.exp(x - peak) for x, peak in zip(scores, peaks)]
        totals = [row_sum(x) for x in weights]
        sums = []
        for p in range(PAIRS):
            v = jnp.concatenate([kv_all[at, :, lanes_of(PAIRS + p)] for at in chosen], axis=0)
            sums.append(weighted(weights[p], v))
        for p in range(PAIRS):
            near_ref[out, lanes_of(p)] = unstacked_pair(sums[p] * (1.0 / totals[p]))
            near_log_ref[b, p] = jnp.broadcast_to(
                peaks[p] + jnp.log(totals[p]), (2 * BLOCK, LANES)
            )

    first(0)
    lax.fori_loop(1, steps, one_step, 0)

    for k in range(1, half):
        spread_along(k, level_of(k)[0]).wait_recv()
    spread_across(odd).start()
    for d in range(2):
        side(d, steps - 1, 1 - core).wait_recv()
    process(side_blocks(steps - 1))
    load_cross = pltpu.make_async_copy(w_cross_hbm, w_kv_ref, local_sem.at[4])
    load_cross.start()

    @pl.when(jnp.logical_and(at_end, jnp.logical_not(holder)))
    def _():
        for p in range(half_pairs):
            lanes = slice(p * LANES, (p + 1) * LANES)
            end_out_ref[:, lanes] = unstacked_pair(acc_ref[p] * (1.0 / sum_ref[p])).astype(
                jnp.bfloat16
            )
        end_out().start()

    together = 2

    def random_keys(t, carry):
        work = [(together * t + i, p) for i in range(together) for p in range(PAIRS)]
        chosen = [[picks_ref[i, start + b] for i in range(picks_ref.shape[0])] for b, _ in work]
        outs = [pl.ds(pl.multiple_of(b * BLOCK, BLOCK), BLOCK) for b, _ in work]
        scores = []
        for (_, p), out, found in zip(work, outs, chosen):
            k = jnp.concatenate([kv_all[at, :, lanes_of(p)] for at in found], axis=0)
            scores.append(dot_t(stacked_pair(q_ref[out, lanes_of(p)]), k))
        logs = [near_log_ref[b, p] for b, p in work]
        peaks = [jnp.maximum(log, row_max(x)) for log, x in zip(logs, scores)]
        weights = [jnp.exp(x - peak[:, :1]) for x, peak in zip(scores, peaks)]
        fades = [jnp.exp(log - peak) for log, peak in zip(logs, peaks)]
        scales = [1.0 / (fade + row_sum(x)) for fade, x in zip(fades, weights)]
        sums = []
        for (_, p), x, found in zip(work, weights, chosen):
            v = jnp.concatenate([kv_all[at, :, lanes_of(PAIRS + p)] for at in found], axis=0)
            sums.append(weighted(x, v))
        for i, (b, p) in enumerate(work):
            o = unstacked_pair(sums[i] * scales[i])
            o = o + near_ref[outs[i], lanes_of(p)] * unstacked_pair(fades[i] * scales[i])
            attended_ref[outs[i], lanes_of(p)] = o.astype(jnp.bfloat16)
        return carry

    lax.fori_loop(0, blocks // together, random_keys, 0)

    @pl.when(holder)
    def _():
        for p in range(half_pairs):
            attended_ref[pl.ds(end_row, BLOCK), pl.ds(half_lanes(p), LANES)] = unstacked_pair(
                acc_ref[p] * (1.0 / sum_ref[p])
            ).astype(jnp.bfloat16)
        end_out().wait_recv()
        there = pl.multiple_of((1 - core) * half_pairs * LANES, LANES)
        attended_ref[pl.ds(end_row, BLOCK), pl.ds(there, half_pairs * LANES)] = end_half_ref[...]

    spread_across(1 - odd).wait_recv()

    def pair_all(c):
        return push(sumq_ref.at[c], sumq_ref.at[c], pair_send.at[1], pair_recv.at[1], sibling)

    pair_all(core).start()
    store = pltpu.make_async_copy(attended_ref, attended_hbm, local_sem.at[6])
    store.start()
    encoded = x_all[me].reshape(rows, features).astype(jnp.float32)
    encoded = encoded + attended_ref[...].astype(jnp.float32)
    encoded_ref[...] = encoded.astype(jnp.bfloat16)
    load_cross.wait()

    def project_cross(t, carry):
        x = encoded_ref[pl.ds(pl.multiple_of(t * 2 * BLOCK, 2 * BLOCK), 2 * BLOCK)]

        def store(cols, y):
            cross_ref[pl.ds(2 * t, 2), :, cols] = y.reshape(2, BLOCK, -1)

        dots(x, w_kv_ref, store)
        return carry

    lax.fori_loop(0, blocks // 2, project_cross, 0)

    def cross_of(p):
        return cross_ref[:, :, lanes_of(p)].reshape(rows, LANES)

    side_levels = half // 2
    group = 2 * side_levels * share
    width = features + LANES
    near_base = jnp.where(level < side_levels, 0, side_levels)
    bases = [side_levels - near_base, near_base]

    def shaped(x):
        return x.reshape(2, side_levels, share, -1)

    def summary_part(i, c):
        place_ = lax.broadcasted_iota(jnp.int32, (group, LANES), 1)
        logs = jnp.zeros((group, LANES), jnp.float32)
        levels = pl.ds(bases[i], side_levels)
        scores = []
        for p in range(PAIRS):
            q = sumq_ref[c, :, levels, :, lanes_of(p)].reshape(group, LANES)
            scores.append(dot_t(stacked_pair(q), cross_of(p)))
        peaks = [row_max(x) for x in scores]
        weights = [jnp.exp(x - peak) for x, peak in zip(scores, peaks)]
        totals = [row_sum(x) for x in weights]
        sums = [weighted(weights[p], cross_of(PAIRS + p)) for p in range(PAIRS)]
        for p in range(PAIRS):
            part = unstacked_pair(sums[p] * (1.0 / totals[p])).astype(jnp.bfloat16)
            part_ref[i, c, :, :, :, lanes_of(p)] = shaped(part)
            log = peaks[p] + jnp.log(totals[p])
            logs = jnp.where(place_ == 2 * p, log[:group], logs)
            logs = jnp.where(place_ == 2 * p + 1, log[group:], logs)
        part_ref[i, c, :, :, :, features:width] = shaped(with_log(logs, group))

    def pair_part(i):
        return push(
            part_ref.at[i, 1 - core],
            sibp_ref.at[i],
            pair_send.at[(2, 7)[i]],
            pair_recv.at[(2, 7)[i]],
            sibling,
        )

    def spread(x, p, left):
        return jnp.where(left, x[:, 2 * p : 2 * p + 1], x[:, 2 * p + 1 : 2 * p + 2])

    def mix(i):
        pair_part(i).wait_recv()
        left = lax.broadcasted_iota(jnp.int32, (group, LANES), 1) < HEAD
        log_a = without_log(part_ref[i, core, :, :, :, features:width].reshape(group, LANES))
        log_b = without_log(sibp_ref[i, :, :, :, features:width].reshape(group, LANES))
        peak = jnp.maximum(log_a, log_b)
        weight_a = jnp.exp(log_a - peak)
        weight_b = jnp.exp(log_b - peak)
        total = weight_a + weight_b
        weight_a, weight_b = weight_a / total, weight_b / total
        for p in range(PAIRS):
            mine = part_ref[i, core, :, :, :, lanes_of(p)].reshape(group, LANES)
            other = sibp_ref[i, :, :, :, lanes_of(p)].reshape(group, LANES)
            mixed = mine.astype(jnp.float32) * spread(weight_a, p, left)
            mixed = mixed + other.astype(jnp.float32) * spread(weight_b, p, left)
            chipp_ref[i, :, :, :, lanes_of(p)] = shaped(mixed.astype(jnp.bfloat16))
        chipp_ref[i, :, :, :, features:width] = shaped(
            with_log(peak + jnp.log(total), group)
        )

    def across_p(i, x, on, slot):
        other = 2 * (bases[i] + on) + x
        return push(
            chipp_ref.at[i, x, on],
            got_ref.at[slot],
            across_send.at[other],
            across_recv.at[slot],
            2 * other + core,
        )

    on_side = level - near_base
    far_ones = [(0, x, on) for on in range(side_levels) for x in range(2)]
    near_ones = [
        (1, (odd + x) % 2, (on_side + on) % side_levels)
        for on in range(side_levels)
        for x in range(2)
        if (x, on) != (0, 0)
    ]

    pair_all(1 - core).wait_recv()
    summary_part(0, 1 - core)
    pair_part(0).start()
    summary_part(0, core)
    mix(0)
    for one in far_ones:
        across_p(*one, chip).start()
    summary_part(1, 1 - core)
    pair_part(1).start()
    summary_part(1, core)
    mix(1)
    for one in near_ones:
        across_p(*one, chip).start()
    got_ref[chip] = chipp_ref[1, odd, on_side]
    def sent(t, carry):
        for d in range(2):
            ring(d, t).wait_send()
            side(d, t, core).wait_send()
        return carry

    lax.fori_loop(0, steps, sent, 0)
    side_own(me).wait_send()
    pair_q().wait_send()
    pair_all(core).wait_send()
    for i in range(2):
        pair_part(i).wait_send()

    @pl.when(holder)
    def _():
        end_q().wait_send()

    @pl.when(jnp.logical_and(at_end, jnp.logical_not(holder)))
    def _():
        end_out().wait_send()

    across_q().wait_send()
    spread_across(odd).wait_send()
    for k in range(1, half):
        along_q(k, level).wait_send()
        spread_along(k, level).wait_send()

    for i, x, on in far_ones + near_ones:
        across_p(i, x, on, 2 * (bases[i] + on) + x).wait_recv()
    left = lax.broadcasted_iota(jnp.int32, (share, LANES), 1) < HEAD
    logs = [without_log(got_ref[k, :, features:width]) for k in range(chips)]
    peak = functools.reduce(jnp.maximum, logs)
    weights = [jnp.exp(log - peak) for log in logs]
    scale = 1.0 / functools.reduce(jnp.add, weights)
    weights = [w * scale for w in weights]
    for p in range(PAIRS):
        lanes = slice(p * LANES, (p + 1) * LANES)
        total = jnp.zeros((share, LANES), jnp.float32)
        for k in range(chips):
            total = total + got_ref[k, :, lanes].astype(jnp.float32) * spread(weights[k], p, left)
        summary_ref[:, lanes] = total.astype(jnp.bfloat16)
    store.wait()
    for one in far_ones + near_ones:
        across_p(*one, chip).wait_send()


def finish_kernel(attended_ref, summary_ref, attended_out, summary_out, held, small, sem):
    parts = held.shape[0]
    rows = held.shape[1]

    def moves(i, source, target, through):
        return (
            pltpu.make_async_copy(source, through, sem.at[0, i]),
            pltpu.make_async_copy(through, target, sem.at[1, i]),
        )

    copies = [moves(parts, summary_ref, summary_out, small)] + [
        moves(
            i,
            attended_ref.at[pl.ds(i * rows, rows)],
            attended_out.at[pl.ds(i * rows, rows)],
            held.at[i],
        )
        for i in range(parts)
    ]
    for fetch, _ in copies:
        fetch.start()
    for fetch, store in copies:
        fetch.wait()
        store.start()
    for _, store in copies:
        store.wait()


def fused(queries, inputs, w_kv, rand_blocks, w_cross, vocab_table, summary_ids):
    n = lax.axis_size("ctx")
    rows, features = inputs.shape
    blocks = rows // BLOCK
    chips = n // 2
    half = chips // 2
    steps = (half - 1) * blocks + blocks // 2
    share = summary_ids.shape[0] // n
    group = chips * share
    wide = features + LANES
    bf16, f32 = jnp.bfloat16, jnp.float32
    dma = pltpu.SemaphoreType.DMA
    results = pl.pallas_call(
        functools.partial(fused_kernel, n),
        out_shape=[
            jax.ShapeDtypeStruct(queries.shape, bf16),
            jax.ShapeDtypeStruct((share, features), bf16),
        ],
        in_specs=[SMEM, VMEM] + [ANY] * 5,
        out_specs=[ANY, VMEM],
        scratch_shapes=[
            pltpu.VMEM(queries.shape, bf16),
            pltpu.VMEM((n, blocks, BLOCK, features), bf16),
            pltpu.VMEM((n * blocks, BLOCK, 2 * features), bf16),
            pltpu.VMEM(w_kv.shape, bf16),
            pltpu.VMEM(queries.shape, bf16),
            pltpu.VMEM((max(rows, vocab_table.shape[0]), features), bf16),
            pltpu.VMEM((2, 2, half, share, features), bf16),
            pltpu.VMEM((2, half, share, features), bf16),
            pltpu.VMEM((2, half, share, features), bf16),
            pltpu.VMEM((half, share, features), bf16),
            pltpu.VMEM((half, share, features), bf16),
            pltpu.VMEM((half, share, features), bf16),
            pltpu.VMEM((share, features), bf16),
            pltpu.VMEM((2, 2, half, share, features), bf16),
            pltpu.VMEM((PAIRS // 2, 2 * BLOCK, LANES), f32),
            pltpu.VMEM((PAIRS // 2, 2 * BLOCK, LANES), f32),
            pltpu.VMEM((PAIRS // 2, 2 * BLOCK, LANES), f32),
            pltpu.VMEM((BLOCK, features), bf16),
            pltpu.VMEM((BLOCK, features // 2), bf16),
            pltpu.VMEM((BLOCK, features // 2), bf16),
            pltpu.VMEM((rows, features), f32),
            pltpu.VMEM((blocks, PAIRS, 2 * BLOCK, LANES), f32),
            pltpu.VMEM((2, 2, 2, half // 2, share, wide), bf16),
            pltpu.VMEM((2, 2, half // 2, share, wide), bf16),
            pltpu.VMEM((2, 2, half // 2, share, wide), bf16),
            pltpu.VMEM((chips, share, wide), bf16),
            dma((2, steps)),
            dma((2, steps)),
            dma((2, steps)),
            dma((2, steps)),
            dma((2, half)),
            dma((2, half)),
            dma,
            dma,
            dma((8,)),
            dma((8,)),
            dma((chips,)),
            dma((chips,)),
            dma((7,)),
        ],
        compiler_params=pltpu.CompilerParams(
            collective_id=4, has_side_effects=True, vmem_limit_bytes=FUSED_LIMIT
        ),
        name="fused",
    )(
        rand_blocks.T,
        summary_ids.reshape(1, -1),
        inputs.reshape(blocks, BLOCK, features),
        queries,
        w_kv,
        w_cross,
        vocab_table,
    )
    return pl.pallas_call(
        finish_kernel,
        out_shape=[jax.ShapeDtypeStruct(r.shape, r.dtype) for r in results],
        in_specs=[ANY] * 2,
        out_specs=[ANY] * 2,
        scratch_shapes=[
            pltpu.VMEM((3, rows // 3, features), bf16),
            pltpu.VMEM((share, features), bf16),
            dma((2, 4)),
        ],
        name="finish",
    )(*results)


def local(queries, inputs, w_kv, rand_blocks, w_cross, vocab_table, summary_ids):
    n = lax.axis_size("ctx")
    held = 3 * n * inputs.size * 2
    path = fused if held <= HELD_LIMIT else staged
    return path(queries, inputs, w_kv, rand_blocks, w_cross, vocab_table, summary_ids)


def solution(mesh):
    return jax.shard_map(
        local,
        mesh=mesh,
        in_specs=(
            P(("groups", "ctx"), None),
            P(("groups", "ctx"), None),
            P(),
            P("groups", None),
            P(),
            P("ctx", None),
            P("groups"),
        ),
        out_specs=(P(("groups", "ctx"), None), P(("groups", "ctx"), None)),
        check_vma=False,
    )
```
